512 devices in a mesh: sect: 4 (over y), blk: 128 (over x, z, core).
Axes of the slice: x: 4, y: 4, z: 16, core: 2. Of those that a mesh axis runs over, the one named last changes fastest.
Arguments:
- site_tensor: bfloat16 [4, 6144, 1536], P('sect', 'blk'), may hold values from -0.5 to 0.5
- left_env: bfloat16 [4, 256, 384, 384], P('sect', 'blk'), may hold values from -0.23925781 to 0.23925781
- boundary_env: bfloat16 [256, 384, 384], P('blk'), may hold values from -6 to 6
- sector_sizes: int32 [16], replicated, may hold values from 110 to 384, as said below
- mpo_ops: float32 [16, 2, 4, 4], replicated, may hold values from -2 to 2
- mpo_mask: int32 [16, 2], replicated, may hold values 0 or 1
Outputs:
- envs: bfloat16 [4, 256, 384, 384], P('sect', 'blk')
- grads: bfloat16 [4, 6144, 1536], P('sect', 'blk')
The draws below stay inside these ranges and needn't reach their ends.
Inputs may be any that keep to these rules, and one draw needn't show every extreme that they name: `sector_sizes`: exactly one sector holds 384 states, the others hold (1664) // 15 states or one more, and all sizes sum to 2048.
All inputs are finite; a program needn't handle non-finite values.
Results may differ from the reference program's by a relative error of at most 0.018.
Values may be sent and summed in bfloat16 or wider, within the bound.
A program may use at most 64 MiB of HBM per device.

```python
import jax
import jax.numpy as jnp
from jax import lax

S = 16
D = 2048
W = 16
PHYS = 4
DMAX = 384
SITES = 4


def draw_sector_sizes(key, part):
    spare_states = D - 3 * D // S
    base_size = spare_states // (S - 1)
    extra_count = spare_states - base_size * (S - 1)
    ordering = jax.random.permutation(key, S)
    ranking = jnp.argsort(ordering)
    sizes = jnp.where(ranking == 0, 3 * D // S, base_size + (ranking <= extra_count).astype(jnp.int32))
    return sizes.astype(jnp.int32)


def plant(values, own_key, low, largest):
    longest = values.shape.index(max(values.shape))
    spots = []
    for shift in (0, 1):
        where = [jax.random.randint(jax.random.fold_in(own_key, axis), (), 0, length) for axis, length in enumerate(values.shape)]
        where[longest] = (where[longest] + shift) % values.shape[longest]
        spots.append(tuple(where))
    return values.at[spots[0]].set(low).at[spots[1]].set(largest)


def block_scale(rng, dims, split, least, top_value):
    def one(axis_at, parts):
        draws = jax.random.uniform(jax.random.fold_in(jax.random.fold_in(rng, 6), axis_at), (parts,), jnp.float32, least / len(split), top_value / len(split))
        return jnp.repeat(jnp.exp(draws), dims[axis_at] // parts).reshape((-1,) + (1,) * (len(dims) - axis_at - 1))

    factor_of = one(*split[0])
    for cut in split[1:]:
        factor_of = factor_of * one(*cut)
    return factor_of


def scatter_about(rng, shape, scale, bound, cuts=(), held_as=jnp.bfloat16):
    result = scale * jax.random.normal(rng, shape, jnp.float32)
    if cuts:
        result = result * block_scale(rng, shape, cuts, -0.22, 0.18)
    return jnp.clip(result, -bound, bound).astype(held_as)


def setup_inputs(seed: int = 0) -> dict:
    streams_of = jax.random.split(jax.random.key(seed), 7)
    return {
        "site_tensor": scatter_about(streams_of[0], (SITES, S * DMAX, PHYS * DMAX), (D // S) ** -0.5, 0.5, ((0, 4), (1, 128))),
        "left_env": scatter_about(streams_of[1], (SITES, S * W, DMAX, DMAX), 0.04, 0.23925781, ((0, 4), (1, 128))),
        "boundary_env": scatter_about(streams_of[2], (S * W, DMAX, DMAX), 1.0, 6.0, ((0, 128),)),
        "sector_sizes": draw_sector_sizes(jax.random.fold_in(streams_of[6], 71), 0),
        "mpo_ops": scatter_about(streams_of[4], (W, 2, PHYS, PHYS), 0.35, 2.0, (), jnp.float32),
        "mpo_mask": plant((jax.random.randint(streams_of[5], (W, 2), 0, 4) < 3).astype(jnp.int32), jax.random.fold_in(streams_of[5], 1), 0, 1),
    }


CHARGE = (0, 1, 1, 2)
CLASSES = ((0,), (1, 2), (1, 2), (3,))


def reference(site_tensor, left_env, boundary_env, sector_sizes, mpo_ops, mpo_mask):
    sizes_ext = jnp.concatenate([sector_sizes, jnp.zeros((2,), jnp.int32)])
    cell_index = jnp.arange(DMAX, dtype=jnp.int32)
    live_rows = (cell_index[None, :] < sizes_ext[:, None]).astype(jnp.bfloat16)
    column_live = jnp.stack([live_rows[CHARGE[p]:CHARGE[p] + S] for p in range(PHYS)], axis=1)
    tensor_mask = live_rows[:S, :, None, None] * column_live[:, None, :, :]
    column_mask = column_live[:, None, :, :]
    env_mask = live_rows[:S, None, :, None] * live_rows[:S, None, None, :]
    coefficients = mpo_ops * mpo_mask.astype(jnp.float32)[:, :, None, None]
    env_in = boundary_env.reshape(S, W, DMAX, DMAX) * env_mask
    env_list = []
    grad_list = []
    for site_index in range(SITES - 1, -1, -1):
        tensor = site_tensor[site_index].reshape(S, DMAX, PHYS, DMAX) * tensor_mask
        left_blocks = left_env[site_index].reshape(S, W, DMAX, DMAX)
        padded_env = jnp.concatenate([env_in, jnp.zeros((2, W, DMAX, DMAX), env_in.dtype)], axis=0)

        def one_sector(sector):
            sector_tensor = lax.dynamic_index_in_dim(tensor, sector, 0, keepdims=False)
            nearby = lax.dynamic_slice_in_dim(padded_env, sector, 3, 0)
            left_sector = lax.dynamic_index_in_dim(left_blocks, sector, 0, keepdims=False)
            col_mask = lax.dynamic_index_in_dim(column_mask, sector, 0, keepdims=False)
            product_list = []
            for phys_state in range(PHYS):
                product = jnp.einsum('xz,wzy->wxy', sector_tensor[:, phys_state, :].astype(jnp.float32),
                                     nearby[CHARGE[phys_state]].astype(jnp.float32))
                product_list.append(product.astype(jnp.bfloat16))
            products = jnp.stack(product_list, axis=1)
            partner = jnp.flip(products.reshape(W // 2, 2, PHYS, DMAX, DMAX), 1).reshape(W, PHYS, DMAX, DMAX)
            term_list = []
            for target in range(PHYS):
                running = jnp.zeros((W, DMAX, DMAX), jnp.float32)
                for source in CLASSES[target]:
                    running = running + coefficients[:, 0, source, target][:, None, None] * products[:, source].astype(jnp.float32)
                    running = running + coefficients[:, 1, source, target][:, None, None] * partner[:, source].astype(jnp.float32)
                term_list.append(running.astype(jnp.bfloat16))
            mixed_blocks = jnp.stack(term_list, axis=1)
            new_env = jnp.einsum('wpxz,ypz->wxy', mixed_blocks.astype(jnp.float32),
                                 sector_tensor.astype(jnp.float32)).astype(jnp.bfloat16)
            grad_part = jnp.einsum('wxy,wpxz->ypz', left_sector.astype(jnp.float32),
                                   mixed_blocks.astype(jnp.float32))
            grad_part = (grad_part * col_mask.astype(jnp.float32)).astype(jnp.bfloat16)
            return new_env, grad_part

        new_envs, new_grads = lax.map(one_sector, jnp.arange(S, dtype=jnp.int32))
        env_list.append(new_envs.reshape(S * W, DMAX, DMAX))
        grad_list.append(new_grads.reshape(S * DMAX, PHYS * DMAX))
        env_in = new_envs
    return (jnp.stack(env_list[::-1], axis=0), jnp.stack(grad_list[::-1], axis=0))
```

```python
from functools import partial

import jax
import jax.numpy as jnp
from jax import lax
from jax.experimental import pallas as pl
from jax.experimental.pallas import tpu as pltpu
from jax.sharding import PartitionSpec as P

S = 16
W = 16
N = 384
T = 128
H = 112
G8 = 8
BF = jnp.bfloat16
F32 = jnp.float32


def mm(a, b):
    return jnp.dot(a, b, preferred_element_type=F32)


def mm_t(a, b):
    return lax.dot_general(a, b, (((1,), (1,)), ((), ())), preferred_element_type=F32)


def t_mm(a, b):
    return lax.dot_general(a, b, (((0,), (0,)), ((), ())), preferred_element_type=F32)


def mix(wts, prods, target):
    sources = ((0,), (1, 2), (1, 2), (3,))[target]
    out = []
    for w in range(2):
        total = None
        for p in sources:
            for k in range(2):
                coef = wts[((w * 2 + k) * 4 + p) * 4 + target]
                term = coef * prods[w ^ k][p].astype(F32)
                total = term if total is None else total + term
        out.append(total.astype(BF))
    return out


def push_mixed(wts, acol, r_ref, size):
    prods = []
    for w in range(2):
        right = r_ref[w, :size, :size]
        own = mm(acol[:size, :size], right).astype(BF)
        halo = mm(acol[N : 2 * N, :size], right).astype(BF)
        prods.append((own, halo[:T], halo[T : 2 * T], halo[2 * T :]))
    return [mix(wts, prods, target) for target in range(4)]


def pull_mixed(wts, pull, base, m1, m3):
    prods = []
    zero = jnp.zeros((T - H, T), BF)
    for w in range(2):
        near = jnp.concatenate([m1[w], zero], axis=0)
        far = jnp.concatenate([m3[w], zero], axis=0)
        prods.append(
            (
                None,
                mm(pull[:, base : base + T], near).astype(BF),
                mm(pull[:, base + T : base + 2 * T], near).astype(BF),
                mm(pull[:, base + 2 * T : base + 3 * T], far).astype(BF),
            )
        )
    return [None] + [mix(wts, prods, target) for target in range(1, 4)]


def push_send(info, wts, acol, r_ref, c0_out, m1_out, m3_out):
    def run(size):
        mixed = push_mixed(wts, acol, r_ref, size)
        for w in range(2):
            c0_out[w, :size, :size] = mm_t(mixed[0][w], acol[:size, :size]).astype(BF)
            near = mm_t(mixed[1][w], acol[N : N + T, :size]) + mm_t(
                mixed[2][w], acol[N + T : N + 2 * T, :size]
            )
            far = mm_t(mixed[3][w], acol[N + 2 * T : 2 * N, :size])
            tile = r_ref[w, :H, :T]
            m1_out[w] = jnp.where(info[1] == 1, tile, near[:H].astype(BF))
            m3_out[w] = jnp.where(info[2] == 1, tile, far[:H].astype(BF))

    @pl.when(info[0] == 1)
    def _():
        run(N)

    @pl.when(info[0] == 0)
    def _():
        run(T)


def combine(info, wts, pull, base, c0, m1, m3, r_out):
    @pl.when(info[0] == 1)
    def _():
        mixed = pull_mixed(wts, pull, base, m1, m3)
        for w in range(2):
            total = c0[w].astype(F32)
            for p in range(1, 4):
                total = total + mm_t(mixed[p][w], pull[:, base + (p - 1) * T : base + p * T])
            r_out[w] = total.astype(BF)

    @pl.when(info[0] == 0)
    def _():
        r_out[...] = jnp.zeros_like(r_out)
        for w in range(2):
            r_out[w, :H, :T] = (
                c0[w, :H, :T].astype(F32) + m1[w].astype(F32) + m3[w].astype(F32)
            ).astype(BF)


def first_kernel(info, wts, ag, bound, acol, pull, r_out, c0_out, m1_out, m3_out):
    for within in range(G8):
        core, pos = within % 2, within // 2
        rows = lax.broadcasted_iota(jnp.int32, (48, 3 * N), 0) + 48 * within
        own = jnp.where(rows < info[3], ag[core, pos, :48, :], jnp.zeros((48, 3 * N), BF))
        acol[48 * within : 48 * within + 48, :] = own[:, :N]
        pull[48 * within : 48 * within + 48, :] = own[:, N:]
        halo_rows = lax.broadcasted_iota(jnp.int32, (16, N), 0) + 16 * within
        for block in range(3):
            limit = info[4] if block < 2 else info[5]
            at = N + T * block + 16 * within
            acol[at : at + 16, :] = jnp.where(
                halo_rows < limit,
                ag[core, pos, 48:, N * block : N * block + N],
                jnp.zeros((16, N), BF),
            )
    row = lax.broadcasted_iota(jnp.int32, (N, N), 0)
    col = lax.broadcasted_iota(jnp.int32, (N, N), 1)
    live = jnp.maximum(row, col) < info[3]
    for w in range(2):
        r_out[w] = jnp.where(live, bound[w], jnp.zeros((N, N), BF))

    @pl.when(info[6] == 3)
    def _():
        push_send(info, wts, acol, r_out, c0_out, m1_out, m3_out)


def next_kernel(active, info, wts, acol, pull, c0, m1, m3, r_in, s1_in, s3_in, r_out, s1, s3, c0_out, m1_out, m3_out):
    del r_in, s1_in, s3_in

    @pl.when(info[6] == active)
    def _():
        combine(info, wts, pull, N, c0, m1, m3, r_out)
        s1[...] = m1[...]
        s3[...] = m3[...]
        push_send(info, wts, acol, r_out, c0_out, m1_out, m3_out)


def last_kernel(info, wts, pull, c0, m1, m3, r_out):
    combine(info, wts, pull, 0, c0, m1, m3, r_out)


def write_rows(out, grads, at, size):
    for within in range(G8):
        spot = (within % 2) * 4 + within // 2
        out[spot, :, at : at + size] = grads[48 * within : 48 * within + 48].astype(BF)


def push_grad_kernel(info, wts, acol, r_ref, left, near, far, out):
    def run(size):
        mixed = push_mixed(wts, acol, r_ref, size)
        if size < N:
            out[...] = jnp.zeros_like(out)
        own = t_mm(left[0, :size, :], mixed[0][0]) + t_mm(left[1, :size, :], mixed[0][1])
        write_rows(out, own, 0, size)
        for p in (1, 2):
            part = t_mm(near[0], mixed[p][0][:H]) + t_mm(near[1], mixed[p][1][:H])
            write_rows(out, part, N * p, size)
        part = t_mm(far[0], mixed[3][0][:H]) + t_mm(far[1], mixed[3][1][:H])
        write_rows(out, part, N * 3, size)

    @pl.when(info[0] == 1)
    def _():
        run(N)

    @pl.when(info[0] == 0)
    def _():
        run(T)


def pull_grad_kernel(info, wts, pull, left, m1, m3, out):
    @pl.when(info[0] == 1)
    def _():
        mixed = pull_mixed(wts, pull, 0, m1, m3)
        for p in range(1, 4):
            part = t_mm(left[0], mixed[p][0]) + t_mm(left[1], mixed[p][1])
            write_rows(out, part, T * (p - 1), T)

    @pl.when(info[0] == 0)
    def _():
        out[...] = jnp.zeros_like(out)


SMEM = pl.BlockSpec(memory_space=pltpu.SMEM)
VMEM = pl.BlockSpec(memory_space=pltpu.VMEM)
PARAMS = pltpu.CompilerParams(vmem_limit_bytes=48 * 1024 * 1024)
R_T = jax.ShapeDtypeStruct((2, N, N), BF)
M_T = jax.ShapeDtypeStruct((2, H, T), BF)


def call(kernel, outs, count, name, **extra):
    return pl.pallas_call(
        kernel,
        out_shape=outs,
        in_specs=[SMEM, SMEM] + [VMEM] * count,
        out_specs=jax.tree.map(lambda _: VMEM, outs),
        compiler_params=PARAMS,
        name=name,
        **extra,
    )


def local(site_tensor, left_env, boundary_env, sector_sizes, mpo_ops, mpo_mask):
    section = lax.axis_index("sect")
    position = lax.axis_index("blk")
    within = position % G8
    sector = position // G8
    blk_devices = 128

    sizes_pad = jnp.concatenate(
        [jnp.zeros((2,), jnp.int32), sector_sizes.astype(jnp.int32)]
    )
    near_sizes = lax.dynamic_slice_in_dim(sizes_pad, sector, 3)
    n_far, n_near, n_own = near_sizes[0], near_sizes[1], near_sizes[2]
    info = jnp.stack(
        [
            (n_own > H).astype(jnp.int32),
            (n_near > H).astype(jnp.int32),
            (n_far > H).astype(jnp.int32),
            n_own,
            n_near,
            n_far,
            section,
            sector,
        ]
    )
    wts = lax.dynamic_slice_in_dim(
        mpo_ops * mpo_mask.astype(F32)[:, :, None, None], within * 2, 2, 0
    ).reshape(64)

    def blk_perm(value, pairs):
        return lax.ppermute(value, "blk", pairs)

    def both_perm(value, pairs):
        return lax.ppermute(value, ("sect", "blk"), pairs)

    def partner(value, mask):
        return blk_perm(value, [(i, i ^ mask) for i in range(blk_devices)])

    rows = site_tensor[0]
    narrow = jnp.concatenate([rows[:, N * p : N * p + T] for p in range(1, 4)], axis=1)
    above = lax.ppermute(narrow, "sect", [(i + 1, i) for i in range(3)])
    halo = jnp.zeros((16, 3 * N), BF)
    pieces = []
    for j in range(3):
        near_pairs = [
            (q * 8 + a, (q + 1) * 8 + 3 * a + j)
            for q in range(S - 1)
            for a in range(3)
            if 3 * a + j < 8
        ]
        far_pairs = [
            (q * 8 + a, (q + 2) * 8 + 3 * a + j)
            for q in range(S - 2)
            for a in range(3)
            if 3 * a + j < 8
        ]
        cut = rows[16 * j : 16 * j + 16]
        pieces.append(
            jnp.concatenate(
                [blk_perm(cut[:, N : 3 * N], near_pairs), blk_perm(cut[:, 3 * N :], far_pairs)],
                axis=1,
            )
        )
    halo = jnp.where(within % 3 == 0, pieces[0], jnp.where(within % 3 == 1, pieces[1], pieces[2]))
    packed = jnp.concatenate(
        [jnp.concatenate([rows[:, :N], narrow, above], axis=1), halo], axis=0
    )[None]
    for mask in (2, 4):
        other = partner(packed, mask)
        packed = jnp.where(
            (within & mask) > 0,
            jnp.concatenate([other, packed], axis=0),
            jnp.concatenate([packed, other], axis=0),
        )
    other = partner(packed, 1)
    gathered = jnp.where(
        (within & 1) > 0, jnp.stack([other, packed]), jnp.stack([packed, other])
    )

    left = left_env[0]
    gathered, left_tile = lax.optimization_barrier((gathered, left[:, :H, :]))
    left_near = blk_perm(left_tile, [(i, i + 8) for i in range(blk_devices - 8)])
    left_far = blk_perm(left_tile, [(i, i + 16) for i in range(blk_devices - 16)])

    acol_t = jax.ShapeDtypeStruct((2 * N, N), BF)
    acol, pull, right, c0, m1, m3 = call(
        first_kernel, (acol_t, jax.ShapeDtypeStruct((N, 2 * N), BF), R_T, R_T, M_T, M_T), 2, "first"
    )(info, wts, gathered, boundary_env)
    seen1 = jnp.zeros((2, H, T), BF)
    seen3 = jnp.zeros((2, H, T), BF)

    def shift(value, site, step, target):
        return both_perm(
            value,
            [
                (site * blk_devices + i, target * blk_devices + i - step)
                for i in range(step, blk_devices)
            ],
        )

    for site in (3, 2, 1):
        got0 = shift(c0, site, 0, site - 1)
        got1 = shift(m1, site, 8, site - 1)
        got3 = shift(m3, site, 16, site - 1)
        right, seen1, seen3, c0, m1, m3 = call(
            partial(next_kernel, site - 1),
            (R_T, M_T, M_T, R_T, M_T, M_T),
            8,
            "next",
            input_output_aliases={7: 0, 8: 1, 9: 2},
        )(info, wts, acol, pull, got0, got1, got3, right, seen1, seen3)
    got1 = shift(m1, 0, 8, 0)
    got3 = shift(m3, 0, 16, 0)
    push_part = call(
        push_grad_kernel, jax.ShapeDtypeStruct((G8, 48, 4 * N), BF), 5, "push_grad"
    )(info, wts, acol, right, left, left_near, left_far)

    up = [(i, i + 1) for i in range(3)]
    back = lax.ppermute(right, "sect", up)
    back1 = lax.ppermute(seen1, "sect", up)
    back3 = lax.ppermute(seen3, "sect", up)
    final = call(last_kernel, R_T, 4, "last")(info, wts, pull, c0, got1, got3)
    env_out = jnp.where(section == 0, final, back)
    at1 = jnp.where(section == 0, got1, back1)
    at3 = jnp.where(section == 0, got3, back3)
    pull_part = call(pull_grad_kernel, jax.ShapeDtypeStruct((G8, 48, N), BF), 4, "pull_grad")(
        info, wts, pull, left, at1, at3
    )

    def scatter(part):
        for mask in (1, 4, 2):
            half = part.shape[0] // 2
            upper = (within & mask) > 0
            send = jnp.where(upper, part[:half], part[half:])
            keep = jnp.where(upper, part[half:], part[:half])
            part = (keep.astype(F32) + partner(send, mask).astype(F32)).astype(BF)
        return part[0]

    push_sum = scatter(push_part)
    pull_sum = scatter(pull_part)
    near_sum = blk_perm(push_sum[:, N : 3 * N], [(i, i - 8) for i in range(8, blk_devices)])
    far_sum = blk_perm(push_sum[:, 3 * N :], [(i, i - 16) for i in range(16, blk_devices)])
    wide = jnp.pad(pull_sum.reshape(48, 3, T), ((0, 0), (0, 0), (0, N - T))).reshape(48, 3 * N)
    rest = jnp.where(n_own > H, wide, jnp.concatenate([near_sum, far_sum], axis=1))
    grads = jnp.concatenate([push_sum[:, :N], rest], axis=1)
    return env_out[None].reshape(1, 2, N, N), grads[None]


def solution(mesh):
    return jax.shard_map(
        local,
        mesh=mesh,
        in_specs=(
            P("sect", "blk", None),
            P("sect", "blk", None, None),
            P("blk", None, None),
            P(),
            P(),
            P(),
        ),
        out_specs=(P("sect", "blk", None, None), P("sect", "blk", None)),
        check_vma=False,
    )
```

```python
from functools import partial

import jax
import jax.numpy as jnp
from jax import lax
from jax.experimental import pallas as pl
from jax.experimental.pallas import tpu as pltpu
from jax.sharding import PartitionSpec as P

S = 16
W = 16
N = 384
T = 128
H = 112
G8 = 8
BF = jnp.bfloat16
F32 = jnp.float32
MESH = pl.DeviceIdType.MESH
DMA = pltpu.SemaphoreType.DMA


def mm(a, b):
    return jnp.dot(a, b, preferred_element_type=F32)


def mm_t(a, b):
    return lax.dot_general(a, b, (((1,), (1,)), ((), ())), preferred_element_type=F32)


def t_mm(a, b):
    return lax.dot_general(a, b, (((0,), (0,)), ((), ())), preferred_element_type=F32)


def mix(wts, prods, target):
    sources = ((0,), (1, 2), (1, 2), (3,))[target]
    out = []
    for w in range(2):
        total = None
        for p in sources:
            for k in range(2):
                coef = wts[((w * 2 + k) * 4 + p) * 4 + target]
                term = coef * prods[w ^ k][p].astype(F32)
                total = term if total is None else total + term
        out.append(total.astype(BF))
    return out


def push_mixed(wts, acol, r_ref, size):
    prods = []
    for w in range(2):
        right = r_ref[w, :size, :size]
        own = mm(acol[:size, :size], right).astype(BF)
        halo = mm(acol[N : 2 * N, :size], right).astype(BF)
        prods.append((own, halo[:T], halo[T : 2 * T], halo[2 * T :]))
    return [mix(wts, prods, target) for target in range(4)]


def pull_mixed(wts, pull, base, m1, m3):
    prods = []
    zero = jnp.zeros((T - H, T), BF)
    for w in range(2):
        near = jnp.concatenate([m1[w], zero], axis=0)
        far = jnp.concatenate([m3[w], zero], axis=0)
        prods.append(
            (
                None,
                mm(pull[:, base : base + T], near).astype(BF),
                mm(pull[:, base + T : base + 2 * T], near).astype(BF),
                mm(pull[:, base + 2 * T : base + 3 * T], far).astype(BF),
            )
        )
    return [None] + [mix(wts, prods, target) for target in range(1, 4)]


def push_send(info, wts, acol, r_ref, c0_out, m1_out, m3_out):
    mixed = push_mixed(wts, acol, r_ref, N)
    for w in range(2):
        tile = r_ref[w, :H, :T]
        near = mm_t(mixed[1][w], acol[N : N + T, :]) + mm_t(mixed[2][w], acol[N + T : N + 2 * T, :])
        far = mm_t(mixed[3][w], acol[N + 2 * T : 2 * N, :])
        m1_out[w] = jnp.where(info[1] == 1, tile, near[:H].astype(BF))
        m3_out[w] = jnp.where(info[2] == 1, tile, far[:H].astype(BF))
        c0_out[w] = mm_t(mixed[0][w], acol[:N, :]).astype(BF)


def combine(info, wts, pull, base, c0, m1, m3, r_out):
    mixed = pull_mixed(wts, pull, base, m1, m3)
    big = info[0] == 1
    for w in range(2):
        kept = c0[w].astype(F32)
        total = kept
        for p in range(1, 4):
            total = total + mm_t(mixed[p][w], pull[:, base + (p - 1) * T : base + p * T])
        r_out[w] = jnp.where(big, total, jnp.zeros_like(total)).astype(BF)
        small = kept[:H, :T] + m1[w].astype(F32) + m3[w].astype(F32)
        r_out[w, :H, :T] = jnp.where(big, total[:H, :T], small).astype(BF)


def remote(src, dst, sems, slot, target):
    return pltpu.make_async_remote_copy(
        src_ref=src,
        dst_ref=dst,
        send_sem=sems[0].at[slot],
        recv_sem=sems[1].at[slot],
        device_id=target,
        device_id_type=MESH,
    )


def greet(targets):
    barrier = pltpu.get_barrier_semaphore()
    for target in targets:
        pl.semaphore_signal(barrier, inc=1, device_id=target, device_id_type=MESH)
    return barrier


def gather_kernel(info, x_in, rows, acol, pull, xs, hs, ab, send, recv, own_sem):
    sect = lax.axis_index("sect")
    blk = lax.axis_index("blk")
    within = lax.rem(blk, G8)
    base = blk - within
    core = lax.rem(within, 2)
    chip = within // 2
    sems = (send, recv)
    upper = lax.rem(sect + 1, 4)
    lower = lax.rem(sect + 3, 4)
    mate = (sect, base + chip * 2 + 1 - core)
    peers = [(sect, base + lax.rem(chip + d, 4) * 2 + core) for d in (1, 2, 3)]
    origin = within // 3
    barrier = greet(
        peers
        + [mate, (upper, blk), (lower, blk)]
        + [(sect, lax.rem(base + 128 - 8 * d + origin, 128)) for d in (1, 2)]
    )
    goals = [[(sect, lax.rem(base + 8 * d, 128) + 3 * within + j) for j in range(3)] for d in (1, 2)]
    sends_halo = [(3 * within + j) < G8 for j in range(3)]
    for j in range(3):

        @pl.when(sends_halo[j])
        def _(j=j):
            for d in range(2):
                pl.semaphore_signal(barrier, inc=1, device_id=goals[d][j], device_id_type=MESH)

    extra = jnp.where(within < 2, 6, jnp.where(within == 2, 4, 0))
    pl.semaphore_wait(barrier, 8 + extra)

    def halo_copy(d, j):
        width = 2 * N if d == 0 else N
        at = N if d == 0 else 3 * N
        to = 0 if d == 0 else 2 * N
        return pltpu.make_async_remote_copy(
            src_ref=rows.at[pl.ds(16 * j, 16), pl.ds(at, width)],
            dst_ref=hs.at[3 * within + j, :, pl.ds(to, width)],
            send_sem=send.at[3 * d + j],
            recv_sem=recv.at[d],
            device_id=goals[d][j],
            device_id_type=MESH,
        )

    for j in range(3):

        @pl.when(sends_halo[j])
        def _(j=j):
            halo_copy(0, j).start()
            halo_copy(1, j).start()

    above = remote(x_in.at[:, pl.ds(N, N)], ab.at[within], sems, 6, (lower, blk))
    above.start()
    own = pltpu.make_async_copy(x_in, xs.at[within], own_sem)
    own.start()
    x_peer = [remote(x_in, xs.at[within], sems, 7 + d, peers[d]) for d in range(3)]
    for copy in x_peer:
        copy.start()
    x_mate = [remote(x_in, xs.at[within], sems, 10, mate)]
    x_mate[0].start()

    def arrive(buf, slot, spot):
        pltpu.make_async_remote_copy(
            src_ref=buf.at[spot],
            dst_ref=buf.at[spot],
            send_sem=send.at[slot],
            recv_sem=recv.at[slot],
            device_id=mate,
            device_id_type=MESH,
        ).wait_recv()

    halo_in_near = pltpu.make_async_remote_copy(
        src_ref=hs.at[within, :, pl.ds(0, 2 * N)],
        dst_ref=hs.at[within, :, pl.ds(0, 2 * N)],
        send_sem=send.at[0],
        recv_sem=recv.at[0],
        device_id=mate,
        device_id_type=MESH,
    )
    halo_in_far = pltpu.make_async_remote_copy(
        src_ref=hs.at[within, :, pl.ds(2 * N, N)],
        dst_ref=hs.at[within, :, pl.ds(2 * N, N)],
        send_sem=send.at[0],
        recv_sem=recv.at[1],
        device_id=mate,
        device_id_type=MESH,
    )
    above.wait_recv()
    a_peer = [remote(ab.at[within], ab.at[within], sems, 14 + d, peers[d]) for d in range(3)]
    a_mate = [remote(ab.at[within], ab.at[within], sems, 17, mate)]
    halo_in_near.wait_recv()
    halo_in_far.wait_recv()
    h_peer = [remote(hs.at[within], hs.at[within], sems, 21 + d, peers[d]) for d in range(3)]
    h_mate = [remote(hs.at[within], hs.at[within], sems, 24, mate)]
    for copy in h_peer + h_mate + a_peer + a_mate:
        copy.start()
    for buf, first, mine in ((xs, 7, x_mate), (hs, 21, h_mate), (ab, 14, a_mate)):
        for d in range(3):
            spot = lax.rem(chip + 3 - d, 4) * 2 + core
            arrive(buf, first + d, spot)
            forward = remote(buf.at[spot], buf.at[spot], sems, first + 4 + d, mate)
            forward.start()
            mine.append(forward)
    own.wait()
    for buf, mine in ((xs, x_mate), (hs, h_mate), (ab, a_mate)):
        for copy in mine:
            copy.wait()
    for copy in x_peer + h_peer + a_peer:
        copy.wait_send()
    above.wait_send()
    for j in range(3):

        @pl.when(sends_halo[j])
        def _(j=j):
            halo_copy(0, j).wait_send()
            halo_copy(1, j).wait_send()

    for w in range(G8):
        line = lax.broadcasted_iota(jnp.int32, (48, N), 0) + 48 * w
        live = line < info[3]
        zero = jnp.zeros((48, N), BF)
        acol[48 * w : 48 * w + 48, :] = jnp.where(live, xs[w, :, :N], zero)
        pull[48 * w : 48 * w + 48, :N] = jnp.where(live, xs[w, :, N:], zero)
        pull[48 * w : 48 * w + 48, N:] = jnp.where(live, ab[w], zero)
        halo_line = lax.broadcasted_iota(jnp.int32, (16, N), 0) + 16 * w
        for block in range(3):
            limit = info[4] if block < 2 else info[5]
            at = N + T * block + 16 * w
            acol[at : at + 16, :] = jnp.where(
                halo_line < limit, hs[w, :, N * block : N * block + N], jnp.zeros((16, N), BF)
            )


def chain_kernel(
    info, wts, acol, pull, bound, left,
    r_out, env_out, at1, at3, near_out, far_out,
    c0, m1, m3, got0, got1, got3, send, recv,
):
    sect = lax.axis_index("sect")
    blk = lax.axis_index("blk")
    upper = lax.rem(sect + 1, 4)
    lower = lax.rem(sect + 3, 4)
    back8, back16 = lax.rem(blk + 120, 128), lax.rem(blk + 112, 128)
    fore8, fore16 = lax.rem(blk + 8, 128), lax.rem(blk + 16, 128)
    sems = (send, recv)
    barrier = greet(
        [(upper, blk), (upper, fore8), (upper, fore16), (lower, blk), (lower, back8), (lower, back16)]
        + [(sect, back8), (sect, back16), (sect, fore8), (sect, fore16)]
    )
    row = lax.broadcasted_iota(jnp.int32, (N, N), 0)
    col = lax.broadcasted_iota(jnp.int32, (N, N), 1)
    live = jnp.maximum(row, col) < info[3]
    for w in range(2):
        r_out[w] = jnp.where(live, bound[w], jnp.zeros((N, N), BF))
    pl.semaphore_wait(barrier, 10)

    l_near = remote(left.at[:, pl.ds(0, H), :], near_out, sems, 6, (sect, fore8))
    l_far = remote(left.at[:, pl.ds(0, H), :], far_out, sems, 7, (sect, fore16))

    @pl.when(sect < 2)
    def _():
        l_near.start()
        l_far.start()

    down0 = remote(c0, got0, sems, 0, (lower, blk))
    down1 = remote(m1, got1, sems, 1, (lower, back8))
    down3 = remote(m3, got3, sems, 2, (lower, back16))
    last1 = remote(m1, at1, sems, 4, (sect, back8))
    last3 = remote(m3, at3, sems, 5, (sect, back16))
    back0 = remote(r_out, env_out, sems, 3, (upper, blk))

    @pl.when(sect < 3)
    def _():
        down1.wait_recv()
        down3.wait_recv()
        down0.wait_recv()
        combine(info, wts, pull, N, got0, got1, got3, r_out)

    push_send(info, wts, acol, r_out, c0, m1, m3)

    @pl.when(sect > 0)
    def _():
        down1.start()
        down3.start()
        down0.start()

    @pl.when(sect == 0)
    def _():
        last1.start()
        last3.start()

    @pl.when(sect < 3)
    def _():
        back0.start()

    @pl.when(sect < 3)
    def _():
        up1 = remote(got1, at1, sems, 8, (upper, blk))
        up3 = remote(got3, at3, sems, 9, (upper, blk))
        up1.start()
        up3.start()

    @pl.when(sect >= 2)
    def _():
        l_near.start()
        l_far.start()

    @pl.when(sect == 0)
    def _():
        last1.wait()
        last3.wait()
        combine(info, wts, pull, 0, c0, at1, at3, env_out)

    @pl.when(sect > 0)
    def _():
        down0.wait_send()
        down1.wait_send()
        down3.wait_send()
        back0.wait_recv()
        remote(got1, at1, sems, 8, (upper, blk)).wait_recv()
        remote(got3, at3, sems, 9, (upper, blk)).wait_recv()

    @pl.when(sect < 3)
    def _():
        back0.wait_send()
        remote(got1, at1, sems, 8, (upper, blk)).wait_send()
        remote(got3, at3, sems, 9, (upper, blk)).wait_send()

    l_near.wait()
    l_far.wait()


def write_rows(out, grads, at, size):
    for within in range(G8):
        spot = (within % 2) * 4 + within // 2
        out[spot, :, at : at + size] = grads[48 * within : 48 * within + 48].astype(BF)


def push_grad_kernel(info, wts, acol, r_ref, left, near, far, out):
    def run(size):
        mixed = push_mixed(wts, acol, r_ref, size)
        if size < N:
            out[...] = jnp.zeros_like(out)
        own = t_mm(left[0, :size, :], mixed[0][0]) + t_mm(left[1, :size, :], mixed[0][1])
        write_rows(out, own, 0, size)
        for p in (1, 2):
            part = t_mm(near[0], mixed[p][0][:H]) + t_mm(near[1], mixed[p][1][:H])
            write_rows(out, part, N * p, size)
        part = t_mm(far[0], mixed[3][0][:H]) + t_mm(far[1], mixed[3][1][:H])
        write_rows(out, part, N * 3, size)

    @pl.when(info[0] == 1)
    def _():
        run(N)

    @pl.when(info[0] == 0)
    def _():
        run(T)


def pull_grad_kernel(info, wts, pull, left, m1, m3, out):
    @pl.when(info[0] == 1)
    def _():
        mixed = pull_mixed(wts, pull, 0, m1, m3)
        for p in range(1, 4):
            part = t_mm(left[0], mixed[p][0]) + t_mm(left[1], mixed[p][1])
            write_rows(out, part, T * (p - 1), T)

    @pl.when(info[0] == 0)
    def _():
        out[...] = jnp.zeros_like(out)


SMEM = pl.BlockSpec(memory_space=pltpu.SMEM)
VMEM = pl.BlockSpec(memory_space=pltpu.VMEM)
PARAMS = pltpu.CompilerParams(vmem_limit_bytes=48 * 1024 * 1024)
R_T = jax.ShapeDtypeStruct((2, N, N), BF)
M_T = jax.ShapeDtypeStruct((2, H, T), BF)


def call(kernel, outs, count, name, **extra):
    return pl.pallas_call(
        kernel,
        out_shape=outs,
        in_specs=[SMEM, SMEM] + [VMEM] * count,
        out_specs=jax.tree.map(lambda _: VMEM, outs),
        compiler_params=PARAMS,
        name=name,
        **extra,
    )


def local(site_tensor, left_env, boundary_env, sector_sizes, mpo_ops, mpo_mask):
    section = lax.axis_index("sect")
    position = lax.axis_index("blk")
    within = position % G8
    sector = position // G8
    blk_devices = 128

    sizes_pad = jnp.concatenate(
        [jnp.zeros((2,), jnp.int32), sector_sizes.astype(jnp.int32)]
    )
    near_sizes = lax.dynamic_slice_in_dim(sizes_pad, sector, 3)
    n_far, n_near, n_own = near_sizes[0], near_sizes[1], near_sizes[2]
    info = jnp.stack(
        [
            (n_own > H).astype(jnp.int32),
            (n_near > H).astype(jnp.int32),
            (n_far > H).astype(jnp.int32),
            n_own,
            n_near,
            n_far,
            section,
            sector,
        ]
    )
    wts = lax.dynamic_slice_in_dim(
        mpo_ops * mpo_mask.astype(F32)[:, :, None, None], within * 2, 2, 0
    ).reshape(64)

    def blk_perm(value, pairs):
        return lax.ppermute(value, "blk", pairs)

    def partner(value, mask):
        return blk_perm(value, [(i, i ^ mask) for i in range(blk_devices)])

    rows = site_tensor[0]
    x_in = jnp.concatenate([rows[:, :N]] + [rows[:, N * p : N * p + T] for p in range(1, 4)], axis=1)
    left = left_env[0]
    acol, pull = pl.pallas_call(
        gather_kernel,
        out_shape=(
            jax.ShapeDtypeStruct((2 * N, N), BF),
            jax.ShapeDtypeStruct((N, 2 * N), BF),
        ),
        in_specs=[SMEM, VMEM, VMEM],
        out_specs=(VMEM, VMEM),
        scratch_shapes=[
            pltpu.VMEM((G8, 48, 2 * N), BF),
            pltpu.VMEM((G8, 16, 3 * N), BF),
            pltpu.VMEM((G8, 48, N), BF),
            DMA((28,)),
            DMA((28,)),
            DMA,
        ],
        compiler_params=pltpu.CompilerParams(
            collective_id=0, has_side_effects=True, vmem_limit_bytes=48 * 1024 * 1024
        ),
        name="gather",
    )(info, x_in, rows)
    l_t = jax.ShapeDtypeStruct((2, H, N), BF)
    right, env_out, at1, at3, left_near, left_far = pl.pallas_call(
        chain_kernel,
        out_shape=(R_T, R_T, M_T, M_T, l_t, l_t),
        in_specs=[SMEM, SMEM] + [VMEM] * 4,
        out_specs=(VMEM,) * 6,
        scratch_shapes=[
            pltpu.VMEM((2, N, N), BF),
            pltpu.VMEM((2, H, T), BF),
            pltpu.VMEM((2, H, T), BF),
            pltpu.VMEM((2, N, N), BF),
            pltpu.VMEM((2, H, T), BF),
            pltpu.VMEM((2, H, T), BF),
            DMA((10,)),
            DMA((10,)),
        ],
        compiler_params=pltpu.CompilerParams(
            collective_id=1, has_side_effects=True, vmem_limit_bytes=48 * 1024 * 1024
        ),
        name="chain",
    )(info, wts, acol, pull, boundary_env, left)
    push_part = call(
        push_grad_kernel, jax.ShapeDtypeStruct((G8, 48, 4 * N), BF), 5, "push_grad"
    )(info, wts, acol, right, left, left_near, left_far)

    pull_part = call(pull_grad_kernel, jax.ShapeDtypeStruct((G8, 48, N), BF), 4, "pull_grad")(
        info, wts, pull, left, at1, at3
    )

    def scatter(part):
        for mask in (1, 4, 2):
            half = part.shape[0] // 2
            upper = (within & mask) > 0
            send = jnp.where(upper, part[:half], part[half:])
            keep = jnp.where(upper, part[half:], part[:half])
            part = (keep.astype(F32) + partner(send, mask).astype(F32)).astype(BF)
        return part[0]

    push_sum = scatter(push_part)
    pull_sum = scatter(pull_part)
    near_sum = blk_perm(push_sum[:, N : 3 * N], [(i, i - 8) for i in range(8, blk_devices)])
    far_sum = blk_perm(push_sum[:, 3 * N :], [(i, i - 16) for i in range(16, blk_devices)])
    wide = jnp.pad(pull_sum.reshape(48, 3, T), ((0, 0), (0, 0), (0, N - T))).reshape(48, 3 * N)
    rest = jnp.where(n_own > H, wide, jnp.concatenate([near_sum, far_sum], axis=1))
    grads = jnp.concatenate([push_sum[:, :N], rest], axis=1)
    return env_out[None].reshape(1, 2, N, N), grads[None]


def solution(mesh):
    return jax.shard_map(
        local,
        mesh=mesh,
        in_specs=(
            P("sect", "blk", None),
            P("sect", "blk", None, None),
            P("blk", None, None),
            P(),
            P(),
            P(),
        ),
        out_specs=(P("sect", "blk", None, None), P("sect", "blk", None)),
        check_vma=False,
    )
```

```python
import jax
import jax.numpy as jnp
from jax import lax
from jax.experimental import pallas as pl
from jax.experimental.pallas import tpu as pltpu
from jax.sharding import PartitionSpec as P

N = 384
T = 128
H = 112
G8 = 8
BF = jnp.bfloat16
F32 = jnp.float32
MESH = pl.DeviceIdType.MESH
DMA = pltpu.SemaphoreType.DMA


def mm(a, b):
    return jnp.dot(a, b, preferred_element_type=F32)


def mm_t(a, b):
    return lax.dot_general(a, b, (((1,), (1,)), ((), ())), preferred_element_type=F32)


def t_mm(a, b):
    return lax.dot_general(a, b, (((0,), (0,)), ((), ())), preferred_element_type=F32)


def mix(coef, prods, target):
    sources = ((0,), (1, 2), (1, 2), (3,))[target]
    out = []
    for w in range(2):
        total = None
        for p in sources:
            for k in range(2):
                term = coef(w, k, p, target) * prods[w ^ k][p].astype(F32)
                total = term if total is None else total + term
        out.append(total.astype(BF))
    return out


def pull_mixed(coef, pull, base, m1, m3):
    prods = []
    zero = jnp.zeros((T - H, T), BF)
    for w in range(2):
        near = jnp.concatenate([m1[w], zero], axis=0)
        far = jnp.concatenate([m3[w], zero], axis=0)
        prods.append(
            (
                None,
                mm(pull[:, base : base + T], near).astype(BF),
                mm(pull[:, base + T : base + 2 * T], near).astype(BF),
                mm(pull[:, base + 2 * T : base + 3 * T], far).astype(BF),
            )
        )
    return [None] + [mix(coef, prods, target) for target in range(1, 4)]


def combine(big, coef, pull, base, c0, m1, m3, put):
    mixed = pull_mixed(coef, pull, base, m1, m3)
    for w in range(2):
        kept = c0[w].astype(F32)
        total = kept
        for p in range(1, 4):
            total = total + mm_t(mixed[p][w], pull[:, base + (p - 1) * T : base + p * T])
        small = kept[:H, :T] + m1[w].astype(F32) + m3[w].astype(F32)
        put(
            w,
            jnp.where(big, total, jnp.zeros_like(total)).astype(BF),
            jnp.where(big, total[:H, :T], small).astype(BF),
        )
    return mixed


def remote(src, dst, sems, slot, target):
    return pltpu.make_async_remote_copy(
        src_ref=src,
        dst_ref=dst,
        send_sem=sems[0].at[slot],
        recv_sem=sems[1].at[slot],
        device_id=target,
        device_id_type=MESH,
    )


def greet(targets):
    barrier = pltpu.get_barrier_semaphore()
    for target in targets:
        pl.semaphore_signal(barrier, inc=1, device_id=target, device_id_type=MESH)
    return barrier


def write_rows(out, grads):
    for within in range(G8):
        spot = (within % 2) * 4 + within // 2
        out[spot] = grads[48 * within : 48 * within + 48].astype(BF)


def sweep_kernel(
    sizes, ops, mask, rows3, bound, left4, env4, grads3,
    acol, pull, xs, hs, ab, right, c0, m1, m3, got0, got1, got3, at1, at3, near_l, far_l,
    mx0, mxh, parts, part_in, sums, sums_in, totals, home,
    send, recv, csend, crecv, gsend, grecv, own_sem,
):
    rows, left, env_out, grads_out = rows3.at[0], left4.at[0], env4.at[0], grads3.at[0]
    sect = lax.axis_index("sect")
    blk = lax.axis_index("blk")
    within = lax.rem(blk, G8)
    base = blk - within
    sector = blk // G8
    core = lax.rem(within, 2)
    chip = within // 2
    upper = lax.rem(sect + 1, 4)
    lower = lax.rem(sect + 3, 4)
    mate = (sect, base + chip * 2 + 1 - core)
    peers = [(sect, base + lax.rem(chip + d, 4) * 2 + core) for d in (1, 2, 3)]
    origin = within // 3
    back8, back16 = lax.rem(blk + 120, 128), lax.rem(blk + 112, 128)
    fore8, fore16 = lax.rem(blk + 8, 128), lax.rem(blk + 16, 128)
    barrier = greet(
        peers
        + [mate, (upper, blk), (lower, blk)]
        + [(sect, lax.rem(base + 128 - 8 * d + origin, 128)) for d in (1, 2)]
        + [(upper, fore8), (upper, fore16), (lower, back8), (lower, back16)]
        + [(sect, back8), (sect, back16), (sect, fore8), (sect, fore16)]
    )
    goals = [[(sect, lax.rem(base + 8 * d, 128) + 3 * within + j) for j in range(3)] for d in (1, 2)]
    sends_halo = [(3 * within + j) < G8 for j in range(3)]
    for j in range(3):

        @pl.when(sends_halo[j])
        def _(j=j):
            for d in range(2):
                pl.semaphore_signal(barrier, inc=1, device_id=goals[d][j], device_id_type=MESH)

    own = [pltpu.make_async_copy(rows.at[:, pl.ds(0, N)], xs.at[within, :, pl.ds(0, N)], own_sem.at[0])]
    for p in range(1, 4):
        own.append(
            pltpu.make_async_copy(
                rows.at[:, pl.ds(N * p, T)], xs.at[within, :, pl.ds(N + T * (p - 1), T)], own_sem.at[p]
            )
        )
    for copy in own:
        copy.start()

    n_own = sizes[sector]
    n_near = jnp.where(sector >= 1, sizes[jnp.maximum(sector - 1, 0)], 0)
    n_far = jnp.where(sector >= 2, sizes[jnp.maximum(sector - 2, 0)], 0)
    big, near_big, far_big = n_own > H, n_near > H, n_far > H

    def coef(w, k, p, target):
        channel = 2 * within + w
        return ops[channel, k, p, target] * mask[channel, k].astype(F32)

    row = lax.broadcasted_iota(jnp.int32, (N, N), 0)
    col = lax.broadcasted_iota(jnp.int32, (N, N), 1)
    live = jnp.maximum(row, col) < n_own
    for w in range(2):
        right[w] = jnp.where(live, bound[w], jnp.zeros((N, N), BF))
    for copy in own:
        copy.wait()
    extra = jnp.where(within < 2, 6, jnp.where(within == 2, 4, 0))
    pl.semaphore_wait(barrier, 16 + extra)

    sems = (send, recv)

    def halo_copy(d, j):
        width = 2 * N if d == 0 else N
        at = N if d == 0 else 3 * N
        to = 0 if d == 0 else 2 * N
        return pltpu.make_async_remote_copy(
            src_ref=rows.at[pl.ds(16 * j, 16), pl.ds(at, width)],
            dst_ref=hs.at[3 * within + j, :, pl.ds(to, width)],
            send_sem=send.at[3 * d + j],
            recv_sem=recv.at[d],
            device_id=goals[d][j],
            device_id_type=MESH,
        )

    for j in range(3):

        @pl.when(sends_halo[j])
        def _(j=j):
            halo_copy(0, j).start()
            halo_copy(1, j).start()

    x_peer = [remote(xs.at[within], xs.at[within], sems, 7 + d, peers[d]) for d in range(3)]
    for copy in x_peer:
        copy.start()
    x_mate = [remote(xs.at[within], xs.at[within], sems, 10, mate)]
    x_mate[0].start()
    above = remote(xs.at[within, :, pl.ds(N, N)], ab.at[within], sems, 6, (lower, blk))
    above.start()
    csems = (csend, crecv)
    l_near = remote(left.at[:, pl.ds(0, H), :], near_l, csems, 6, (sect, fore8))
    l_far = remote(left.at[:, pl.ds(0, H), :], far_l, csems, 7, (sect, fore16))

    def landed(ref, slot):
        pltpu.make_async_remote_copy(
            src_ref=ref,
            dst_ref=ref,
            send_sem=send.at[slot],
            recv_sem=recv.at[slot],
            device_id=mate,
            device_id_type=MESH,
        ).wait_recv()

    landed(hs.at[within, :, pl.ds(0, 2 * N)], 0)
    landed(hs.at[within, :, pl.ds(2 * N, N)], 1)
    h_peer = [remote(hs.at[within], hs.at[within], sems, 21 + d, peers[d]) for d in range(3)]
    h_mate = [remote(hs.at[within], hs.at[within], sems, 24, mate)]
    for copy in h_peer + h_mate:
        copy.start()
    landed(ab.at[within], 6)
    a_peer = [remote(ab.at[within], ab.at[within], sems, 14 + d, peers[d]) for d in range(3)]
    a_mate = [remote(ab.at[within], ab.at[within], sems, 17, mate)]
    for copy in a_peer + a_mate:
        copy.start()

    def pass_on(buf, first, mine):
        for d in range(3):
            spot = lax.rem(chip + 3 - d, 4) * 2 + core
            landed(buf.at[spot], first + d)
            forward = remote(buf.at[spot], buf.at[spot], sems, first + 4 + d, mate)
            forward.start()
            mine.append(forward)

    pass_on(xs, 7, x_mate)
    pass_on(hs, 21, h_mate)
    for copy in x_mate + h_mate:
        copy.wait()
    for w in range(G8):
        line = lax.broadcasted_iota(jnp.int32, (48, N), 0) + 48 * w
        zero = jnp.zeros((48, N), BF)
        acol[48 * w : 48 * w + 48, :] = jnp.where(line < n_own, xs[w, :, :N], zero)
        pull[48 * w : 48 * w + 48, :N] = jnp.where(line < n_own, xs[w, :, N:], zero)
        halo_line = lax.broadcasted_iota(jnp.int32, (16, N), 0) + 16 * w
        for block in range(3):
            limit = n_near if block < 2 else n_far
            at = N + T * block + 16 * w
            acol[at : at + 16, :] = jnp.where(
                halo_line < limit, hs[w, :, N * block : N * block + N], jnp.zeros((16, N), BF)
            )

    def finish_above():
        pass_on(ab, 14, a_mate)
        for copy in a_mate:
            copy.wait()
        for w in range(G8):
            line = lax.broadcasted_iota(jnp.int32, (48, N), 0) + 48 * w
            pull[48 * w : 48 * w + 48, N:] = jnp.where(line < n_own, ab[w], jnp.zeros((48, N), BF))

    @pl.when(sect < 2)
    def _():
        l_near.start()
        l_far.start()

    down0 = [remote(c0.at[w], got0.at[w], csems, 2 + w, (lower, blk)) for w in range(2)]
    down1 = remote(m1, got1, csems, 0, (lower, back8))
    down3 = remote(m3, got3, csems, 1, (lower, back16))
    last1 = remote(m1, at1, csems, 4, (sect, back8))
    last3 = remote(m3, at3, csems, 5, (sect, back16))
    back0 = remote(right, env_out, csems, 8, (upper, blk))
    up1 = remote(got1, at1, csems, 9, (upper, blk))
    up3 = remote(got3, at3, csems, 10, (upper, blk))

    def put_right(w, whole, tile):
        right[w] = whole
        right[w, :H, :T] = tile

    def put_env(w, whole, tile):
        env_out[w] = whole
        env_out[w, :H, :T] = tile

    finish_above()

    @pl.when(sect < 3)
    def _():
        down1.wait_recv()
        down3.wait_recv()
        down0[0].wait_recv()
        down0[1].wait_recv()
        combine(big, coef, pull, N, got0, got1, got3, put_right)

    prods = []
    for w in range(2):
        own_p = mm(acol[:N, :], right[w]).astype(BF)
        halo_p = mm(acol[N : 2 * N, :], right[w]).astype(BF)
        prods.append((own_p, halo_p[:T], halo_p[T : 2 * T], halo_p[2 * T :]))
    for p in range(1, 4):
        blend = mix(coef, prods, p)
        for w in range(2):
            mxh[w, p - 1] = blend[w]
    for w in range(2):
        tile = right[w, :H, :T]
        near = mm_t(mxh[w, 0], acol[N : N + T, :]) + mm_t(mxh[w, 1], acol[N + T : N + 2 * T, :])
        far = mm_t(mxh[w, 2], acol[N + 2 * T : 2 * N, :])
        m1[w] = jnp.where(near_big, tile, near[:H].astype(BF))
        m3[w] = jnp.where(far_big, tile, far[:H].astype(BF))

    @pl.when(sect > 0)
    def _():
        down3.start()
        down1.start()

    @pl.when(sect == 0)
    def _():
        last3.start()
        last1.start()

    blend = mix(coef, prods, 0)
    for w in range(2):
        mx0[w] = blend[w]
        c0[w] = mm_t(blend[w], acol[:N, :]).astype(BF)

        @pl.when(sect > 0)
        def _(w=w):
            down0[w].start()

    @pl.when(sect < 3)
    def _():
        back0.start()
        up1.start()
        up3.start()

    @pl.when(sect >= 2)
    def _():
        l_near.start()
        l_far.start()

    gsems = (gsend, grecv)
    core_copy = [
        remote(parts.at[k, pl.ds((1 - core) * 4, 4)], part_in.at[k], gsems, k, mate) for k in range(5)
    ]
    peer_copy = [
        [
            remote(sums.at[k, lax.rem(chip + d + 1, 4)], sums_in.at[k, d], gsems, 5 + 3 * k + d, peers[d])
            for d in range(3)
        ]
        for k in range(5)
    ]
    home_copy = [
        remote(totals.at[k], home.at[k], gsems, 20 + k, (sect, back16 if k == 0 else back8))
        for k in range(3)
    ]

    def add_core(k):
        core_copy[k].wait_recv()
        mine = parts[k, pl.ds(core * 4, 4)]
        sums[k] = (mine.astype(F32) + part_in[k].astype(F32)).astype(BF)
        for copy in peer_copy[k]:
            copy.start()

    def add_line(k):
        for copy in peer_copy[k]:
            copy.wait_recv()
        total = sums[k, chip].astype(F32)
        for d in range(3):
            total = total + sums_in[k, d].astype(F32)
        totals[k] = total.astype(BF)

    write_rows(parts.at[3], t_mm(left[0], mx0[0]) + t_mm(left[1], mx0[1]))
    core_copy[3].start()
    l_far.wait_recv()
    write_rows(parts.at[0], t_mm(far_l[0], mxh[0, 2, :H]) + t_mm(far_l[1], mxh[1, 2, :H]))
    core_copy[0].start()
    l_near.wait_recv()
    for p in (1, 2):
        write_rows(parts.at[p], t_mm(near_l[0], mxh[0, p - 1, :H]) + t_mm(near_l[1], mxh[1, p - 1, :H]))
        core_copy[p].start()
    for k in (0, 1, 2, 3):
        add_core(k)

    @pl.when(sect == 0)
    def _():
        last1.wait_recv()
        last3.wait_recv()
        combine(big, coef, pull, 0, c0, at1, at3, put_env)

    @pl.when(sect > 0)
    def _():
        up1.wait_recv()
        up3.wait_recv()

    mixed = pull_mixed(coef, pull, 0, at1, at3)
    narrow = [t_mm(left[0], mixed[p][0]) + t_mm(left[1], mixed[p][1]) for p in range(1, 4)]
    write_rows(parts.at[4], jnp.concatenate(narrow, axis=1))
    core_copy[4].start()
    for k in range(3):
        add_line(k)
        home_copy[k].start()
    add_core(4)
    add_line(3)
    add_line(4)
    grads_out[:, :N] = totals[3]
    zero = jnp.zeros((48, N - T), BF)
    for p in range(1, 4):
        k = p % 3
        home_copy[k].wait_recv()
        thin = jnp.concatenate([totals[4, :, T * (p - 1) : T * p], zero], axis=1)
        grads_out[:, N * p : N * p + N] = jnp.where(big, thin, home[k])

    for copy in x_peer + h_peer + a_peer + [above, l_near, l_far] + core_copy + home_copy:
        copy.wait_send()
    for k in range(5):
        for copy in peer_copy[k]:
            copy.wait_send()
    for j in range(3):

        @pl.when(sends_halo[j])
        def _(j=j):
            halo_copy(0, j).wait_send()
            halo_copy(1, j).wait_send()

    @pl.when(sect == 0)
    def _():
        last1.wait_send()
        last3.wait_send()

    @pl.when(sect > 0)
    def _():
        down1.wait_send()
        down3.wait_send()
        down0[0].wait_send()
        down0[1].wait_send()
        back0.wait_recv()

    @pl.when(sect < 3)
    def _():
        back0.wait_send()
        up1.wait_send()
        up3.wait_send()


SMEM = pl.BlockSpec(memory_space=pltpu.SMEM)
VMEM = pl.BlockSpec(memory_space=pltpu.VMEM)


def local(site_tensor, left_env, boundary_env, sector_sizes, mpo_ops, mpo_mask):
    def buf(*shape):
        return pltpu.VMEM(shape, BF)

    return pl.pallas_call(
        sweep_kernel,
        out_shape=(
            jax.ShapeDtypeStruct((1, 2, N, N), BF),
            jax.ShapeDtypeStruct((1, 48, 4 * N), BF),
        ),
        in_specs=[SMEM] * 3 + [VMEM] * 3,
        out_specs=(VMEM, VMEM),
        scratch_shapes=[
            buf(2 * N, N),
            buf(N, 2 * N),
            buf(G8, 48, 2 * N),
            buf(G8, 16, 3 * N),
            buf(G8, 48, N),
            buf(2, N, N),
            buf(2, N, N),
            buf(2, H, T),
            buf(2, H, T),
            buf(2, N, N),
            buf(2, H, T),
            buf(2, H, T),
            buf(2, H, T),
            buf(2, H, T),
            buf(2, H, N),
            buf(2, H, N),
            buf(2, N, N),
            buf(2, 3, T, N),
            buf(5, G8, 48, N),
            buf(5, 4, 48, N),
            buf(5, 4, 48, N),
            buf(5, 3, 48, N),
            buf(5, 48, N),
            buf(3, 48, N),
            DMA((28,)),
            DMA((28,)),
            DMA((11,)),
            DMA((11,)),
            DMA((23,)),
            DMA((23,)),
            DMA((4,)),
        ],
        compiler_params=pltpu.CompilerParams(
            collective_id=0, has_side_effects=True, vmem_limit_bytes=48 * 1024 * 1024
        ),
        name="sweep",
    )(sector_sizes, mpo_ops, mpo_mask, site_tensor, boundary_env, left_env)


def solution(mesh):
    return jax.shard_map(
        local,
        mesh=mesh,
        in_specs=(
            P("sect", "blk", None),
            P("sect", "blk", None, None),
            P("blk", None, None),
            P(),
            P(),
            P(),
        ),
        out_specs=(P("sect", "blk", None, None), P("sect", "blk", None)),
        check_vma=False,
    )
```

```python
import jax
import jax.numpy as jnp
from jax import lax
from jax.experimental import pallas as pl
from jax.experimental.pallas import tpu as pltpu
from jax.sharding import PartitionSpec as P

N = 384
T = 128
H = 112
G8 = 8
BF = jnp.bfloat16
F32 = jnp.float32
MESH = pl.DeviceIdType.MESH
DMA = pltpu.SemaphoreType.DMA


def mm(a, b):
    return jnp.dot(a, b, preferred_element_type=F32)


def mm_t(a, b):
    return lax.dot_general(a, b, (((1,), (1,)), ((), ())), preferred_element_type=F32)


def t_mm(a, b):
    return lax.dot_general(a, b, (((0,), (0,)), ((), ())), preferred_element_type=F32)


def mix(coef, prods, target):
    sources = ((0,), (1, 2), (1, 2), (3,))[target]
    out = []
    for w in range(2):
        total = None
        for p in sources:
            for k in range(2):
                term = coef(w, k, p, target) * prods[w ^ k][p].astype(F32)
                total = term if total is None else total + term
        out.append(total.astype(BF))
    return out


def widen(tile):
    return jnp.concatenate([tile, jnp.zeros((T - H, T), BF)], axis=0)


def pull_near(coef, pull, base, m1):
    prods = []
    for w in range(2):
        near = widen(m1[w])
        prods.append(
            (
                None,
                mm(pull[:, base : base + T], near).astype(BF),
                mm(pull[:, base + T : base + 2 * T], near).astype(BF),
            )
        )
    return [mix(coef, prods, 1), mix(coef, prods, 2)]


def pull_far(coef, pull, base, m3):
    prods = [
        (None, None, None, mm(pull[:, base + 2 * T : base + 3 * T], widen(m3[w])).astype(BF))
        for w in range(2)
    ]
    return mix(coef, prods, 3)


def near_terms(mixed, pull, base, w):
    return mm_t(mixed[0][w], pull[:, base : base + T]) + mm_t(
        mixed[1][w], pull[:, base + T : base + 2 * T]
    )


def far_term(mixed, pull, base, w):
    return mm_t(mixed[w], pull[:, base + 2 * T : base + 3 * T])


def settle(big, out, w, c0, m1, m3, near, far):
    kept = c0[w].astype(F32)
    total = kept + near + far
    small = kept[:H, :T] + m1[w].astype(F32) + m3[w].astype(F32)
    out[w] = jnp.where(big, total, jnp.zeros_like(total)).astype(BF)
    out[w, :H, :T] = jnp.where(big, total[:H, :T], small).astype(BF)


def remote(src, dst, sems, slot, target):
    return pltpu.make_async_remote_copy(
        src_ref=src,
        dst_ref=dst,
        send_sem=sems[0].at[slot],
        recv_sem=sems[1].at[slot],
        device_id=target,
        device_id_type=MESH,
    )


def greet(targets):
    barrier = pltpu.get_barrier_semaphore()
    for target in targets:
        pl.semaphore_signal(barrier, inc=1, device_id=target, device_id_type=MESH)
    return barrier


def write_rows(out, grads):
    for within in range(G8):
        spot = (within % 2) * 4 + within // 2
        out[spot] = grads[48 * within : 48 * within + 48].astype(BF)


def sweep_kernel(
    sizes, ops, mask, rows3, bound_hbm, left4, env4, grads3,
    bound, left, near_acc, acol, pull, xs, hs, ab, right, c0, m1, m3, got0, got1, got3, at1, at3, near_l, far_l,
    mx0, mxh, mx_pull, parts, part_in, sums, sums_in, totals, home,
    send, recv, csend, crecv, gsend, grecv, own_sem,
):
    rows, left_hbm, env_out, grads_out = rows3.at[0], left4.at[0], env4.at[0], grads3.at[0]
    sect = lax.axis_index("sect")
    blk = lax.axis_index("blk")
    within = lax.rem(blk, G8)
    base = blk - within
    sector = blk // G8
    core = lax.rem(within, 2)
    chip = within // 2
    upper = lax.rem(sect + 1, 4)
    lower = lax.rem(sect + 3, 4)
    mate = (sect, base + chip * 2 + 1 - core)
    peers = [(sect, base + lax.rem(chip + d, 4) * 2 + core) for d in (1, 2, 3)]
    origin = within // 3
    back8, back16 = lax.rem(blk + 120, 128), lax.rem(blk + 112, 128)
    fore8, fore16 = lax.rem(blk + 8, 128), lax.rem(blk + 16, 128)
    barrier = greet(
        peers
        + [mate, (upper, blk), (lower, blk)]
        + [(sect, lax.rem(base + 128 - 8 * d + origin, 128)) for d in (1, 2)]
        + [(upper, fore8), (upper, fore16), (lower, back8), (lower, back16)]
        + [(sect, back8), (sect, back16), (sect, fore8), (sect, fore16)]
    )
    goals = [[(sect, lax.rem(base + 8 * d, 128) + 3 * within + j) for j in range(3)] for d in (1, 2)]
    sends_halo = [(3 * within + j) < G8 for j in range(3)]
    for j in range(3):

        @pl.when(sends_halo[j])
        def _(j=j):
            for d in range(2):
                pl.semaphore_signal(barrier, inc=1, device_id=goals[d][j], device_id_type=MESH)

    own = [pltpu.make_async_copy(rows.at[:, pl.ds(0, N)], xs.at[within, :, pl.ds(0, N)], own_sem.at[0])]
    for p in range(1, 4):
        own.append(
            pltpu.make_async_copy(
                rows.at[:, pl.ds(N * p, T)], xs.at[within, :, pl.ds(N + T * (p - 1), T)], own_sem.at[p]
            )
        )
    for copy in own:
        copy.start()
    bound_in = pltpu.make_async_copy(bound_hbm, bound, own_sem.at[4])
    left_in = pltpu.make_async_copy(left_hbm, left, own_sem.at[5])
    bound_in.start()
    left_in.start()

    n_own = sizes[sector]
    n_near = jnp.where(sector >= 1, sizes[jnp.maximum(sector - 1, 0)], 0)
    n_far = jnp.where(sector >= 2, sizes[jnp.maximum(sector - 2, 0)], 0)
    big, near_big, far_big = n_own > H, n_near > H, n_far > H

    def coef(w, k, p, target):
        channel = 2 * within + w
        return ops[k, p, target, channel] * mask[k, channel].astype(F32)

    bound_in.wait()
    row = lax.broadcasted_iota(jnp.int32, (N, N), 0)
    col = lax.broadcasted_iota(jnp.int32, (N, N), 1)
    live = jnp.maximum(row, col) < n_own
    for w in range(2):
        right[w] = jnp.where(live, bound[w], jnp.zeros((N, N), BF))
    for copy in own:
        copy.wait()
    extra = jnp.where(within < 2, 6, jnp.where(within == 2, 4, 0))
    pl.semaphore_wait(barrier, 16 + extra)

    sems = (send, recv)

    def halo_copy(d, j):
        width = 2 * N if d == 0 else N
        at = N if d == 0 else 3 * N
        to = 0 if d == 0 else 2 * N
        return pltpu.make_async_remote_copy(
            src_ref=rows.at[pl.ds(16 * j, 16), pl.ds(at, width)],
            dst_ref=hs.at[3 * within + j, :, pl.ds(to, width)],
            send_sem=send.at[3 * d + j],
            recv_sem=recv.at[d],
            device_id=goals[d][j],
            device_id_type=MESH,
        )

    for j in range(3):

        @pl.when(sends_halo[j])
        def _(j=j):
            halo_copy(0, j).start()
            halo_copy(1, j).start()

    x_peer = [remote(xs.at[within], xs.at[within], sems, 7 + d, peers[d]) for d in range(3)]
    for copy in x_peer:
        copy.start()
    x_mate = [remote(xs.at[within], xs.at[within], sems, 10, mate)]
    x_mate[0].start()
    above = remote(xs.at[within, :, pl.ds(N, N)], ab.at[within], sems, 6, (lower, blk))
    above.start()
    csems = (csend, crecv)
    l_near = remote(left_hbm.at[:, pl.ds(0, H), :], near_l, csems, 6, (sect, fore8))
    l_far = remote(left_hbm.at[:, pl.ds(0, H), :], far_l, csems, 7, (sect, fore16))

    def landed(ref, slot):
        pltpu.make_async_remote_copy(
            src_ref=ref,
            dst_ref=ref,
            send_sem=send.at[slot],
            recv_sem=recv.at[slot],
            device_id=mate,
            device_id_type=MESH,
        ).wait_recv()

    landed(hs.at[within, :, pl.ds(0, 2 * N)], 0)
    landed(hs.at[within, :, pl.ds(2 * N, N)], 1)
    h_peer = [remote(hs.at[within], hs.at[within], sems, 21 + d, peers[d]) for d in range(3)]
    h_mate = [remote(hs.at[within], hs.at[within], sems, 24, mate)]
    for copy in h_peer + h_mate:
        copy.start()
    landed(ab.at[within], 6)
    a_peer = [remote(ab.at[within], ab.at[within], sems, 14 + d, peers[d]) for d in range(3)]
    a_mate = [remote(ab.at[within], ab.at[within], sems, 17, mate)]
    for copy in a_peer + a_mate:
        copy.start()

    def pass_on(buf, first, mine):
        for d in range(3):
            spot = lax.rem(chip + 3 - d, 4) * 2 + core
            landed(buf.at[spot], first + d)
            forward = remote(buf.at[spot], buf.at[spot], sems, first + 4 + d, mate)
            forward.start()
            mine.append(forward)

    down0 = [remote(c0.at[w], got0.at[w], csems, 2 + w, (lower, blk)) for w in range(2)]
    down1 = remote(m1, got1, csems, 0, (lower, back8))
    down3 = remote(m3, got3, csems, 1, (lower, back16))
    last1 = remote(m1, at1, csems, 4, (sect, back8))
    last3 = remote(m3, at3, csems, 5, (sect, back16))
    back0 = remote(right, env_out, csems, 8, (upper, blk))
    up1 = remote(got1, at1, csems, 9, (upper, blk))
    up3 = remote(got3, at3, csems, 10, (upper, blk))

    def own_terms():
        prods = [(mm(acol[:N, :], right[w]).astype(BF),) for w in range(2)]
        blend = mix(coef, prods, 0)
        for w in range(2):
            mx0[w] = blend[w]
            c0[w] = mm_t(blend[w], acol[:N, :]).astype(BF)

            @pl.when(sect > 0)
            def _(w=w):
                down0[w].start()

    def finish_above():
        pass_on(ab, 14, [])
        for d in range(3):
            remote(ab.at[within], ab.at[within], sems, 18 + d, mate).wait()
        a_mate[0].wait()
        for w in range(G8):
            line = lax.broadcasted_iota(jnp.int32, (48, N), 0) + 48 * w
            pull[48 * w : 48 * w + 48, N:] = jnp.where(line < n_own, ab[w], jnp.zeros((48, N), BF))

    pass_on(xs, 7, x_mate)
    for copy in x_mate:
        copy.wait()
    for w in range(G8):
        line = lax.broadcasted_iota(jnp.int32, (48, N), 0) + 48 * w
        acol[48 * w : 48 * w + 48, :] = jnp.where(line < n_own, xs[w, :, :N], jnp.zeros((48, N), BF))

    @pl.when(sect == 3)
    def _():
        own_terms()

    pass_on(hs, 21, h_mate)
    for copy in h_mate:
        copy.wait()
    for w in range(G8):
        halo_line = lax.broadcasted_iota(jnp.int32, (16, N), 0) + 16 * w
        for block in range(3):
            limit = n_near if block < 2 else n_far
            at = N + T * block + 16 * w
            acol[at : at + 16, :] = jnp.where(
                halo_line < limit, hs[w, :, N * block : N * block + N], jnp.zeros((16, N), BF)
            )

    @pl.when(sect < 2)
    def _():
        l_near.start()
        l_far.start()

    @pl.when(sect < 3)
    def _():
        finish_above()
        down1.wait_recv()
        mixed = pull_near(coef, pull, N, got1)
        for w in range(2):
            near_acc[w] = near_terms(mixed, pull, N, w)
        down3.wait_recv()
        mixed = pull_far(coef, pull, N, got3)
        for w in range(2):
            down0[w].wait_recv()
            settle(big, right, w, got0, got1, got3, near_acc[w], far_term(mixed, pull, N, w))

    far_p = [
        (None, None, None, mm(acol[N + 2 * T : 2 * N, :], right[w]).astype(BF)) for w in range(2)
    ]
    blend = mix(coef, far_p, 3)
    for w in range(2):
        mxh[w, 2] = blend[w]
        far = mm_t(blend[w], acol[N + 2 * T : 2 * N, :])
        m3[w] = jnp.where(far_big, right[w, :H, :T], far[:H].astype(BF))

    @pl.when(sect > 0)
    def _():
        down3.start()

    @pl.when(sect == 0)
    def _():
        last3.start()

    @pl.when(sect < 3)
    def _():
        own_terms()

    near_p = []
    for w in range(2):
        both = mm(acol[N : N + 2 * T, :], right[w]).astype(BF)
        near_p.append((None, both[:T], both[T:]))
    blend = [mix(coef, near_p, p) for p in (1, 2)]
    for w in range(2):
        mxh[w, 0] = blend[0][w]
        mxh[w, 1] = blend[1][w]
        near = mm_t(blend[0][w], acol[N : N + T, :]) + mm_t(blend[1][w], acol[N + T : N + 2 * T, :])
        m1[w] = jnp.where(near_big, right[w, :H, :T], near[:H].astype(BF))

    @pl.when(sect > 0)
    def _():
        down1.start()

    @pl.when(sect == 0)
    def _():
        last1.start()

    @pl.when(sect < 3)
    def _():
        up1.start()
        up3.start()
        back0.start()

    @pl.when(sect >= 2)
    def _():
        l_near.start()
        l_far.start()

    @pl.when(sect == 3)
    def _():
        finish_above()

    for w in range(G8):
        line = lax.broadcasted_iota(jnp.int32, (48, N), 0) + 48 * w
        pull[48 * w : 48 * w + 48, :N] = jnp.where(line < n_own, xs[w, :, N:], jnp.zeros((48, N), BF))

    gsems = (gsend, grecv)
    core_copy = [
        remote(parts.at[k, pl.ds((1 - core) * 4, 4)], part_in.at[k], gsems, k, mate) for k in range(5)
    ]
    peer_copy = [
        [
            remote(sums.at[k, lax.rem(chip + d + 1, 4)], sums_in.at[k, d], gsems, 5 + 3 * k + d, peers[d])
            for d in range(3)
        ]
        for k in range(5)
    ]
    home_copy = [
        remote(totals.at[k], home.at[k], gsems, 20 + k, (sect, back16 if k == 0 else back8))
        for k in range(3)
    ]

    def add_core(k):
        core_copy[k].wait_recv()
        mine = parts[k, pl.ds(core * 4, 4)]
        sums[k] = (mine.astype(F32) + part_in[k].astype(F32)).astype(BF)
        for copy in peer_copy[k]:
            copy.start()

    def add_line(k):
        for copy in peer_copy[k]:
            copy.wait_recv()
        total = sums[k, chip].astype(F32)
        for d in range(3):
            total = total + sums_in[k, d].astype(F32)
        totals[k] = total.astype(BF)

    left_in.wait()
    l_far.wait_recv()
    write_rows(parts.at[0], t_mm(far_l[0], mxh[0, 2, :H]) + t_mm(far_l[1], mxh[1, 2, :H]))
    core_copy[0].start()
    l_near.wait_recv()
    for p in (1, 2):
        write_rows(parts.at[p], t_mm(near_l[0], mxh[0, p - 1, :H]) + t_mm(near_l[1], mxh[1, p - 1, :H]))
        core_copy[p].start()
    add_core(0)
    write_rows(parts.at[3], t_mm(left[0], mx0[0]) + t_mm(left[1], mx0[1]))
    core_copy[3].start()
    for k in (1, 2, 3):
        add_core(k)
    for k in range(3):
        add_line(k)
        home_copy[k].start()

    @pl.when(sect == 0)
    def _():
        last1.wait_recv()
        last3.wait_recv()

    @pl.when(sect > 0)
    def _():
        up1.wait_recv()
        up3.wait_recv()

    mixed = pull_near(coef, pull, 0, at1)
    mixed.append(pull_far(coef, pull, 0, at3))
    narrow = [t_mm(left[0], mixed[p][0]) + t_mm(left[1], mixed[p][1]) for p in range(3)]
    write_rows(parts.at[4], jnp.concatenate(narrow, axis=1))
    core_copy[4].start()
    add_line(3)
    for p in range(3):
        for w in range(2):
            mx_pull[w, p] = mixed[p][w]
    add_core(4)

    @pl.when(sect == 0)
    def _():
        for w in range(2):
            near = mm_t(mx_pull[w, 0], pull[:, :T]) + mm_t(mx_pull[w, 1], pull[:, T : 2 * T])
            far = mm_t(mx_pull[w, 2], pull[:, 2 * T : 3 * T])
            settle(big, env_out, w, c0, at1, at3, near, far)

    add_line(4)
    grads_out[:, :N] = totals[3]
    zero = jnp.zeros((48, N - T), BF)
    for p in range(1, 4):
        k = p % 3
        home_copy[k].wait_recv()
        thin = jnp.concatenate([totals[4, :, T * (p - 1) : T * p], zero], axis=1)
        grads_out[:, N * p : N * p + N] = jnp.where(big, thin, home[k])

    for copy in x_peer + h_peer + a_peer + [above, l_near, l_far] + core_copy + home_copy:
        copy.wait_send()
    for k in range(5):
        for copy in peer_copy[k]:
            copy.wait_send()
    for j in range(3):

        @pl.when(sends_halo[j])
        def _(j=j):
            halo_copy(0, j).wait_send()
            halo_copy(1, j).wait_send()

    @pl.when(sect == 0)
    def _():
        last1.wait_send()
        last3.wait_send()

    @pl.when(sect > 0)
    def _():
        down1.wait_send()
        down3.wait_send()
        down0[0].wait_send()
        down0[1].wait_send()
        back0.wait_recv()

    @pl.when(sect < 3)
    def _():
        back0.wait_send()
        up1.wait_send()
        up3.wait_send()


SMEM = pl.BlockSpec(memory_space=pltpu.SMEM)
VMEM = pl.BlockSpec(memory_space=pltpu.VMEM)
HBM = pl.BlockSpec(memory_space=pltpu.HBM)


def local(site_tensor, left_env, boundary_env, sector_sizes, mpo_ops, mpo_mask):
    def buf(*shape):
        return pltpu.VMEM(shape, BF)

    return pl.pallas_call(
        sweep_kernel,
        out_shape=(
            jax.ShapeDtypeStruct((1, 2, N, N), BF),
            jax.ShapeDtypeStruct((1, 48, 4 * N), BF),
        ),
        in_specs=[SMEM] * 3 + [HBM] * 3,
        out_specs=(VMEM, VMEM),
        scratch_shapes=[
            buf(2, N, N),
            buf(2, N, N),
            pltpu.VMEM((2, N, N), F32),
            buf(2 * N, N),
            buf(N, 2 * N),
            buf(G8, 48, 2 * N),
            buf(G8, 16, 3 * N),
            buf(G8, 48, N),
            buf(2, N, N),
            buf(2, N, N),
            buf(2, H, T),
            buf(2, H, T),
            buf(2, N, N),
            buf(2, H, T),
            buf(2, H, T),
            buf(2, H, T),
            buf(2, H, T),
            buf(2, H, N),
            buf(2, H, N),
            buf(2, N, N),
            buf(2, 3, T, N),
            buf(2, 3, N, T),
            buf(5, G8, 48, N),
            buf(5, 4, 48, N),
            buf(5, 4, 48, N),
            buf(5, 3, 48, N),
            buf(5, 48, N),
            buf(3, 48, N),
            DMA((28,)),
            DMA((28,)),
            DMA((11,)),
            DMA((11,)),
            DMA((23,)),
            DMA((23,)),
            DMA((6,)),
        ],
        compiler_params=pltpu.CompilerParams(
            collective_id=0, has_side_effects=True, vmem_limit_bytes=64_000_000
        ),
        name="sweep",
    )(
        sector_sizes,
        jnp.transpose(mpo_ops, (1, 2, 3, 0)),
        jnp.transpose(mpo_mask, (1, 0)),
        site_tensor,
        boundary_env,
        left_env,
    )


def solution(mesh):
    return jax.shard_map(
        local,
        mesh=mesh,
        in_specs=(
            P("sect", "blk", None),
            P("sect", "blk", None, None),
            P("blk", None, None),
            P(),
            P(),
            P(),
        ),
        out_specs=(P("sect", "blk", None, None), P("sect", "blk", None)),
        check_vma=False,
    )
```

```python
import jax
import jax.numpy as jnp
from jax import lax
from jax.experimental import pallas as pl
from jax.experimental.pallas import tpu as pltpu
from jax.sharding import PartitionSpec as P

N = 384
T = 128
H = 112
G8 = 8
BF = jnp.bfloat16
F32 = jnp.float32
MESH = pl.DeviceIdType.MESH
DMA = pltpu.SemaphoreType.DMA


def mm(a, b):
    return jnp.dot(a, b, preferred_element_type=F32)


def mm_t(a, b):
    return lax.dot_general(a, b, (((1,), (1,)), ((), ())), preferred_element_type=F32)


def t_mm(a, b):
    return lax.dot_general(a, b, (((0,), (0,)), ((), ())), preferred_element_type=F32)


def mix(coef, prods, target):
    sources = ((0,), (1, 2), (1, 2), (3,))[target]
    out = []
    for w in range(2):
        total = None
        for p in sources:
            for k in range(2):
                term = coef(w, k, p, target) * prods[w ^ k][p].astype(F32)
                total = term if total is None else total + term
        out.append(total.astype(BF))
    return out


def widen(tile):
    return jnp.concatenate([tile, jnp.zeros((T - H, T), BF)], axis=0)


def pull_near(coef, pull, base, m1):
    prods = []
    for w in range(2):
        near = widen(m1[w])
        prods.append(
            (
                None,
                mm(pull[:, base : base + T], near).astype(BF),
                mm(pull[:, base + T : base + 2 * T], near).astype(BF),
            )
        )
    return [mix(coef, prods, 1), mix(coef, prods, 2)]


def pull_far(coef, pull, base, m3):
    prods = [
        (None, None, None, mm(pull[:, base + 2 * T : base + 3 * T], widen(m3[w])).astype(BF))
        for w in range(2)
    ]
    return mix(coef, prods, 3)


def near_terms(mixed, pull, base, w):
    return mm_t(mixed[0][w], pull[:, base : base + T]) + mm_t(
        mixed[1][w], pull[:, base + T : base + 2 * T]
    )


def far_term(mixed, pull, base, w):
    return mm_t(mixed[w], pull[:, base + 2 * T : base + 3 * T])


def settle(big, out, w, c0, m1, m3, near, far):
    kept = c0[w].astype(F32)
    total = kept + near + far
    small = kept[:H, :T] + m1[w].astype(F32) + m3[w].astype(F32)
    out[w] = jnp.where(big, total, jnp.zeros_like(total)).astype(BF)
    out[w, :H, :T] = jnp.where(big, total[:H, :T], small).astype(BF)


def remote(src, dst, sems, slot, target):
    return pltpu.make_async_remote_copy(
        src_ref=src,
        dst_ref=dst,
        send_sem=sems[0].at[slot],
        recv_sem=sems[1].at[slot],
        device_id=target,
        device_id_type=MESH,
    )


def greet(targets):
    barrier = pltpu.get_barrier_semaphore()
    for target in targets:
        pl.semaphore_signal(barrier, inc=1, device_id=target, device_id_type=MESH)
    return barrier


def write_rows(out, grads):
    for within in range(G8):
        chip = within // 2
        spot = (within % 2) * 4 + (chip % 2) * 2 + chip // 2
        out[spot] = grads[48 * within : 48 * within + 48].astype(BF)


def sweep_kernel(
    sizes, ops, mask, rows3, bound_hbm, left4, env4, grads3,
    bound, left, near_acc, acol, pull, xs, hs, ab, right, c0, m1, m3, got0, got1, got3, at1, at3, near_l, far_l,
    mx0, mxh, mx_pull, parts, part_in, sums, sums_in, mids, mids_in, totals, home,
    send, recv, csend, crecv, gsend, grecv, own_sem,
):
    rows, left_hbm, env_out, grads_out = rows3.at[0], left4.at[0], env4.at[0], grads3.at[0]
    sect = lax.axis_index("sect")
    blk = lax.axis_index("blk")
    within = lax.rem(blk, G8)
    base = blk - within
    sector = blk // G8
    core = lax.rem(within, 2)
    chip = within // 2
    upper = lax.rem(sect + 1, 4)
    lower = lax.rem(sect + 3, 4)
    mate = (sect, base + chip * 2 + 1 - core)
    peers = [(sect, base + lax.rem(chip + d, 4) * 2 + core) for d in (1, 2, 3)]
    origin = within // 3
    back8, back16 = lax.rem(blk + 120, 128), lax.rem(blk + 112, 128)
    fore8, fore16 = lax.rem(blk + 8, 128), lax.rem(blk + 16, 128)
    barrier = greet(
        peers
        + [mate, (upper, blk), (lower, blk)]
        + [(sect, lax.rem(base + 128 - 8 * d + origin, 128)) for d in (1, 2)]
        + [(upper, fore8), (upper, fore16), (lower, back8), (lower, back16)]
        + [(sect, back8), (sect, back16), (sect, fore8), (sect, fore16)]
    )
    goals = [[(sect, lax.rem(base + 8 * d, 128) + 3 * within + j) for j in range(3)] for d in (1, 2)]
    sends_halo = [(3 * within + j) < G8 for j in range(3)]
    for j in range(3):

        @pl.when(sends_halo[j])
        def _(j=j):
            for d in range(2):
                pl.semaphore_signal(barrier, inc=1, device_id=goals[d][j], device_id_type=MESH)

    own = [pltpu.make_async_copy(rows.at[:, pl.ds(0, N)], xs.at[within, :, pl.ds(0, N)], own_sem.at[0])]
    for p in range(1, 4):
        own.append(
            pltpu.make_async_copy(
                rows.at[:, pl.ds(N * p, T)], xs.at[within, :, pl.ds(N + T * (p - 1), T)], own_sem.at[p]
            )
        )
    for copy in own:
        copy.start()
    bound_in = pltpu.make_async_copy(bound_hbm, bound, own_sem.at[4])
    left_in = pltpu.make_async_copy(left_hbm, left, own_sem.at[5])
    bound_in.start()
    left_in.start()

    n_own = sizes[sector]
    n_near = jnp.where(sector >= 1, sizes[jnp.maximum(sector - 1, 0)], 0)
    n_far = jnp.where(sector >= 2, sizes[jnp.maximum(sector - 2, 0)], 0)
    big, near_big, far_big = n_own > H, n_near > H, n_far > H

    def coef(w, k, p, target):
        channel = 2 * within + w
        return ops[k, p, target, channel] * mask[k, channel].astype(F32)

    bound_in.wait()
    row = lax.broadcasted_iota(jnp.int32, (N, N), 0)
    col = lax.broadcasted_iota(jnp.int32, (N, N), 1)
    live = jnp.maximum(row, col) < n_own
    for w in range(2):
        right[w] = jnp.where(live, bound[w], jnp.zeros((N, N), BF))
    for copy in own:
        copy.wait()
    extra = jnp.where(within < 2, 6, jnp.where(within == 2, 4, 0))
    pl.semaphore_wait(barrier, 16 + extra)

    sems = (send, recv)

    def halo_copy(d, j):
        width = 2 * N if d == 0 else N
        at = N if d == 0 else 3 * N
        to = 0 if d == 0 else 2 * N
        return pltpu.make_async_remote_copy(
            src_ref=rows.at[pl.ds(16 * j, 16), pl.ds(at, width)],
            dst_ref=hs.at[3 * within + j, :, pl.ds(to, width)],
            send_sem=send.at[3 * d + j],
            recv_sem=recv.at[d],
            device_id=goals[d][j],
            device_id_type=MESH,
        )

    for j in range(3):

        @pl.when(sends_halo[j])
        def _(j=j):
            halo_copy(0, j).start()
            halo_copy(1, j).start()

    x_peer = [remote(xs.at[within], xs.at[within], sems, 7 + d, peers[d]) for d in range(3)]
    for copy in x_peer:
        copy.start()
    x_mate = [remote(xs.at[within], xs.at[within], sems, 10, mate)]
    x_mate[0].start()
    above = remote(xs.at[within, :, pl.ds(N, N)], ab.at[within], sems, 6, (lower, blk))
    above.start()
    csems = (csend, crecv)
    l_near = remote(left_hbm.at[:, pl.ds(0, H), :], near_l, csems, 6, (sect, fore8))
    l_far = remote(near_l, far_l, csems, 7, (sect, fore8))

    def landed(ref, slot):
        pltpu.make_async_remote_copy(
            src_ref=ref,
            dst_ref=ref,
            send_sem=send.at[slot],
            recv_sem=recv.at[slot],
            device_id=mate,
            device_id_type=MESH,
        ).wait_recv()

    landed(hs.at[within, :, pl.ds(0, 2 * N)], 0)
    landed(hs.at[within, :, pl.ds(2 * N, N)], 1)
    h_peer = [remote(hs.at[within], hs.at[within], sems, 21 + d, peers[d]) for d in range(3)]
    h_mate = [remote(hs.at[within], hs.at[within], sems, 24, mate)]
    for copy in h_peer + h_mate:
        copy.start()
    landed(ab.at[within], 6)
    a_peer = [remote(ab.at[within], ab.at[within], sems, 14 + d, peers[d]) for d in range(3)]
    a_mate = [remote(ab.at[within], ab.at[within], sems, 17, mate)]
    for copy in a_peer + a_mate:
        copy.start()

    def pass_on(buf, first, mine):
        for d in range(3):
            spot = lax.rem(chip + 3 - d, 4) * 2 + core
            landed(buf.at[spot], first + d)
            forward = remote(buf.at[spot], buf.at[spot], sems, first + 4 + d, mate)
            forward.start()
            mine.append(forward)

    down0 = [remote(c0.at[w], got0.at[w], csems, 2 + w, (lower, blk)) for w in range(2)]
    down1 = remote(m1, got1, csems, 0, (lower, back8))
    down3 = remote(m3, got3, csems, 1, (lower, back16))
    last1 = remote(m1, at1, csems, 4, (sect, back8))
    last3 = remote(m3, at3, csems, 5, (sect, back16))
    back0 = remote(right, env_out, csems, 8, (upper, blk))
    up1 = remote(got1, at1, csems, 9, (upper, blk))
    up3 = remote(got3, at3, csems, 10, (upper, blk))

    def own_terms():
        prods = [(mm(acol[:N, :], right[w]).astype(BF),) for w in range(2)]
        blend = mix(coef, prods, 0)
        for w in range(2):
            mx0[w] = blend[w]
            c0[w] = mm_t(blend[w], acol[:N, :]).astype(BF)

            @pl.when(sect > 0)
            def _(w=w):
                down0[w].start()

    def finish_above():
        pass_on(ab, 14, [])
        for d in range(3):
            remote(ab.at[within], ab.at[within], sems, 18 + d, mate).wait()
        a_mate[0].wait()
        for w in range(G8):
            line = lax.broadcasted_iota(jnp.int32, (48, N), 0) + 48 * w
            pull[48 * w : 48 * w + 48, N:] = jnp.where(line < n_own, ab[w], jnp.zeros((48, N), BF))

    pass_on(xs, 7, x_mate)
    for copy in x_mate:
        copy.wait()
    for w in range(G8):
        line = lax.broadcasted_iota(jnp.int32, (48, N), 0) + 48 * w
        acol[48 * w : 48 * w + 48, :] = jnp.where(line < n_own, xs[w, :, :N], jnp.zeros((48, N), BF))

    @pl.when(sect == 3)
    def _():
        own_terms()

    pass_on(hs, 21, h_mate)
    for copy in h_mate:
        copy.wait()
    for w in range(G8):
        halo_line = lax.broadcasted_iota(jnp.int32, (16, N), 0) + 16 * w
        for block in range(3):
            limit = n_near if block < 2 else n_far
            at = N + T * block + 16 * w
            acol[at : at + 16, :] = jnp.where(
                halo_line < limit, hs[w, :, N * block : N * block + N], jnp.zeros((16, N), BF)
            )

    @pl.when(sect < 2)
    def _():
        l_near.start()
        finish_above()
        l_near.wait_recv()
        l_far.start()

    @pl.when(sect == 2)
    def _():
        finish_above()

    @pl.when(sect < 3)
    def _():
        down1.wait_recv()
        mixed = pull_near(coef, pull, N, got1)
        for w in range(2):
            near_acc[w] = near_terms(mixed, pull, N, w)
        down3.wait_recv()
        mixed = pull_far(coef, pull, N, got3)
        for w in range(2):
            down0[w].wait_recv()
            settle(big, right, w, got0, got1, got3, near_acc[w], far_term(mixed, pull, N, w))

    far_p = [
        (None, None, None, mm(acol[N + 2 * T : 2 * N, :], right[w]).astype(BF)) for w in range(2)
    ]
    blend = mix(coef, far_p, 3)
    for w in range(2):
        mxh[w, 2] = blend[w]
        far = mm_t(blend[w], acol[N + 2 * T : 2 * N, :])
        m3[w] = jnp.where(far_big, right[w, :H, :T], far[:H].astype(BF))

    @pl.when(sect > 0)
    def _():
        down3.start()

    @pl.when(sect == 0)
    def _():
        last3.start()

    @pl.when(sect < 3)
    def _():
        own_terms()

    near_p = []
    for w in range(2):
        both = mm(acol[N : N + 2 * T, :], right[w]).astype(BF)
        near_p.append((None, both[:T], both[T:]))
    blend = [mix(coef, near_p, p) for p in (1, 2)]
    for w in range(2):
        mxh[w, 0] = blend[0][w]
        mxh[w, 1] = blend[1][w]
        near = mm_t(blend[0][w], acol[N : N + T, :]) + mm_t(blend[1][w], acol[N + T : N + 2 * T, :])
        m1[w] = jnp.where(near_big, right[w, :H, :T], near[:H].astype(BF))

    @pl.when(sect > 0)
    def _():
        down1.start()

    @pl.when(sect == 0)
    def _():
        last1.start()

    @pl.when(sect < 3)
    def _():
        up1.start()
        up3.start()
        back0.start()

    @pl.when(sect >= 2)
    def _():
        l_near.start()

    @pl.when(sect == 3)
    def _():
        finish_above()

    for w in range(G8):
        line = lax.broadcasted_iota(jnp.int32, (48, N), 0) + 48 * w
        pull[48 * w : 48 * w + 48, :N] = jnp.where(line < n_own, xs[w, :, N:], jnp.zeros((48, N), BF))

    gsems = (gsend, grecv)
    core_copy = [
        remote(parts.at[k, pl.ds((1 - core) * 4, 4)], part_in.at[k], gsems, k, mate) for k in range(5)
    ]
    odd, half = lax.rem(chip, 2), chip // 2
    side = (sect, base + (chip + 1 - 2 * odd) * 2 + core)
    across = (sect, base + lax.rem(chip + 2, 4) * 2 + core)
    side_copy = [
        remote(sums.at[k, pl.ds((1 - odd) * 2, 2)], sums_in.at[k], gsems, 5 + k, side)
        for k in range(5)
    ]
    across_copy = [
        remote(mids.at[k, 1 - half], mids_in.at[k], gsems, 10 + k, across) for k in range(5)
    ]
    home_copy = [
        remote(totals.at[k], home.at[k], gsems, 15 + k, (sect, back16 if k == 0 else back8))
        for k in range(3)
    ]

    def add_core(k):
        core_copy[k].wait_recv()
        mine = parts[k, pl.ds(core * 4, 4)]
        sums[k] = (mine.astype(F32) + part_in[k].astype(F32)).astype(BF)
        side_copy[k].start()

    def add_side(k):
        side_copy[k].wait_recv()
        mine = sums[k, pl.ds(odd * 2, 2)]
        mids[k] = (mine.astype(F32) + sums_in[k].astype(F32)).astype(BF)
        across_copy[k].start()

    def add_across(k):
        across_copy[k].wait_recv()
        totals[k] = (mids[k, half].astype(F32) + mids_in[k].astype(F32)).astype(BF)

    left_in.wait()

    @pl.when(sect >= 2)
    def _():
        l_near.wait_recv()
        l_far.start()

    for p in (1, 2):
        write_rows(parts.at[p], t_mm(near_l[0], mxh[0, p - 1, :H]) + t_mm(near_l[1], mxh[1, p - 1, :H]))
        core_copy[p].start()
    l_far.wait_recv()
    write_rows(parts.at[0], t_mm(far_l[0], mxh[0, 2, :H]) + t_mm(far_l[1], mxh[1, 2, :H]))
    core_copy[0].start()
    add_core(1)
    add_core(2)
    write_rows(parts.at[3], t_mm(left[0], mx0[0]) + t_mm(left[1], mx0[1]))
    core_copy[3].start()
    add_core(0)
    add_side(1)
    add_side(2)
    add_side(0)
    add_core(3)
    for k in (1, 2, 0):
        add_across(k)
        home_copy[k].start()
    add_side(3)

    @pl.when(sect == 0)
    def _():
        last1.wait_recv()
        last3.wait_recv()

    @pl.when(sect > 0)
    def _():
        up1.wait_recv()
        up3.wait_recv()

    mixed = pull_near(coef, pull, 0, at1)
    mixed.append(pull_far(coef, pull, 0, at3))
    narrow = [t_mm(left[0], mixed[p][0]) + t_mm(left[1], mixed[p][1]) for p in range(3)]
    write_rows(parts.at[4], jnp.concatenate(narrow, axis=1))
    core_copy[4].start()
    add_across(3)
    for p in range(3):
        for w in range(2):
            mx_pull[w, p] = mixed[p][w]
    add_core(4)
    add_side(4)

    @pl.when(sect == 0)
    def _():
        for w in range(2):
            near = mm_t(mx_pull[w, 0], pull[:, :T]) + mm_t(mx_pull[w, 1], pull[:, T : 2 * T])
            far = mm_t(mx_pull[w, 2], pull[:, 2 * T : 3 * T])
            settle(big, env_out, w, c0, at1, at3, near, far)

    add_across(4)
    grads_out[:, :N] = totals[3]
    zero = jnp.zeros((48, N - T), BF)
    for p in range(1, 4):
        k = p % 3
        home_copy[k].wait_recv()
        thin = jnp.concatenate([totals[4, :, T * (p - 1) : T * p], zero], axis=1)
        grads_out[:, N * p : N * p + N] = jnp.where(big, thin, home[k])

    for copy in x_peer + h_peer + a_peer + [above, l_near, l_far] + core_copy + home_copy:
        copy.wait_send()
    for copy in side_copy + across_copy:
        copy.wait_send()
    for j in range(3):

        @pl.when(sends_halo[j])
        def _(j=j):
            halo_copy(0, j).wait_send()
            halo_copy(1, j).wait_send()

    @pl.when(sect == 0)
    def _():
        last1.wait_send()
        last3.wait_send()

    @pl.when(sect > 0)
    def _():
        down1.wait_send()
        down3.wait_send()
        down0[0].wait_send()
        down0[1].wait_send()
        back0.wait_recv()

    @pl.when(sect < 3)
    def _():
        back0.wait_send()
        up1.wait_send()
        up3.wait_send()


SMEM = pl.BlockSpec(memory_space=pltpu.SMEM)
VMEM = pl.BlockSpec(memory_space=pltpu.VMEM)
HBM = pl.BlockSpec(memory_space=pltpu.HBM)


def local(site_tensor, left_env, boundary_env, sector_sizes, mpo_ops, mpo_mask):
    def buf(*shape):
        return pltpu.VMEM(shape, BF)

    return pl.pallas_call(
        sweep_kernel,
        out_shape=(
            jax.ShapeDtypeStruct((1, 2, N, N), BF),
            jax.ShapeDtypeStruct((1, 48, 4 * N), BF),
        ),
        in_specs=[SMEM] * 3 + [HBM] * 3,
        out_specs=(VMEM, VMEM),
        scratch_shapes=[
            buf(2, N, N),
            buf(2, N, N),
            pltpu.VMEM((2, N, N), F32),
            buf(2 * N, N),
            buf(N, 2 * N),
            buf(G8, 48, 2 * N),
            buf(G8, 16, 3 * N),
            buf(G8, 48, N),
            buf(2, N, N),
            buf(2, N, N),
            buf(2, H, T),
            buf(2, H, T),
            buf(2, N, N),
            buf(2, H, T),
            buf(2, H, T),
            buf(2, H, T),
            buf(2, H, T),
            buf(2, H, N),
            buf(2, H, N),
            buf(2, N, N),
            buf(2, 3, T, N),
            buf(2, 3, N, T),
            buf(5, G8, 48, N),
            buf(5, 4, 48, N),
            buf(5, 4, 48, N),
            buf(5, 2, 48, N),
            buf(5, 2, 48, N),
            buf(5, 48, N),
            buf(5, 48, N),
            buf(3, 48, N),
            DMA((28,)),
            DMA((28,)),
            DMA((11,)),
            DMA((11,)),
            DMA((18,)),
            DMA((18,)),
            DMA((6,)),
        ],
        compiler_params=pltpu.CompilerParams(
            collective_id=0, has_side_effects=True, vmem_limit_bytes=64_000_000
        ),
        name="sweep",
    )(
        sector_sizes,
        jnp.transpose(mpo_ops, (1, 2, 3, 0)),
        jnp.transpose(mpo_mask, (1, 0)),
        site_tensor,
        boundary_env,
        left_env,
    )


def solution(mesh):
    return jax.shard_map(
        local,
        mesh=mesh,
        in_specs=(
            P("sect", "blk", None),
            P("sect", "blk", None, None),
            P("blk", None, None),
            P(),
            P(),
            P(),
        ),
        out_specs=(P("sect", "blk", None, None), P("sect", "blk", None)),
        check_vma=False,
    )
```

```python
import jax
import jax.numpy as jnp
from jax import lax
from jax.experimental import pallas as pl
from jax.experimental.pallas import tpu as pltpu
from jax.sharding import PartitionSpec as P

N = 384
T = 128
H = 112
G8 = 8
BF = jnp.bfloat16
F32 = jnp.float32
MESH = pl.DeviceIdType.MESH
DMA = pltpu.SemaphoreType.DMA


def mm(a, b):
    return jnp.dot(a, b, preferred_element_type=F32)


def mm_t(a, b):
    return lax.dot_general(a, b, (((1,), (1,)), ((), ())), preferred_element_type=F32)


def t_mm(a, b):
    return lax.dot_general(a, b, (((0,), (0,)), ((), ())), preferred_element_type=F32)


def mix(coef, prods, target):
    sources = ((0,), (1, 2), (1, 2), (3,))[target]
    out = []
    for w in range(2):
        total = None
        for p in sources:
            for k in range(2):
                term = coef(w, k, p, target) * prods[w ^ k][p].astype(F32)
                total = term if total is None else total + term
        out.append(total.astype(BF))
    return out


def widen(tile):
    return jnp.concatenate([tile, jnp.zeros((T - H, T), BF)], axis=0)


def pull_near(coef, pull, base, m1):
    prods = []
    for w in range(2):
        near = widen(m1[w])
        prods.append(
            (
                None,
                mm(pull[:, base : base + T], near).astype(BF),
                mm(pull[:, base + T : base + 2 * T], near).astype(BF),
            )
        )
    return [mix(coef, prods, 1), mix(coef, prods, 2)]


def pull_far(coef, pull, base, m3):
    prods = [
        (None, None, None, mm(pull[:, base + 2 * T : base + 3 * T], widen(m3[w])).astype(BF))
        for w in range(2)
    ]
    return mix(coef, prods, 3)


def near_terms(mixed, pull, base, w):
    return mm_t(mixed[0][w], pull[:, base : base + T]) + mm_t(
        mixed[1][w], pull[:, base + T : base + 2 * T]
    )


def far_term(mixed, pull, base, w):
    return mm_t(mixed[w], pull[:, base + 2 * T : base + 3 * T])


def settle(big, out, w, c0, m1, m3, near, far):
    kept = c0[w].astype(F32)
    total = kept + near + far
    small = kept[:H, :T] + m1[w].astype(F32) + m3[w].astype(F32)
    out[w] = jnp.where(big, total, jnp.zeros_like(total)).astype(BF)
    out[w, :H, :T] = jnp.where(big, total[:H, :T], small).astype(BF)


def remote(src, dst, sems, slot, target):
    return pltpu.make_async_remote_copy(
        src_ref=src,
        dst_ref=dst,
        send_sem=sems[0].at[slot],
        recv_sem=sems[1].at[slot],
        device_id=target,
        device_id_type=MESH,
    )


def greet(targets):
    barrier = pltpu.get_barrier_semaphore()
    for target in targets:
        pl.semaphore_signal(barrier, inc=1, device_id=target, device_id_type=MESH)
    return barrier


def write_rows(out, grads):
    for within in range(G8):
        chip = within // 2
        spot = (within % 2) * 4 + (chip % 2) * 2 + chip // 2
        out[spot] = grads[48 * within : 48 * within + 48].astype(BF)


def sweep_kernel(
    sizes, ops, mask, rows3, bound_hbm, left4, env4, grads3,
    bound, left, near_acc, acol, pull, xs, hn, hf, ab, right, c0, m1, m3, got0, got1, got3, at1, at3, near_l, far_l,
    mx0, mxh, mx_pull, parts, part_in, sums, sums_in, mids, mids_in, totals, home,
    send, recv, csend, crecv, gsend, grecv, own_sem,
):
    rows, left_hbm, env_out, grads_out = rows3.at[0], left4.at[0], env4.at[0], grads3.at[0]
    sect = lax.axis_index("sect")
    blk = lax.axis_index("blk")
    within = lax.rem(blk, G8)
    base = blk - within
    sector = blk // G8
    core = lax.rem(within, 2)
    chip = within // 2
    upper = lax.rem(sect + 1, 4)
    lower = lax.rem(sect + 3, 4)
    mate = (sect, base + chip * 2 + 1 - core)
    peers = [(sect, base + lax.rem(chip + d, 4) * 2 + core) for d in (1, 2, 3)]
    origin = within // 3
    back8, back16 = lax.rem(blk + 120, 128), lax.rem(blk + 112, 128)
    fore8, fore16 = lax.rem(blk + 8, 128), lax.rem(blk + 16, 128)
    barrier = greet(
        peers
        + [mate, (upper, blk), (lower, blk)]
        + [(sect, lax.rem(base + 128 - 8 * d + origin, 128)) for d in (1, 2)]
        + [(upper, fore8), (upper, fore16), (lower, back8), (lower, back16)]
        + [(sect, back8), (sect, back16), (sect, fore8), (sect, fore16)]
    )
    goals = [[(sect, lax.rem(base + 8 * d, 128) + 3 * within + j) for j in range(3)] for d in (1, 2)]
    sends_halo = [(3 * within + j) < G8 for j in range(3)]
    for j in range(3):

        @pl.when(sends_halo[j])
        def _(j=j):
            for d in range(2):
                pl.semaphore_signal(barrier, inc=1, device_id=goals[d][j], device_id_type=MESH)

    own = [pltpu.make_async_copy(rows.at[:, pl.ds(0, N)], xs.at[within, :, pl.ds(0, N)], own_sem.at[0])]
    for p in range(1, 4):
        own.append(
            pltpu.make_async_copy(
                rows.at[:, pl.ds(N * p, T)], xs.at[within, :, pl.ds(N + T * (p - 1), T)], own_sem.at[p]
            )
        )
    for copy in own:
        copy.start()
    bound_in = pltpu.make_async_copy(bound_hbm, bound, own_sem.at[4])
    left_in = pltpu.make_async_copy(left_hbm, left, own_sem.at[5])
    bound_in.start()
    left_in.start()

    n_own = sizes[sector]
    n_near = jnp.where(sector >= 1, sizes[jnp.maximum(sector - 1, 0)], 0)
    n_far = jnp.where(sector >= 2, sizes[jnp.maximum(sector - 2, 0)], 0)
    big, near_big, far_big = n_own > H, n_near > H, n_far > H

    def coef(w, k, p, target):
        channel = 2 * within + w
        return ops[k, p, target, channel] * mask[k, channel].astype(F32)

    bound_in.wait()
    row = lax.broadcasted_iota(jnp.int32, (N, N), 0)
    col = lax.broadcasted_iota(jnp.int32, (N, N), 1)
    live = jnp.maximum(row, col) < n_own
    for w in range(2):
        right[w] = jnp.where(live, bound[w], jnp.zeros((N, N), BF))
    for copy in own:
        copy.wait()
    extra = jnp.where(within < 2, 6, jnp.where(within == 2, 4, 0))
    pl.semaphore_wait(barrier, 16 + extra)

    sems = (send, recv)

    def halo_copy(d, j):
        width = 2 * N if d == 0 else N
        at = N if d == 0 else 3 * N
        return pltpu.make_async_remote_copy(
            src_ref=rows.at[pl.ds(16 * j, 16), pl.ds(at, width)],
            dst_ref=(hn if d == 0 else hf).at[3 * within + j],
            send_sem=send.at[3 * d + j],
            recv_sem=recv.at[d],
            device_id=goals[d][j],
            device_id_type=MESH,
        )

    for j in range(3):

        @pl.when(sends_halo[j])
        def _(j=j):
            halo_copy(1, j).start()
            halo_copy(0, j).start()

    x_peer = [remote(xs.at[within], xs.at[within], sems, 7 + d, peers[d]) for d in range(3)]
    for copy in x_peer:
        copy.start()
    x_mate = [remote(xs.at[within], xs.at[within], sems, 10, mate)]
    x_mate[0].start()
    above = remote(xs.at[within, :, pl.ds(N, N)], ab.at[within], sems, 6, (lower, blk))
    above.start()
    csems = (csend, crecv)
    l_near = remote(left_hbm.at[:, pl.ds(0, H), :], near_l, csems, 6, (sect, fore8))
    l_far = remote(near_l, far_l, csems, 7, (sect, fore8))

    def landed(ref, slot):
        pltpu.make_async_remote_copy(
            src_ref=ref,
            dst_ref=ref,
            send_sem=send.at[slot],
            recv_sem=recv.at[slot],
            device_id=mate,
            device_id_type=MESH,
        ).wait_recv()

    landed(hf.at[within], 1)
    f_peer = [remote(hf.at[within], hf.at[within], sems, 28 + d, peers[d]) for d in range(3)]
    f_mate = [remote(hf.at[within], hf.at[within], sems, 31, mate)]
    for copy in f_peer + f_mate:
        copy.start()
    landed(hn.at[within], 0)
    h_peer = [remote(hn.at[within], hn.at[within], sems, 21 + d, peers[d]) for d in range(3)]
    h_mate = [remote(hn.at[within], hn.at[within], sems, 24, mate)]
    for copy in h_peer + h_mate:
        copy.start()
    landed(ab.at[within], 6)
    a_peer = [remote(ab.at[within], ab.at[within], sems, 14 + d, peers[d]) for d in range(3)]
    a_mate = [remote(ab.at[within], ab.at[within], sems, 17, mate)]
    for copy in a_peer + a_mate:
        copy.start()

    def pass_on(buf, first, mine):
        for d in range(3):
            spot = lax.rem(chip + 3 - d, 4) * 2 + core
            landed(buf.at[spot], first + d)
            forward = remote(buf.at[spot], buf.at[spot], sems, first + 4 + d, mate)
            forward.start()
            mine.append(forward)

    down0 = [remote(c0.at[w], got0.at[w], csems, 2 + w, (lower, blk)) for w in range(2)]
    down1 = remote(m1, got1, csems, 0, (lower, back8))
    down3 = remote(m3, got3, csems, 1, (lower, back16))
    last1 = remote(m1, at1, csems, 4, (sect, back8))
    last3 = remote(m3, at3, csems, 5, (sect, back16))
    back0 = remote(right, env_out, csems, 8, (upper, blk))
    up1 = remote(got1, at1, csems, 9, (upper, blk))
    up3 = remote(got3, at3, csems, 10, (upper, blk))

    def own_terms():
        prods = [(mm(acol[:N, :], right[w]).astype(BF),) for w in range(2)]
        blend = mix(coef, prods, 0)
        for w in range(2):
            mx0[w] = blend[w]
            c0[w] = mm_t(blend[w], acol[:N, :]).astype(BF)

            @pl.when(sect > 0)
            def _(w=w):
                down0[w].start()

    def finish_above():
        pass_on(ab, 14, [])
        for d in range(3):
            remote(ab.at[within], ab.at[within], sems, 18 + d, mate).wait()
        a_mate[0].wait()
        for w in range(G8):
            line = lax.broadcasted_iota(jnp.int32, (48, N), 0) + 48 * w
            pull[48 * w : 48 * w + 48, N:] = jnp.where(line < n_own, ab[w], jnp.zeros((48, N), BF))

    pass_on(xs, 7, x_mate)
    for copy in x_mate:
        copy.wait()
    for w in range(G8):
        line = lax.broadcasted_iota(jnp.int32, (48, N), 0) + 48 * w
        acol[48 * w : 48 * w + 48, :] = jnp.where(line < n_own, xs[w, :, :N], jnp.zeros((48, N), BF))

    @pl.when(sect == 3)
    def _():
        own_terms()

    pass_on(hf, 28, f_mate)
    for copy in f_mate:
        copy.wait()
    for w in range(G8):
        halo_line = lax.broadcasted_iota(jnp.int32, (16, N), 0) + 16 * w
        at = N + 2 * T + 16 * w
        acol[at : at + 16, :] = jnp.where(halo_line < n_far, hf[w], jnp.zeros((16, N), BF))

    def finish_near():
        pass_on(hn, 21, [])
        for d in range(3):
            remote(hn.at[within], hn.at[within], sems, 25 + d, mate).wait()
        h_mate[0].wait()
        for w in range(G8):
            halo_line = lax.broadcasted_iota(jnp.int32, (16, N), 0) + 16 * w
            for block in range(2):
                at = N + T * block + 16 * w
                acol[at : at + 16, :] = jnp.where(
                    halo_line < n_near, hn[w, :, N * block : N * block + N], jnp.zeros((16, N), BF)
                )

    @pl.when(sect < 2)
    def _():
        l_near.start()
        finish_near()
        finish_above()
        l_near.wait_recv()
        l_far.start()

    @pl.when(sect == 2)
    def _():
        finish_near()
        finish_above()

    @pl.when(sect < 3)
    def _():
        down1.wait_recv()
        mixed = pull_near(coef, pull, N, got1)
        for w in range(2):
            near_acc[w] = near_terms(mixed, pull, N, w)
        down3.wait_recv()
        mixed = pull_far(coef, pull, N, got3)
        for w in range(2):
            down0[w].wait_recv()
            settle(big, right, w, got0, got1, got3, near_acc[w], far_term(mixed, pull, N, w))

    far_p = [
        (None, None, None, mm(acol[N + 2 * T : 2 * N, :], right[w]).astype(BF)) for w in range(2)
    ]
    blend = mix(coef, far_p, 3)
    for w in range(2):
        mxh[w, 2] = blend[w]
        far = mm_t(blend[w], acol[N + 2 * T : 2 * N, :])
        m3[w] = jnp.where(far_big, right[w, :H, :T], far[:H].astype(BF))

    @pl.when(sect > 0)
    def _():
        down3.start()

    @pl.when(sect == 0)
    def _():
        last3.start()

    @pl.when(sect < 3)
    def _():
        own_terms()

    @pl.when(sect == 3)
    def _():
        finish_near()

    near_p = []
    for w in range(2):
        both = mm(acol[N : N + 2 * T, :], right[w]).astype(BF)
        near_p.append((None, both[:T], both[T:]))
    blend = [mix(coef, near_p, p) for p in (1, 2)]
    for w in range(2):
        mxh[w, 0] = blend[0][w]
        mxh[w, 1] = blend[1][w]
        near = mm_t(blend[0][w], acol[N : N + T, :]) + mm_t(blend[1][w], acol[N + T : N + 2 * T, :])
        m1[w] = jnp.where(near_big, right[w, :H, :T], near[:H].astype(BF))

    @pl.when(sect > 0)
    def _():
        down1.start()

    @pl.when(sect == 0)
    def _():
        last1.start()

    @pl.when(sect < 3)
    def _():
        up1.start()
        up3.start()
        back0.start()

    @pl.when(sect >= 2)
    def _():
        l_near.start()

    @pl.when(sect == 3)
    def _():
        finish_above()

    for w in range(G8):
        line = lax.broadcasted_iota(jnp.int32, (48, N), 0) + 48 * w
        pull[48 * w : 48 * w + 48, :N] = jnp.where(line < n_own, xs[w, :, N:], jnp.zeros((48, N), BF))

    gsems = (gsend, grecv)
    core_copy = [
        remote(parts.at[k, pl.ds((1 - core) * 4, 4)], part_in.at[k], gsems, k, mate) for k in range(5)
    ]
    odd, half = lax.rem(chip, 2), chip // 2
    side = (sect, base + (chip + 1 - 2 * odd) * 2 + core)
    across = (sect, base + lax.rem(chip + 2, 4) * 2 + core)
    side_copy = [
        remote(sums.at[k, pl.ds((1 - odd) * 2, 2)], sums_in.at[k], gsems, 5 + k, side)
        for k in range(5)
    ]
    across_copy = [
        remote(mids.at[k, 1 - half], mids_in.at[k], gsems, 10 + k, across) for k in range(5)
    ]
    home_copy = [
        remote(totals.at[k], home.at[k], gsems, 15 + k, (sect, back16 if k == 0 else back8))
        for k in range(3)
    ]

    def add_core(k):
        core_copy[k].wait_recv()
        mine = parts[k, pl.ds(core * 4, 4)]
        sums[k] = (mine.astype(F32) + part_in[k].astype(F32)).astype(BF)
        side_copy[k].start()

    def add_side(k):
        side_copy[k].wait_recv()
        mine = sums[k, pl.ds(odd * 2, 2)]
        mids[k] = (mine.astype(F32) + sums_in[k].astype(F32)).astype(BF)
        across_copy[k].start()

    def add_across(k):
        across_copy[k].wait_recv()
        totals[k] = (mids[k, half].astype(F32) + mids_in[k].astype(F32)).astype(BF)

    left_in.wait()

    @pl.when(sect >= 2)
    def _():
        l_near.wait_recv()
        l_far.start()

    l_far.wait_recv()
    write_rows(parts.at[0], t_mm(far_l[0], mxh[0, 2, :H]) + t_mm(far_l[1], mxh[1, 2, :H]))
    core_copy[0].start()
    for p in (1, 2):
        write_rows(parts.at[p], t_mm(near_l[0], mxh[0, p - 1, :H]) + t_mm(near_l[1], mxh[1, p - 1, :H]))
        core_copy[p].start()
        if p == 1:
            add_core(0)
    add_core(1)
    write_rows(parts.at[3], t_mm(left[0], mx0[0]) + t_mm(left[1], mx0[1]))
    core_copy[3].start()
    add_side(0)
    add_core(2)
    add_side(1)
    add_across(0)
    home_copy[0].start()
    add_core(3)
    add_side(2)
    add_across(1)
    home_copy[1].start()
    add_across(2)
    home_copy[2].start()

    @pl.when(sect == 0)
    def _():
        last1.wait_recv()
        last3.wait_recv()

    @pl.when(sect > 0)
    def _():
        up1.wait_recv()
        up3.wait_recv()

    mixed = pull_near(coef, pull, 0, at1)
    mixed.append(pull_far(coef, pull, 0, at3))
    narrow = [t_mm(left[0], mixed[p][0]) + t_mm(left[1], mixed[p][1]) for p in range(3)]
    write_rows(parts.at[4], jnp.concatenate(narrow, axis=1))
    core_copy[4].start()
    add_side(3)
    for p in range(3):
        for w in range(2):
            mx_pull[w, p] = mixed[p][w]
    add_core(4)
    add_across(3)

    @pl.when(sect == 0)
    def _():
        for w in range(2):
            near = mm_t(mx_pull[w, 0], pull[:, :T]) + mm_t(mx_pull[w, 1], pull[:, T : 2 * T])
            far = mm_t(mx_pull[w, 2], pull[:, 2 * T : 3 * T])
            settle(big, env_out, w, c0, at1, at3, near, far)

    add_side(4)
    add_across(4)
    grads_out[:, :N] = totals[3]
    zero = jnp.zeros((48, N - T), BF)
    for p in range(1, 4):
        k = p % 3
        home_copy[k].wait_recv()
        thin = jnp.concatenate([totals[4, :, T * (p - 1) : T * p], zero], axis=1)
        grads_out[:, N * p : N * p + N] = jnp.where(big, thin, home[k])

    for copy in x_peer + f_peer + h_peer + a_peer + [above, l_near, l_far] + core_copy + home_copy:
        copy.wait_send()
    for copy in side_copy + across_copy:
        copy.wait_send()
    for j in range(3):

        @pl.when(sends_halo[j])
        def _(j=j):
            halo_copy(0, j).wait_send()
            halo_copy(1, j).wait_send()

    @pl.when(sect == 0)
    def _():
        last1.wait_send()
        last3.wait_send()

    @pl.when(sect > 0)
    def _():
        down1.wait_send()
        down3.wait_send()
        down0[0].wait_send()
        down0[1].wait_send()
        back0.wait_recv()

    @pl.when(sect < 3)
    def _():
        back0.wait_send()
        up1.wait_send()
        up3.wait_send()


SMEM = pl.BlockSpec(memory_space=pltpu.SMEM)
VMEM = pl.BlockSpec(memory_space=pltpu.VMEM)
HBM = pl.BlockSpec(memory_space=pltpu.HBM)


def local(site_tensor, left_env, boundary_env, sector_sizes, mpo_ops, mpo_mask):
    def buf(*shape):
        return pltpu.VMEM(shape, BF)

    return pl.pallas_call(
        sweep_kernel,
        out_shape=(
            jax.ShapeDtypeStruct((1, 2, N, N), BF),
            jax.ShapeDtypeStruct((1, 48, 4 * N), BF),
        ),
        in_specs=[SMEM] * 3 + [HBM] * 3,
        out_specs=(VMEM, VMEM),
        scratch_shapes=[
            buf(2, N, N),
            buf(2, N, N),
            pltpu.VMEM((2, N, N), F32),
            buf(2 * N, N),
            buf(N, 2 * N),
            buf(G8, 48, 2 * N),
            buf(G8, 16, 2 * N),
            buf(G8, 16, N),
            buf(G8, 48, N),
            buf(2, N, N),
            buf(2, N, N),
            buf(2, H, T),
            buf(2, H, T),
            buf(2, N, N),
            buf(2, H, T),
            buf(2, H, T),
            buf(2, H, T),
            buf(2, H, T),
            buf(2, H, N),
            buf(2, H, N),
            buf(2, N, N),
            buf(2, 3, T, N),
            buf(2, 3, N, T),
            buf(5, G8, 48, N),
            buf(5, 4, 48, N),
            buf(5, 4, 48, N),
            buf(5, 2, 48, N),
            buf(5, 2, 48, N),
            buf(5, 48, N),
            buf(5, 48, N),
            buf(3, 48, N),
            DMA((35,)),
            DMA((35,)),
            DMA((11,)),
            DMA((11,)),
            DMA((18,)),
            DMA((18,)),
            DMA((6,)),
        ],
        compiler_params=pltpu.CompilerParams(
            collective_id=0, has_side_effects=True, vmem_limit_bytes=64_000_000
        ),
        name="sweep",
    )(
        sector_sizes,
        jnp.transpose(mpo_ops, (1, 2, 3, 0)),
        jnp.transpose(mpo_mask, (1, 0)),
        site_tensor,
        boundary_env,
        left_env,
    )


def solution(mesh):
    return jax.shard_map(
        local,
        mesh=mesh,
        in_specs=(
            P("sect", "blk", None),
            P("sect", "blk", None, None),
            P("blk", None, None),
            P(),
            P(),
            P(),
        ),
        out_specs=(P("sect", "blk", None, None), P("sect", "blk", None)),
        check_vma=False,
    )
```

```python
import jax
import jax.numpy as jnp
from jax import lax
from jax.experimental import pallas as pl
from jax.experimental.pallas import tpu as pltpu
from jax.sharding import PartitionSpec as P

N = 384
T = 128
H = 112
G8 = 8
BF = jnp.bfloat16
F32 = jnp.float32
MESH = pl.DeviceIdType.MESH
DMA = pltpu.SemaphoreType.DMA


def mm(a, b):
    return jnp.dot(a, b, preferred_element_type=F32)


def mm_t(a, b):
    return lax.dot_general(a, b, (((1,), (1,)), ((), ())), preferred_element_type=F32)


def mix(coef, prods, target):
    sources = ((0,), (1, 2), (1, 2), (3,))[target]
    out = []
    for w in range(2):
        total = None
        for p in sources:
            for k in range(2):
                term = coef(w, k, p, target) * prods[w ^ k][p].astype(F32)
                total = term if total is None else total + term
        out.append(total.astype(BF))
    return out


def widen(tile):
    return jnp.concatenate([tile, jnp.zeros((T - H, T), BF)], axis=0)


def widen_wide(tile):
    return jnp.concatenate([tile, jnp.zeros((T - H, N), BF)], axis=0)


def pull_near(coef, pull, base, m1):
    prods = []
    for w in range(2):
        near = widen(m1[w])
        prods.append(
            (
                None,
                mm(pull[:, base : base + T], near).astype(BF),
                mm(pull[:, base + T : base + 2 * T], near).astype(BF),
            )
        )
    return [mix(coef, prods, 1), mix(coef, prods, 2)]


def pull_far(coef, pull, base, m3):
    prods = [
        (None, None, None, mm(pull[:, base + 2 * T : base + 3 * T], widen(m3[w])).astype(BF))
        for w in range(2)
    ]
    return mix(coef, prods, 3)


def near_terms(mixed, pull, base, w):
    return mm_t(mixed[0][w], pull[:, base : base + T]) + mm_t(
        mixed[1][w], pull[:, base + T : base + 2 * T]
    )


def far_term(mixed, pull, base, w):
    return mm_t(mixed[w], pull[:, base + 2 * T : base + 3 * T])


def settle(big, out, w, c0, m1, m3, near, far):
    kept = c0[w].astype(F32)
    total = kept + near + far
    small = kept[:H, :T] + m1[w].astype(F32) + m3[w].astype(F32)
    out[w] = jnp.where(big, total, jnp.zeros_like(total)).astype(BF)
    out[w, :H, :T] = jnp.where(big, total[:H, :T], small).astype(BF)


def remote(src, dst, sems, slot, target):
    return pltpu.make_async_remote_copy(
        src_ref=src,
        dst_ref=dst,
        send_sem=sems[0].at[slot],
        recv_sem=sems[1].at[slot],
        device_id=target,
        device_id_type=MESH,
    )


def greet(targets):
    barrier = pltpu.get_barrier_semaphore()
    for target in targets:
        pl.semaphore_signal(barrier, inc=1, device_id=target, device_id_type=MESH)
    return barrier


def write_rows(out, grads):
    for within in range(G8):
        chip = within // 2
        spot = (within % 2) * 4 + (chip % 2) * 2 + chip // 2
        out[spot] = grads[48 * within : 48 * within + 48].astype(BF)


def sweep_kernel(
    sizes, ops, mask, rows3, bound_hbm, left4, env4, grads3,
    bound, left, near_acc, acol, pull, xs, hn, hf, ab, right, c0, m1, m3, got0, got1, got3, at1, at3, near_l, far_l,
    mx0, mxh, mx_pull, left_t, near_t, far_t, parts, part_in, sums, sums_in, mids, mids_in, totals, home,
    send, recv, csend, crecv, gsend, grecv, own_sem,
):
    rows, left_hbm, env_out, grads_out = rows3.at[0], left4.at[0], env4.at[0], grads3.at[0]
    sect = lax.axis_index("sect")
    blk = lax.axis_index("blk")
    within = lax.rem(blk, G8)
    base = blk - within
    sector = blk // G8
    core = lax.rem(within, 2)
    chip = within // 2
    upper = lax.rem(sect + 1, 4)
    lower = lax.rem(sect + 3, 4)
    mate = (sect, base + chip * 2 + 1 - core)
    peers = [(sect, base + lax.rem(chip + d, 4) * 2 + core) for d in (1, 2, 3)]
    origin = within // 3
    back8, back16 = lax.rem(blk + 120, 128), lax.rem(blk + 112, 128)
    fore8, fore16 = lax.rem(blk + 8, 128), lax.rem(blk + 16, 128)
    barrier = greet(
        peers
        + [mate, (upper, blk), (lower, blk)]
        + [(sect, lax.rem(base + 128 - 8 * d + origin, 128)) for d in (1, 2)]
        + [(upper, fore8), (upper, fore16), (lower, back8), (lower, back16)]
        + [(sect, back8), (sect, back16), (sect, fore8), (sect, fore16)]
    )
    goals = [[(sect, lax.rem(base + 8 * d, 128) + 3 * within + j) for j in range(3)] for d in (1, 2)]
    sends_halo = [(3 * within + j) < G8 for j in range(3)]
    for j in range(3):

        @pl.when(sends_halo[j])
        def _(j=j):
            for d in range(2):
                pl.semaphore_signal(barrier, inc=1, device_id=goals[d][j], device_id_type=MESH)

    own = [pltpu.make_async_copy(rows.at[:, pl.ds(0, N)], xs.at[within, :, pl.ds(0, N)], own_sem.at[0])]
    for p in range(1, 4):
        own.append(
            pltpu.make_async_copy(
                rows.at[:, pl.ds(N * p, T)], xs.at[within, :, pl.ds(N + T * (p - 1), T)], own_sem.at[p]
            )
        )
    for copy in own:
        copy.start()
    bound_in = pltpu.make_async_copy(bound_hbm, bound, own_sem.at[4])
    left_in = pltpu.make_async_copy(left_hbm, left, own_sem.at[5])
    bound_in.start()
    left_in.start()

    n_own = sizes[sector]
    n_near = jnp.where(sector >= 1, sizes[jnp.maximum(sector - 1, 0)], 0)
    n_far = jnp.where(sector >= 2, sizes[jnp.maximum(sector - 2, 0)], 0)
    big, near_big, far_big = n_own > H, n_near > H, n_far > H

    def coef(w, k, p, target):
        channel = 2 * within + w
        return ops[k, p, target, channel] * mask[k, channel].astype(F32)

    bound_in.wait()
    row = lax.broadcasted_iota(jnp.int32, (N, N), 0)
    col = lax.broadcasted_iota(jnp.int32, (N, N), 1)
    live = jnp.maximum(row, col) < n_own
    for w in range(2):
        right[w] = jnp.where(live, bound[w], jnp.zeros((N, N), BF))
    for copy in own:
        copy.wait()
    extra = jnp.where(within < 2, 6, jnp.where(within == 2, 4, 0))
    pl.semaphore_wait(barrier, 16 + extra)

    sems = (send, recv)

    def halo_copy(d, j):
        width = 2 * N if d == 0 else N
        at = N if d == 0 else 3 * N
        return pltpu.make_async_remote_copy(
            src_ref=rows.at[pl.ds(16 * j, 16), pl.ds(at, width)],
            dst_ref=(hn if d == 0 else hf).at[3 * within + j],
            send_sem=send.at[3 * d + j],
            recv_sem=recv.at[d],
            device_id=goals[d][j],
            device_id_type=MESH,
        )

    for j in range(3):

        @pl.when(sends_halo[j])
        def _(j=j):
            halo_copy(1, j).start()
            halo_copy(0, j).start()

    x_peer = [remote(xs.at[within], xs.at[within], sems, 7 + d, peers[d]) for d in range(3)]
    for copy in x_peer:
        copy.start()
    x_mate = [remote(xs.at[within], xs.at[within], sems, 10, mate)]
    x_mate[0].start()
    above = remote(xs.at[within, :, pl.ds(N, N)], ab.at[within], sems, 6, (lower, blk))
    above.start()
    csems = (csend, crecv)
    l_near = remote(left_hbm.at[:, pl.ds(0, H), :], near_l, csems, 6, (sect, fore8))
    l_far = remote(near_l, far_l, csems, 7, (sect, fore8))

    def landed(ref, slot):
        pltpu.make_async_remote_copy(
            src_ref=ref,
            dst_ref=ref,
            send_sem=send.at[slot],
            recv_sem=recv.at[slot],
            device_id=mate,
            device_id_type=MESH,
        ).wait_recv()

    landed(hf.at[within], 1)
    f_peer = [remote(hf.at[within], hf.at[within], sems, 28 + d, peers[d]) for d in range(3)]
    f_mate = [remote(hf.at[within], hf.at[within], sems, 31, mate)]
    for copy in f_peer + f_mate:
        copy.start()
    landed(hn.at[within], 0)
    h_peer = [remote(hn.at[within], hn.at[within], sems, 21 + d, peers[d]) for d in range(3)]
    h_mate = [remote(hn.at[within], hn.at[within], sems, 24, mate)]
    for copy in h_peer + h_mate:
        copy.start()
    landed(ab.at[within], 6)
    a_peer = [remote(ab.at[within], ab.at[within], sems, 14 + d, peers[d]) for d in range(3)]
    a_mate = [remote(ab.at[within], ab.at[within], sems, 17, mate)]
    for copy in a_peer + a_mate:
        copy.start()

    def pass_on(buf, first, mine):
        for d in range(3):
            spot = lax.rem(chip + 3 - d, 4) * 2 + core
            landed(buf.at[spot], first + d)
            forward = remote(buf.at[spot], buf.at[spot], sems, first + 4 + d, mate)
            forward.start()
            mine.append(forward)

    down0 = [remote(c0.at[w], got0.at[w], csems, 2 + w, (lower, blk)) for w in range(2)]
    down1 = remote(m1, got1, csems, 0, (lower, back8))
    down3 = remote(m3, got3, csems, 1, (lower, back16))
    last1 = remote(m1, at1, csems, 4, (sect, back8))
    last3 = remote(m3, at3, csems, 5, (sect, back16))
    back0 = remote(right, env_out, csems, 8, (upper, blk))
    up1 = remote(got1, at1, csems, 9, (upper, blk))
    up3 = remote(got3, at3, csems, 10, (upper, blk))

    def own_terms():
        prods = [(mm(acol[:N, :], right[w]).astype(BF),) for w in range(2)]
        blend = mix(coef, prods, 0)
        for w in range(2):
            mx0[w] = blend[w]
            c0[w] = mm_t(blend[w], acol[:N, :]).astype(BF)

            @pl.when(sect > 0)
            def _(w=w):
                down0[w].start()

    def turn(tile, out):
        for w in range(2):
            out[:, T * w : T * w + T] = jnp.transpose(widen_wide(tile[w]))

    def turn_left():
        left_in.wait()
        for w in range(2):
            left_t[:, N * w : N * w + N] = jnp.transpose(left[w])

    def finish_above():
        pass_on(ab, 14, [])
        for d in range(3):
            remote(ab.at[within], ab.at[within], sems, 18 + d, mate).wait()
        a_mate[0].wait()
        for w in range(G8):
            line = lax.broadcasted_iota(jnp.int32, (48, N), 0) + 48 * w
            pull[48 * w : 48 * w + 48, N:] = jnp.where(line < n_own, ab[w], jnp.zeros((48, N), BF))

    pass_on(xs, 7, x_mate)
    for copy in x_mate:
        copy.wait()
    for w in range(G8):
        line = lax.broadcasted_iota(jnp.int32, (48, N), 0) + 48 * w
        acol[48 * w : 48 * w + 48, :] = jnp.where(line < n_own, xs[w, :, :N], jnp.zeros((48, N), BF))

    @pl.when(sect == 3)
    def _():
        own_terms()

    pass_on(hf, 28, f_mate)
    for copy in f_mate:
        copy.wait()
    for w in range(G8):
        halo_line = lax.broadcasted_iota(jnp.int32, (16, N), 0) + 16 * w
        at = N + 2 * T + 16 * w
        acol[at : at + 16, :] = jnp.where(halo_line < n_far, hf[w], jnp.zeros((16, N), BF))

    def finish_near():
        pass_on(hn, 21, [])
        for d in range(3):
            remote(hn.at[within], hn.at[within], sems, 25 + d, mate).wait()
        h_mate[0].wait()
        for w in range(G8):
            halo_line = lax.broadcasted_iota(jnp.int32, (16, N), 0) + 16 * w
            for block in range(2):
                at = N + T * block + 16 * w
                acol[at : at + 16, :] = jnp.where(
                    halo_line < n_near, hn[w, :, N * block : N * block + N], jnp.zeros((16, N), BF)
                )

    @pl.when(sect < 2)
    def _():
        l_near.start()
        finish_near()
        finish_above()
        l_near.wait_recv()
        l_far.start()
        turn(near_l, near_t)
        turn_left()

    @pl.when(sect == 0)
    def _():
        l_far.wait_recv()
        turn(far_l, far_t)

    @pl.when(sect == 2)
    def _():
        finish_near()
        finish_above()

    @pl.when(sect < 3)
    def _():
        down1.wait_recv()
        mixed = pull_near(coef, pull, N, got1)
        for w in range(2):
            near_acc[w] = near_terms(mixed, pull, N, w)
        down3.wait_recv()
        mixed = pull_far(coef, pull, N, got3)
        for w in range(2):
            down0[w].wait_recv()
            settle(big, right, w, got0, got1, got3, near_acc[w], far_term(mixed, pull, N, w))

    far_p = [
        (None, None, None, mm(acol[N + 2 * T : 2 * N, :], right[w]).astype(BF)) for w in range(2)
    ]
    blend = mix(coef, far_p, 3)
    for w in range(2):
        mxh[2, w] = blend[w]
        far = mm_t(blend[w], acol[N + 2 * T : 2 * N, :])
        m3[w] = jnp.where(far_big, right[w, :H, :T], far[:H].astype(BF))

    @pl.when(sect > 0)
    def _():
        down3.start()

    @pl.when(sect == 0)
    def _():
        last3.start()

    @pl.when((sect > 0) & (sect < 3))
    def _():
        own_terms()

    @pl.when(sect == 3)
    def _():
        finish_near()

    near_p = []
    for w in range(2):
        both = mm(acol[N : N + 2 * T, :], right[w]).astype(BF)
        near_p.append((None, both[:T], both[T:]))
    blend = [mix(coef, near_p, p) for p in (1, 2)]
    for w in range(2):
        mxh[0, w] = blend[0][w]
        mxh[1, w] = blend[1][w]
        near = mm_t(blend[0][w], acol[N : N + T, :]) + mm_t(blend[1][w], acol[N + T : N + 2 * T, :])
        m1[w] = jnp.where(near_big, right[w, :H, :T], near[:H].astype(BF))

    @pl.when(sect > 0)
    def _():
        down1.start()

    @pl.when(sect == 0)
    def _():
        last1.start()

    @pl.when(sect < 3)
    def _():
        up1.start()
        up3.start()
        back0.start()

    @pl.when(sect >= 2)
    def _():
        l_near.start()

    @pl.when(sect == 3)
    def _():
        finish_above()

    for w in range(G8):
        line = lax.broadcasted_iota(jnp.int32, (48, N), 0) + 48 * w
        pull[48 * w : 48 * w + 48, :N] = jnp.where(line < n_own, xs[w, :, N:], jnp.zeros((48, N), BF))

    gsems = (gsend, grecv)
    core_copy = [
        remote(parts.at[k, pl.ds((1 - core) * 4, 4)], part_in.at[k], gsems, k, mate) for k in range(5)
    ]
    odd, half = lax.rem(chip, 2), chip // 2
    side = (sect, base + (chip + 1 - 2 * odd) * 2 + core)
    across = (sect, base + lax.rem(chip + 2, 4) * 2 + core)
    side_copy = [
        remote(sums.at[k, pl.ds((1 - odd) * 2, 2)], sums_in.at[k], gsems, 5 + k, side)
        for k in range(5)
    ]
    across_copy = [
        remote(mids.at[k, 1 - half], mids_in.at[k], gsems, 10 + k, across) for k in range(5)
    ]
    home_copy = [
        remote(totals.at[k], home.at[k], gsems, 15 + k, (sect, back16 if k == 0 else back8))
        for k in range(3)
    ]

    def add_core(k):
        core_copy[k].wait_recv()
        mine = parts[k, pl.ds(core * 4, 4)]
        sums[k] = (mine.astype(F32) + part_in[k].astype(F32)).astype(BF)
        side_copy[k].start()

    def add_side(k):
        side_copy[k].wait_recv()
        mine = sums[k, pl.ds(odd * 2, 2)]
        mids[k] = (mine.astype(F32) + sums_in[k].astype(F32)).astype(BF)
        across_copy[k].start()

    def add_across(k):
        across_copy[k].wait_recv()
        totals[k] = (mids[k, half].astype(F32) + mids_in[k].astype(F32)).astype(BF)

    @pl.when(sect >= 2)
    def _():
        turn_left()
        l_near.wait_recv()
        l_far.start()
        turn(near_l, near_t)

    @pl.when(sect > 0)
    def _():
        l_far.wait_recv()
        turn(far_l, far_t)

    write_rows(parts.at[0], mm(far_t[...], mxh[2].reshape(2 * T, N)))
    core_copy[0].start()
    for p in (1, 2):
        write_rows(parts.at[p], mm(near_t[...], mxh[p - 1].reshape(2 * T, N)))
        core_copy[p].start()
        if p == 1:
            add_core(0)
    add_core(1)

    @pl.when(sect == 0)
    def _():
        own_terms()

    write_rows(parts.at[3], mm(left_t[...], mx0[...].reshape(2 * N, N)))
    core_copy[3].start()
    add_side(0)
    add_core(2)
    add_side(1)
    add_across(0)
    home_copy[0].start()
    add_core(3)
    add_side(2)
    add_across(1)
    home_copy[1].start()
    add_across(2)
    home_copy[2].start()

    @pl.when(sect == 0)
    def _():
        last1.wait_recv()
        last3.wait_recv()

    @pl.when(sect > 0)
    def _():
        up1.wait_recv()
        up3.wait_recv()

    mixed = pull_near(coef, pull, 0, at1)
    mixed.append(pull_far(coef, pull, 0, at3))
    narrow = [mm(left_t[...], jnp.concatenate(mixed[p], axis=0)) for p in range(3)]
    write_rows(parts.at[4], jnp.concatenate(narrow, axis=1))
    core_copy[4].start()
    add_side(3)
    for p in range(3):
        for w in range(2):
            mx_pull[w, p] = mixed[p][w]
    add_core(4)
    add_across(3)

    @pl.when(sect == 0)
    def _():
        for w in range(2):
            near = mm_t(mx_pull[w, 0], pull[:, :T]) + mm_t(mx_pull[w, 1], pull[:, T : 2 * T])
            far = mm_t(mx_pull[w, 2], pull[:, 2 * T : 3 * T])
            settle(big, env_out, w, c0, at1, at3, near, far)

    add_side(4)
    add_across(4)
    grads_out[:, :N] = totals[3]
    zero = jnp.zeros((48, N - T), BF)
    for p in range(1, 4):
        k = p % 3
        home_copy[k].wait_recv()
        thin = jnp.concatenate([totals[4, :, T * (p - 1) : T * p], zero], axis=1)
        grads_out[:, N * p : N * p + N] = jnp.where(big, thin, home[k])

    for copy in x_peer + f_peer + h_peer + a_peer + [above, l_near, l_far] + core_copy + home_copy:
        copy.wait_send()
    for copy in side_copy + across_copy:
        copy.wait_send()
    for j in range(3):

        @pl.when(sends_halo[j])
        def _(j=j):
            halo_copy(0, j).wait_send()
            halo_copy(1, j).wait_send()

    @pl.when(sect == 0)
    def _():
        last1.wait_send()
        last3.wait_send()

    @pl.when(sect > 0)
    def _():
        down1.wait_send()
        down3.wait_send()
        down0[0].wait_send()
        down0[1].wait_send()
        back0.wait_recv()

    @pl.when(sect < 3)
    def _():
        back0.wait_send()
        up1.wait_send()
        up3.wait_send()


SMEM = pl.BlockSpec(memory_space=pltpu.SMEM)
VMEM = pl.BlockSpec(memory_space=pltpu.VMEM)
HBM = pl.BlockSpec(memory_space=pltpu.HBM)


def local(site_tensor, left_env, boundary_env, sector_sizes, mpo_ops, mpo_mask):
    def buf(*shape):
        return pltpu.VMEM(shape, BF)

    return pl.pallas_call(
        sweep_kernel,
        out_shape=(
            jax.ShapeDtypeStruct((1, 2, N, N), BF),
            jax.ShapeDtypeStruct((1, 48, 4 * N), BF),
        ),
        in_specs=[SMEM] * 3 + [HBM] * 3,
        out_specs=(VMEM, VMEM),
        scratch_shapes=[
            buf(2, N, N),
            buf(2, N, N),
            pltpu.VMEM((2, N, N), F32),
            buf(2 * N, N),
            buf(N, 2 * N),
            buf(G8, 48, 2 * N),
            buf(G8, 16, 2 * N),
            buf(G8, 16, N),
            buf(G8, 48, N),
            buf(2, N, N),
            buf(2, N, N),
            buf(2, H, T),
            buf(2, H, T),
            buf(2, N, N),
            buf(2, H, T),
            buf(2, H, T),
            buf(2, H, T),
            buf(2, H, T),
            buf(2, H, N),
            buf(2, H, N),
            buf(2, N, N),
            buf(3, 2, T, N),
            buf(2, 3, N, T),
            buf(N, 2 * N),
            buf(N, 2 * T),
            buf(N, 2 * T),
            buf(5, G8, 48, N),
            buf(5, 4, 48, N),
            buf(5, 4, 48, N),
            buf(5, 2, 48, N),
            buf(5, 2, 48, N),
            buf(5, 48, N),
            buf(5, 48, N),
            buf(3, 48, N),
            DMA((35,)),
            DMA((35,)),
            DMA((11,)),
            DMA((11,)),
            DMA((18,)),
            DMA((18,)),
            DMA((6,)),
        ],
        compiler_params=pltpu.CompilerParams(
            collective_id=0, has_side_effects=True, vmem_limit_bytes=50_000_000
        ),
        name="sweep",
    )(
        sector_sizes,
        jnp.transpose(mpo_ops, (1, 2, 3, 0)),
        jnp.transpose(mpo_mask, (1, 0)),
        *[pltpu.with_memory_space_constraint(a, pltpu.HBM) for a in (site_tensor, boundary_env, left_env)],
    )


def solution(mesh):
    return jax.shard_map(
        local,
        mesh=mesh,
        in_specs=(
            P("sect", "blk", None),
            P("sect", "blk", None, None),
            P("blk", None, None),
            P(),
            P(),
            P(),
        ),
        out_specs=(P("sect", "blk", None, None), P("sect", "blk", None)),
        check_vma=False,
    )
```

```python
import jax
import jax.numpy as jnp
from jax import lax
from jax.experimental import pallas as pl
from jax.experimental.pallas import tpu as pltpu
from jax.sharding import PartitionSpec as P

N = 384
T = 128
H = 112
G8 = 8
BF = jnp.bfloat16
F32 = jnp.float32
MESH = pl.DeviceIdType.MESH
DMA = pltpu.SemaphoreType.DMA


def mm(a, b):
    return jnp.dot(a, b, preferred_element_type=F32)


def mm_t(a, b):
    return lax.dot_general(a, b, (((1,), (1,)), ((), ())), preferred_element_type=F32)


def mix(coef, prods, target):
    sources = ((0,), (1, 2), (1, 2), (3,))[target]
    out = []
    for w in range(2):
        total = None
        for p in sources:
            for k in range(2):
                term = coef(w, k, p, target) * prods[w ^ k][p].astype(F32)
                total = term if total is None else total + term
        out.append(total.astype(BF))
    return out


def widen(tile):
    return jnp.concatenate([tile, jnp.zeros((T - H, T), BF)], axis=0)


def widen_wide(tile):
    return jnp.concatenate([tile, jnp.zeros((T - H, N), BF)], axis=0)


def pull_near(coef, pull, base, m1):
    prods = []
    for w in range(2):
        near = widen(m1[w])
        prods.append(
            (
                None,
                mm(pull[:, base : base + T], near).astype(BF),
                mm(pull[:, base + T : base + 2 * T], near).astype(BF),
            )
        )
    return [mix(coef, prods, 1), mix(coef, prods, 2)]


def pull_far(coef, pull, base, m3):
    prods = [
        (None, None, None, mm(pull[:, base + 2 * T : base + 3 * T], widen(m3[w])).astype(BF))
        for w in range(2)
    ]
    return mix(coef, prods, 3)


def near_terms(mixed, pull, base, w):
    return mm_t(mixed[0][w], pull[:, base : base + T]) + mm_t(
        mixed[1][w], pull[:, base + T : base + 2 * T]
    )


def far_term(mixed, pull, base, w):
    return mm_t(mixed[w], pull[:, base + 2 * T : base + 3 * T])


def settle(big, out, w, c0, m1, m3, near, far):
    kept = c0[w].astype(F32)
    total = kept + near + far
    small = kept[:H, :T] + m1[w].astype(F32) + m3[w].astype(F32)
    out[w] = jnp.where(big, total, jnp.zeros_like(total)).astype(BF)
    out[w, :H, :T] = jnp.where(big, total[:H, :T], small).astype(BF)


def remote(src, dst, sems, slot, target):
    return pltpu.make_async_remote_copy(
        src_ref=src,
        dst_ref=dst,
        send_sem=sems[0].at[slot],
        recv_sem=sems[1].at[slot],
        device_id=target,
        device_id_type=MESH,
    )


def greet(targets):
    barrier = pltpu.get_barrier_semaphore()
    for target in targets:
        pl.semaphore_signal(barrier, inc=1, device_id=target, device_id_type=MESH)
    return barrier


def write_rows(out, grads):
    for within in range(G8):
        chip = within // 2
        spot = (within % 2) * 4 + (chip % 2) * 2 + chip // 2
        out[spot] = grads[48 * within : 48 * within + 48].astype(BF)


def sweep_kernel(
    sizes, ops, mask, rows3, bound_hbm, left4, env4, grads3,
    bound, left, near_acc, acol, pull, xs, hn, hf, ab, right, c0, m1, m3, got0, got1, got3, at1, at3, near_l, far_l,
    mx0, mxh, mx_pull, left_t, near_t, far_t, parts, part_in, sums, sums_in, mids, mids_in, totals, home,
    send, recv, csend, crecv, gsend, grecv, own_sem,
):
    rows, left_hbm, env_out, grads_out = rows3.at[0], left4.at[0], env4.at[0], grads3.at[0]
    sect = lax.axis_index("sect")
    blk = lax.axis_index("blk")
    within = lax.rem(blk, G8)
    base = blk - within
    sector = blk // G8
    core = lax.rem(within, 2)
    chip = within // 2
    upper = lax.rem(sect + 1, 4)
    lower = lax.rem(sect + 3, 4)
    mate = (sect, base + chip * 2 + 1 - core)
    peers = [(sect, base + lax.rem(chip + d, 4) * 2 + core) for d in (1, 2, 3)]
    origin = within // 3
    back8, back16 = lax.rem(blk + 120, 128), lax.rem(blk + 112, 128)
    fore8, fore16 = lax.rem(blk + 8, 128), lax.rem(blk + 16, 128)
    barrier = greet(
        peers
        + [mate, (upper, blk), (lower, blk)]
        + [(sect, lax.rem(base + 128 - 8 * d + origin, 128)) for d in (1, 2)]
        + [(upper, fore8), (upper, fore16), (lower, back8), (lower, back16)]
        + [(sect, back8), (sect, back16), (sect, fore8), (sect, fore16)]
    )
    goals = [[(sect, lax.rem(base + 8 * d, 128) + 3 * within + j) for j in range(3)] for d in (1, 2)]
    sends_halo = [(3 * within + j) < G8 for j in range(3)]
    for j in range(3):

        @pl.when(sends_halo[j])
        def _(j=j):
            for d in range(2):
                pl.semaphore_signal(barrier, inc=1, device_id=goals[d][j], device_id_type=MESH)

    own = [pltpu.make_async_copy(rows.at[:, pl.ds(0, N)], xs.at[within], own_sem.at[0])]
    for p in range(1, 4):
        own.append(
            pltpu.make_async_copy(
                rows.at[:, pl.ds(N * p, T)], ab.at[within, :, pl.ds(T * (p - 1), T)], own_sem.at[p]
            )
        )
    for copy in own:
        copy.start()
    bound_in = pltpu.make_async_copy(bound_hbm, bound, own_sem.at[4])
    left_in = pltpu.make_async_copy(left_hbm, left, own_sem.at[5])
    bound_in.start()
    left_in.start()

    n_own = sizes[sector]
    n_near = jnp.where(sector >= 1, sizes[jnp.maximum(sector - 1, 0)], 0)
    n_far = jnp.where(sector >= 2, sizes[jnp.maximum(sector - 2, 0)], 0)
    big, near_big, far_big = n_own > H, n_near > H, n_far > H

    def coef(w, k, p, target):
        channel = 2 * within + w
        return ops[k, p, target, channel] * mask[k, channel].astype(F32)

    bound_in.wait()
    row = lax.broadcasted_iota(jnp.int32, (N, N), 0)
    col = lax.broadcasted_iota(jnp.int32, (N, N), 1)
    live = jnp.maximum(row, col) < n_own
    for w in range(2):
        right[w] = jnp.where(live, bound[w], jnp.zeros((N, N), BF))
    for copy in own:
        copy.wait()
    extra = jnp.where(within < 2, 6, jnp.where(within == 2, 4, 0))
    pl.semaphore_wait(barrier, 16 + extra)

    sems = (send, recv)

    def halo_copy(d, j):
        width = 2 * N if d == 0 else N
        at = N if d == 0 else 3 * N
        return pltpu.make_async_remote_copy(
            src_ref=rows.at[pl.ds(16 * j, 16), pl.ds(at, width)],
            dst_ref=(hn if d == 0 else hf).at[3 * within + j],
            send_sem=send.at[3 * d + j],
            recv_sem=recv.at[d],
            device_id=goals[d][j],
            device_id_type=MESH,
        )

    for j in range(3):

        @pl.when(sends_halo[j])
        def _(j=j):
            halo_copy(1, j).start()
            halo_copy(0, j).start()

    x_peer = [remote(xs.at[within], xs.at[within], sems, 7 + d, peers[d]) for d in range(3)]
    for copy in x_peer:
        copy.start()
    x_mate = [remote(xs.at[within], xs.at[within], sems, 10, mate)]
    x_mate[0].start()
    above = remote(
        ab.at[within, :, pl.ds(0, N)], ab.at[within, :, pl.ds(N, N)], sems, 6, (lower, blk)
    )
    above.start()
    csems = (csend, crecv)
    l_near = remote(left_hbm.at[:, pl.ds(0, H), :], near_l, csems, 6, (sect, fore8))
    l_far = remote(near_l, far_l, csems, 7, (sect, fore8))

    def landed(ref, slot):
        pltpu.make_async_remote_copy(
            src_ref=ref,
            dst_ref=ref,
            send_sem=send.at[slot],
            recv_sem=recv.at[slot],
            device_id=mate,
            device_id_type=MESH,
        ).wait_recv()

    landed(hf.at[within], 1)
    f_peer = [remote(hf.at[within], hf.at[within], sems, 28 + d, peers[d]) for d in range(3)]
    f_mate = [remote(hf.at[within], hf.at[within], sems, 31, mate)]
    for copy in f_peer + f_mate:
        copy.start()
    landed(hn.at[within], 0)
    h_peer = [remote(hn.at[within], hn.at[within], sems, 21 + d, peers[d]) for d in range(3)]
    h_mate = [remote(hn.at[within], hn.at[within], sems, 24, mate)]
    for copy in h_peer + h_mate:
        copy.start()
    landed(ab.at[within, :, pl.ds(N, N)], 6)
    a_peer = [remote(ab.at[within], ab.at[within], sems, 14 + d, peers[d]) for d in range(3)]
    a_mate = [remote(ab.at[within], ab.at[within], sems, 17, mate)]
    for copy in a_peer + a_mate:
        copy.start()

    def pass_on(buf, first, mine):
        for d in range(3):
            spot = lax.rem(chip + 3 - d, 4) * 2 + core
            landed(buf.at[spot], first + d)
            forward = remote(buf.at[spot], buf.at[spot], sems, first + 4 + d, mate)
            forward.start()
            mine.append(forward)

    down0 = [remote(c0.at[w], got0.at[w], csems, 2 + w, (lower, blk)) for w in range(2)]
    down1 = remote(m1, got1, csems, 0, (lower, back8))
    down3 = remote(m3, got3, csems, 1, (lower, back16))
    last1 = remote(m1, at1, csems, 4, (sect, back8))
    last3 = remote(m3, at3, csems, 5, (sect, back16))
    back0 = remote(right, env_out, csems, 8, (upper, blk))
    up1 = remote(got1, at1, csems, 9, (upper, blk))
    up3 = remote(got3, at3, csems, 10, (upper, blk))

    def own_terms():
        prods = [(mm(acol[:N, :], right[w]).astype(BF),) for w in range(2)]
        blend = mix(coef, prods, 0)
        for w in range(2):
            mx0[w] = blend[w]
            c0[w] = mm_t(blend[w], acol[:N, :]).astype(BF)

            @pl.when(sect > 0)
            def _(w=w):
                down0[w].start()

    def turn(tile, out):
        for w in range(2):
            out[:, T * w : T * w + T] = jnp.transpose(widen_wide(tile[w]))

    def turn_left():
        left_in.wait()
        for w in range(2):
            left_t[:, N * w : N * w + N] = jnp.transpose(left[w])

    def finish_above():
        pass_on(ab, 14, [])
        for d in range(3):
            remote(ab.at[within], ab.at[within], sems, 18 + d, mate).wait()
        a_mate[0].wait()
        for w in range(G8):
            line = lax.broadcasted_iota(jnp.int32, (48, 2 * N), 0) + 48 * w
            pull[48 * w : 48 * w + 48, :] = jnp.where(
                line < n_own, ab[w], jnp.zeros((48, 2 * N), BF)
            )

    pass_on(xs, 7, x_mate)
    for copy in x_mate:
        copy.wait()
    for w in range(G8):
        line = lax.broadcasted_iota(jnp.int32, (48, N), 0) + 48 * w
        acol[48 * w : 48 * w + 48, :] = jnp.where(line < n_own, xs[w], jnp.zeros((48, N), BF))

    @pl.when(sect == 3)
    def _():
        own_terms()

    pass_on(hf, 28, f_mate)
    for copy in f_mate:
        copy.wait()
    for w in range(G8):
        halo_line = lax.broadcasted_iota(jnp.int32, (16, N), 0) + 16 * w
        at = N + 2 * T + 16 * w
        acol[at : at + 16, :] = jnp.where(halo_line < n_far, hf[w], jnp.zeros((16, N), BF))

    def finish_near():
        pass_on(hn, 21, [])
        for d in range(3):
            remote(hn.at[within], hn.at[within], sems, 25 + d, mate).wait()
        h_mate[0].wait()
        for w in range(G8):
            halo_line = lax.broadcasted_iota(jnp.int32, (16, N), 0) + 16 * w
            for block in range(2):
                at = N + T * block + 16 * w
                acol[at : at + 16, :] = jnp.where(
                    halo_line < n_near, hn[w, :, N * block : N * block + N], jnp.zeros((16, N), BF)
                )

    @pl.when(sect < 2)
    def _():
        l_near.start()
        finish_near()
        finish_above()
        l_near.wait_recv()
        l_far.start()
        turn(near_l, near_t)
        turn_left()

    @pl.when(sect == 0)
    def _():
        l_far.wait_recv()
        turn(far_l, far_t)

    @pl.when(sect == 2)
    def _():
        finish_near()
        finish_above()

    @pl.when(sect < 3)
    def _():
        down1.wait_recv()
        mixed = pull_near(coef, pull, N, got1)
        for w in range(2):
            near_acc[w] = near_terms(mixed, pull, N, w)
        down3.wait_recv()
        mixed = pull_far(coef, pull, N, got3)
        for w in range(2):
            down0[w].wait_recv()
            settle(big, right, w, got0, got1, got3, near_acc[w], far_term(mixed, pull, N, w))

    far_p = [
        (None, None, None, mm(acol[N + 2 * T : 2 * N, :], right[w]).astype(BF)) for w in range(2)
    ]
    blend = mix(coef, far_p, 3)
    for w in range(2):
        mxh[2, w] = blend[w]
        far = mm_t(blend[w], acol[N + 2 * T : 2 * N, :])
        m3[w] = jnp.where(far_big, right[w, :H, :T], far[:H].astype(BF))

    @pl.when(sect > 0)
    def _():
        down3.start()

    @pl.when(sect == 0)
    def _():
        last3.start()

    @pl.when((sect > 0) & (sect < 3))
    def _():
        own_terms()

    @pl.when(sect == 3)
    def _():
        finish_near()

    near_p = []
    for w in range(2):
        both = mm(acol[N : N + 2 * T, :], right[w]).astype(BF)
        near_p.append((None, both[:T], both[T:]))
    blend = [mix(coef, near_p, p) for p in (1, 2)]
    for w in range(2):
        mxh[0, w] = blend[0][w]
        mxh[1, w] = blend[1][w]
        near = mm_t(blend[0][w], acol[N : N + T, :]) + mm_t(blend[1][w], acol[N + T : N + 2 * T, :])
        m1[w] = jnp.where(near_big, right[w, :H, :T], near[:H].astype(BF))

    @pl.when(sect > 0)
    def _():
        down1.start()

    @pl.when(sect == 0)
    def _():
        last1.start()

    @pl.when(sect < 3)
    def _():
        up1.start()
        up3.start()
        back0.start()

    @pl.when(sect >= 2)
    def _():
        l_near.start()

    @pl.when(sect == 3)
    def _():
        finish_above()


    gsems = (gsend, grecv)
    core_copy = [
        remote(parts.at[k, pl.ds((1 - core) * 4, 4)], part_in.at[k], gsems, k, mate) for k in range(5)
    ]
    odd, half = lax.rem(chip, 2), chip // 2
    side = (sect, base + (chip + 1 - 2 * odd) * 2 + core)
    across = (sect, base + lax.rem(chip + 2, 4) * 2 + core)
    side_copy = [
        remote(sums.at[k, pl.ds((1 - odd) * 2, 2)], sums_in.at[k], gsems, 5 + k, side)
        for k in range(5)
    ]
    across_copy = [
        remote(mids.at[k, 1 - half], mids_in.at[k], gsems, 10 + k, across) for k in range(5)
    ]
    home_copy = [
        remote(totals.at[k], home.at[k], gsems, 15 + k, (sect, back16 if k == 0 else back8))
        for k in range(3)
    ]

    def add_core(k):
        core_copy[k].wait_recv()
        mine = parts[k, pl.ds(core * 4, 4)]
        sums[k] = (mine.astype(F32) + part_in[k].astype(F32)).astype(BF)
        side_copy[k].start()

    def add_side(k):
        side_copy[k].wait_recv()
        mine = sums[k, pl.ds(odd * 2, 2)]
        mids[k] = (mine.astype(F32) + sums_in[k].astype(F32)).astype(BF)
        across_copy[k].start()

    def add_across(k):
        across_copy[k].wait_recv()
        totals[k] = (mids[k, half].astype(F32) + mids_in[k].astype(F32)).astype(BF)

    @pl.when(sect >= 2)
    def _():
        turn_left()
        l_near.wait_recv()
        l_far.start()
        turn(near_l, near_t)

    @pl.when(sect > 0)
    def _():
        l_far.wait_recv()
        turn(far_l, far_t)

    write_rows(parts.at[0], mm(far_t[...], mxh[2].reshape(2 * T, N)))
    core_copy[0].start()
    for p in (1, 2):
        write_rows(parts.at[p], mm(near_t[...], mxh[p - 1].reshape(2 * T, N)))
        core_copy[p].start()
        if p == 1:
            add_core(0)
    add_core(1)

    @pl.when(sect == 0)
    def _():
        own_terms()

    write_rows(parts.at[3], mm(left_t[...], mx0[...].reshape(2 * N, N)))
    core_copy[3].start()
    add_side(0)
    add_core(2)
    add_side(1)
    add_across(0)
    home_copy[0].start()
    add_core(3)
    add_side(2)
    add_across(1)
    home_copy[1].start()
    add_across(2)
    home_copy[2].start()

    @pl.when(sect == 0)
    def _():
        last1.wait_recv()
        last3.wait_recv()

    @pl.when(sect > 0)
    def _():
        up1.wait_recv()
        up3.wait_recv()

    mixed = pull_near(coef, pull, 0, at1)
    mixed.append(pull_far(coef, pull, 0, at3))
    narrow = [mm(left_t[...], jnp.concatenate(mixed[p], axis=0)) for p in range(3)]
    write_rows(parts.at[4], jnp.concatenate(narrow, axis=1))
    core_copy[4].start()
    add_side(3)
    for p in range(3):
        for w in range(2):
            mx_pull[w, p] = mixed[p][w]
    add_core(4)
    add_across(3)

    @pl.when(sect == 0)
    def _():
        for w in range(2):
            near = mm_t(mx_pull[w, 0], pull[:, :T]) + mm_t(mx_pull[w, 1], pull[:, T : 2 * T])
            far = mm_t(mx_pull[w, 2], pull[:, 2 * T : 3 * T])
            settle(big, env_out, w, c0, at1, at3, near, far)

    add_side(4)
    add_across(4)
    grads_out[:, :N] = totals[3]
    zero = jnp.zeros((48, N - T), BF)
    for p in range(1, 4):
        k = p % 3
        home_copy[k].wait_recv()
        thin = jnp.concatenate([totals[4, :, T * (p - 1) : T * p], zero], axis=1)
        grads_out[:, N * p : N * p + N] = jnp.where(big, thin, home[k])

    for copy in x_peer + f_peer + h_peer + a_peer + [above, l_near, l_far] + core_copy + home_copy:
        copy.wait_send()
    for copy in side_copy + across_copy:
        copy.wait_send()
    for j in range(3):

        @pl.when(sends_halo[j])
        def _(j=j):
            halo_copy(0, j).wait_send()
            halo_copy(1, j).wait_send()

    @pl.when(sect == 0)
    def _():
        last1.wait_send()
        last3.wait_send()

    @pl.when(sect > 0)
    def _():
        down1.wait_send()
        down3.wait_send()
        down0[0].wait_send()
        down0[1].wait_send()
        back0.wait_recv()

    @pl.when(sect < 3)
    def _():
        back0.wait_send()
        up1.wait_send()
        up3.wait_send()


SMEM = pl.BlockSpec(memory_space=pltpu.SMEM)
VMEM = pl.BlockSpec(memory_space=pltpu.VMEM)
HBM = pl.BlockSpec(memory_space=pltpu.HBM)


def local(site_tensor, left_env, boundary_env, sector_sizes, mpo_ops, mpo_mask):
    def buf(*shape):
        return pltpu.VMEM(shape, BF)

    return pl.pallas_call(
        sweep_kernel,
        out_shape=(
            jax.ShapeDtypeStruct((1, 2, N, N), BF),
            jax.ShapeDtypeStruct((1, 48, 4 * N), BF),
        ),
        in_specs=[SMEM] * 3 + [HBM] * 3,
        out_specs=(VMEM, VMEM),
        scratch_shapes=[
            buf(2, N, N),
            buf(2, N, N),
            pltpu.VMEM((2, N, N), F32),
            buf(2 * N, N),
            buf(N, 2 * N),
            buf(G8, 48, N),
            buf(G8, 16, 2 * N),
            buf(G8, 16, N),
            buf(G8, 48, 2 * N),
            buf(2, N, N),
            buf(2, N, N),
            buf(2, H, T),
            buf(2, H, T),
            buf(2, N, N),
            buf(2, H, T),
            buf(2, H, T),
            buf(2, H, T),
            buf(2, H, T),
            buf(2, H, N),
            buf(2, H, N),
            buf(2, N, N),
            buf(3, 2, T, N),
            buf(2, 3, N, T),
            buf(N, 2 * N),
            buf(N, 2 * T),
            buf(N, 2 * T),
            buf(5, G8, 48, N),
            buf(5, 4, 48, N),
            buf(5, 4, 48, N),
            buf(5, 2, 48, N),
            buf(5, 2, 48, N),
            buf(5, 48, N),
            buf(5, 48, N),
            buf(3, 48, N),
            DMA((35,)),
            DMA((35,)),
            DMA((11,)),
            DMA((11,)),
            DMA((18,)),
            DMA((18,)),
            DMA((6,)),
        ],
        compiler_params=pltpu.CompilerParams(
            collective_id=0, has_side_effects=True, vmem_limit_bytes=50_000_000
        ),
        name="sweep",
    )(
        sector_sizes,
        jnp.transpose(mpo_ops, (1, 2, 3, 0)),
        jnp.transpose(mpo_mask, (1, 0)),
        *[pltpu.with_memory_space_constraint(a, pltpu.HBM) for a in (site_tensor, boundary_env, left_env)],
    )


def solution(mesh):
    return jax.shard_map(
        local,
        mesh=mesh,
        in_specs=(
            P("sect", "blk", None),
            P("sect", "blk", None, None),
            P("blk", None, None),
            P(),
            P(),
            P(),
        ),
        out_specs=(P("sect", "blk", None, None), P("sect", "blk", None)),
        check_vma=False,
    )
```

```python
import jax
import jax.numpy as jnp
from jax import lax
from jax.experimental import pallas as pl
from jax.experimental.pallas import tpu as pltpu
from jax.sharding import PartitionSpec as P

N = 384
T = 128
H = 112
G8 = 8
BF = jnp.bfloat16
F32 = jnp.float32
MESH = pl.DeviceIdType.MESH
DMA = pltpu.SemaphoreType.DMA


def mm(a, b):
    return jnp.dot(a, b, preferred_element_type=F32)


def mm_t(a, b):
    return lax.dot_general(a, b, (((1,), (1,)), ((), ())), preferred_element_type=F32)


def mix(coef, prods, target):
    sources = ((0,), (1, 2), (1, 2), (3,))[target]
    out = []
    for w in range(2):
        total = None
        for p in sources:
            for k in range(2):
                term = coef(w, k, p, target) * prods[w ^ k][p].astype(F32)
                total = term if total is None else total + term
        out.append(total.astype(BF))
    return out


def widen(tile):
    return jnp.concatenate([tile, jnp.zeros((T - H, T), BF)], axis=0)


def widen_wide(tile):
    return jnp.concatenate([tile, jnp.zeros((T - H, N), BF)], axis=0)


def pull_near(coef, pull, base, m1):
    prods = []
    for w in range(2):
        near = widen(m1[w])
        prods.append(
            (
                None,
                mm(pull[:, base : base + T], near).astype(BF),
                mm(pull[:, base + T : base + 2 * T], near).astype(BF),
            )
        )
    return [mix(coef, prods, 1), mix(coef, prods, 2)]


def pull_far(coef, pull, base, m3):
    prods = [
        (None, None, None, mm(pull[:, base + 2 * T : base + 3 * T], widen(m3[w])).astype(BF))
        for w in range(2)
    ]
    return mix(coef, prods, 3)


def near_terms(mixed, pull, base, w):
    return mm_t(mixed[0][w], pull[:, base : base + T]) + mm_t(
        mixed[1][w], pull[:, base + T : base + 2 * T]
    )


def far_term(mixed, pull, base, w):
    return mm_t(mixed[w], pull[:, base + 2 * T : base + 3 * T])


def settle(big, out, w, c0, m1, m3, near, far):
    kept = c0[w].astype(F32)
    total = kept + near + far
    small = kept[:H, :T] + m1[w].astype(F32) + m3[w].astype(F32)
    out[w] = jnp.where(big, total, jnp.zeros_like(total)).astype(BF)
    out[w, :H, :T] = jnp.where(big, total[:H, :T], small).astype(BF)


def remote(src, dst, sems, slot, target):
    return pltpu.make_async_remote_copy(
        src_ref=src,
        dst_ref=dst,
        send_sem=sems[0].at[slot],
        recv_sem=sems[1].at[slot],
        device_id=target,
        device_id_type=MESH,
    )


def greet(targets):
    barrier = pltpu.get_barrier_semaphore()
    for target in targets:
        pl.semaphore_signal(barrier, inc=1, device_id=target, device_id_type=MESH)
    return barrier


def write_rows(out, grads):
    for within in range(G8):
        chip = within // 2
        spot = (within % 2) * 4 + (chip % 2) * 2 + chip // 2
        out[spot] = grads[48 * within : 48 * within + 48].astype(BF)


def sweep_kernel(
    sizes, ops, mask, rows3, bound_hbm, left4, env4, grads3,
    bound, left, near_acc, acol, pull, xs, hn, hf, ab, right, c0, m1, m3, got0, got1, got3, at1, at3, near_l, far_l,
    mx0, mxh, mx_pull, left_t, near_t, far_t, parts, part_in, sums, sums_in, mids, mids_in, totals, home,
    send, recv, csend, crecv, gsend, grecv, own_sem,
):
    rows, left_hbm, env_out, grads_out = rows3.at[0], left4.at[0], env4.at[0], grads3.at[0]
    sect = lax.axis_index("sect")
    blk = lax.axis_index("blk")
    within = lax.rem(blk, G8)
    base = blk - within
    sector = blk // G8
    core = lax.rem(within, 2)
    chip = within // 2
    upper = lax.rem(sect + 1, 4)
    lower = lax.rem(sect + 3, 4)
    mate = (sect, base + chip * 2 + 1 - core)
    peers = [(sect, base + lax.rem(chip + d, 4) * 2 + core) for d in (1, 2, 3)]
    origin = within // 3
    back8, back16 = lax.rem(blk + 120, 128), lax.rem(blk + 112, 128)
    fore8, fore16 = lax.rem(blk + 8, 128), lax.rem(blk + 16, 128)
    barrier = greet(
        peers
        + [mate, (upper, blk), (lower, blk)]
        + [(sect, lax.rem(base + 128 - 8 * d + origin, 128)) for d in (1, 2)]
        + [(upper, fore8), (upper, fore16), (lower, back8), (lower, back16)]
        + [(sect, back8), (sect, back16), (sect, fore8), (sect, fore16)]
    )
    goals = [[(sect, lax.rem(base + 8 * d, 128) + 3 * within + j) for j in range(3)] for d in (1, 2)]
    sends_halo = [(3 * within + j) < G8 for j in range(3)]
    for j in range(3):

        @pl.when(sends_halo[j])
        def _(j=j):
            for d in range(2):
                pl.semaphore_signal(barrier, inc=1, device_id=goals[d][j], device_id_type=MESH)

    own = [pltpu.make_async_copy(rows.at[:, pl.ds(0, N)], xs.at[within], own_sem.at[0])]
    for p in range(1, 4):
        own.append(
            pltpu.make_async_copy(
                rows.at[:, pl.ds(N * p, T)], ab.at[within, :, pl.ds(T * (p - 1), T)], own_sem.at[p]
            )
        )
    for copy in own:
        copy.start()
    bound_in = pltpu.make_async_copy(bound_hbm, bound, own_sem.at[4])
    left_in = pltpu.make_async_copy(left_hbm, left, own_sem.at[5])
    bound_in.start()
    left_in.start()

    n_own = sizes[sector]
    n_near = jnp.where(sector >= 1, sizes[jnp.maximum(sector - 1, 0)], 0)
    n_far = jnp.where(sector >= 2, sizes[jnp.maximum(sector - 2, 0)], 0)
    big, near_big, far_big = n_own > H, n_near > H, n_far > H

    def coef(w, k, p, target):
        channel = 2 * within + w
        return ops[k, p, target, channel] * mask[k, channel].astype(F32)

    bound_in.wait()
    row = lax.broadcasted_iota(jnp.int32, (N, N), 0)
    col = lax.broadcasted_iota(jnp.int32, (N, N), 1)
    live = jnp.maximum(row, col) < n_own
    for w in range(2):
        right[w] = jnp.where(live, bound[w], jnp.zeros((N, N), BF))
    for copy in own:
        copy.wait()
    extra = jnp.where(within < 2, 6, jnp.where(within == 2, 4, 0))
    pl.semaphore_wait(barrier, 16 + extra)

    sems = (send, recv)

    def halo_copy(d, j):
        width = 2 * N if d == 0 else N
        at = N if d == 0 else 3 * N
        return pltpu.make_async_remote_copy(
            src_ref=rows.at[pl.ds(16 * j, 16), pl.ds(at, width)],
            dst_ref=(hn if d == 0 else hf).at[3 * within + j],
            send_sem=send.at[3 * d + j],
            recv_sem=recv.at[d],
            device_id=goals[d][j],
            device_id_type=MESH,
        )

    for j in range(3):

        @pl.when(sends_halo[j])
        def _(j=j):
            halo_copy(1, j).start()
            halo_copy(0, j).start()

    x_peer = [remote(xs.at[within], xs.at[within], sems, 7 + d, peers[d]) for d in range(3)]
    for copy in x_peer:
        copy.start()
    x_mate = [remote(xs.at[within], xs.at[within], sems, 10, mate)]
    x_mate[0].start()
    above = remote(
        ab.at[within, :, pl.ds(0, N)], ab.at[within, :, pl.ds(N, N)], sems, 6, (lower, blk)
    )
    above.start()
    csems = (csend, crecv)
    l_near = remote(left_hbm.at[:, pl.ds(0, H), :], near_l, csems, 6, (sect, fore8))
    l_far = remote(near_l, far_l, csems, 7, (sect, fore8))

    def landed(ref, slot):
        pltpu.make_async_remote_copy(
            src_ref=ref,
            dst_ref=ref,
            send_sem=send.at[slot],
            recv_sem=recv.at[slot],
            device_id=mate,
            device_id_type=MESH,
        ).wait_recv()

    landed(hf.at[within], 1)
    f_peer = [remote(hf.at[within], hf.at[within], sems, 28 + d, peers[d]) for d in range(3)]
    f_mate = [remote(hf.at[within], hf.at[within], sems, 31, mate)]
    for copy in f_peer + f_mate:
        copy.start()
    landed(hn.at[within], 0)
    h_peer = [remote(hn.at[within], hn.at[within], sems, 21 + d, peers[d]) for d in range(3)]
    h_mate = [remote(hn.at[within], hn.at[within], sems, 24, mate)]
    for copy in h_peer + h_mate:
        copy.start()
    landed(ab.at[within, :, pl.ds(N, N)], 6)
    a_peer = [remote(ab.at[within], ab.at[within], sems, 14 + d, peers[d]) for d in range(3)]
    a_mate = [remote(ab.at[within], ab.at[within], sems, 17, mate)]
    for copy in a_peer + a_mate:
        copy.start()

    def pass_on(buf, first, mine):
        for d in range(3):
            spot = lax.rem(chip + 3 - d, 4) * 2 + core
            landed(buf.at[spot], first + d)
            forward = remote(buf.at[spot], buf.at[spot], sems, first + 4 + d, mate)
            forward.start()
            mine.append(forward)

    down0 = [remote(c0.at[w], got0.at[w], csems, 2 + w, (lower, blk)) for w in range(2)]
    down1 = remote(m1, got1, csems, 0, (lower, back8))
    down3 = remote(m3, got3, csems, 1, (lower, back16))
    last1 = remote(m1, at1, csems, 4, (sect, back8))
    last3 = remote(m3, at3, csems, 5, (sect, back16))
    back0 = remote(right, env_out, csems, 8, (upper, blk))
    up1 = remote(got1, at1, csems, 9, (upper, blk))
    up3 = remote(got3, at3, csems, 10, (upper, blk))

    def own_terms():
        prods = [(mm(acol[:N, :], right[w]).astype(BF),) for w in range(2)]
        blend = mix(coef, prods, 0)
        for w in range(2):
            mx0[w] = blend[w]
            c0[w] = mm_t(blend[w], acol[:N, :]).astype(BF)

            @pl.when(sect > 0)
            def _(w=w):
                down0[w].start()

    def turn(tile, out):
        for w in range(2):
            out[:, T * w : T * w + T] = jnp.transpose(widen_wide(tile[w]))

    def turn_left():
        left_in.wait()
        for w in range(2):
            left_t[:, N * w : N * w + N] = jnp.transpose(left[w])

    def finish_above():
        pass_on(ab, 14, [])
        for d in range(3):
            remote(ab.at[within], ab.at[within], sems, 18 + d, mate).wait()
        a_mate[0].wait()
        for w in range(G8):
            line = lax.broadcasted_iota(jnp.int32, (48, 2 * N), 0) + 48 * w
            pull[48 * w : 48 * w + 48, :] = jnp.where(
                line < n_own, ab[w], jnp.zeros((48, 2 * N), BF)
            )

    pass_on(xs, 7, x_mate)
    for copy in x_mate:
        copy.wait()
    for w in range(G8):
        line = lax.broadcasted_iota(jnp.int32, (48, N), 0) + 48 * w
        acol[48 * w : 48 * w + 48, :] = jnp.where(line < n_own, xs[w], jnp.zeros((48, N), BF))

    @pl.when(sect == 3)
    def _():
        own_terms()

    pass_on(hf, 28, f_mate)
    for copy in f_mate:
        copy.wait()
    for w in range(G8):
        halo_line = lax.broadcasted_iota(jnp.int32, (16, N), 0) + 16 * w
        at = N + 2 * T + 16 * w
        acol[at : at + 16, :] = jnp.where(halo_line < n_far, hf[w], jnp.zeros((16, N), BF))

    def finish_near():
        pass_on(hn, 21, [])
        for d in range(3):
            remote(hn.at[within], hn.at[within], sems, 25 + d, mate).wait()
        h_mate[0].wait()
        for w in range(G8):
            halo_line = lax.broadcasted_iota(jnp.int32, (16, N), 0) + 16 * w
            for block in range(2):
                at = N + T * block + 16 * w
                acol[at : at + 16, :] = jnp.where(
                    halo_line < n_near, hn[w, :, N * block : N * block + N], jnp.zeros((16, N), BF)
                )

    @pl.when(sect < 2)
    def _():
        l_near.start()
        finish_near()
        finish_above()
        l_near.wait_recv()

        @pl.when(sect == 0)
        def _():
            l_far.start()

        turn(near_l, near_t)
        turn_left()

    @pl.when(sect == 0)
    def _():
        l_far.wait_recv()
        turn(far_l, far_t)

    @pl.when(sect == 2)
    def _():
        finish_near()
        finish_above()

    @pl.when(sect < 3)
    def _():
        down1.wait_recv()
        mixed = pull_near(coef, pull, N, got1)
        for w in range(2):
            near_acc[w] = near_terms(mixed, pull, N, w)
        down3.wait_recv()
        mixed = pull_far(coef, pull, N, got3)
        for w in range(2):
            down0[w].wait_recv()
            settle(big, right, w, got0, got1, got3, near_acc[w], far_term(mixed, pull, N, w))

    far_p = [
        (None, None, None, mm(acol[N + 2 * T : 2 * N, :], right[w]).astype(BF)) for w in range(2)
    ]
    blend = mix(coef, far_p, 3)
    for w in range(2):
        mxh[2, w] = blend[w]
        far = mm_t(blend[w], acol[N + 2 * T : 2 * N, :])
        m3[w] = jnp.where(far_big, right[w, :H, :T], far[:H].astype(BF))

    @pl.when(sect > 0)
    def _():
        down3.start()

    @pl.when(sect == 0)
    def _():
        last3.start()

    @pl.when((sect > 0) & (sect < 3))
    def _():
        own_terms()

    @pl.when(sect == 3)
    def _():
        finish_near()

    near_p = []
    for w in range(2):
        both = mm(acol[N : N + 2 * T, :], right[w]).astype(BF)
        near_p.append((None, both[:T], both[T:]))
    blend = [mix(coef, near_p, p) for p in (1, 2)]
    for w in range(2):
        mxh[0, w] = blend[0][w]
        mxh[1, w] = blend[1][w]
        near = mm_t(blend[0][w], acol[N : N + T, :]) + mm_t(blend[1][w], acol[N + T : N + 2 * T, :])
        m1[w] = jnp.where(near_big, right[w, :H, :T], near[:H].astype(BF))

    @pl.when(sect > 0)
    def _():
        down1.start()

    @pl.when(sect == 0)
    def _():
        last1.start()

    @pl.when(sect < 3)
    def _():
        up1.start()
        up3.start()
        back0.start()

    @pl.when(sect == 1)
    def _():
        l_far.start()

    @pl.when(sect >= 2)
    def _():
        l_near.start()

    @pl.when(sect == 3)
    def _():
        finish_above()


    gsems = (gsend, grecv)
    core_copy = [
        remote(parts.at[k, pl.ds((1 - core) * 4, 4)], part_in.at[k], gsems, k, mate) for k in range(5)
    ]
    odd, half = lax.rem(chip, 2), chip // 2
    side = (sect, base + (chip + 1 - 2 * odd) * 2 + core)
    across = (sect, base + lax.rem(chip + 2, 4) * 2 + core)
    side_copy = [
        remote(sums.at[k, pl.ds((1 - odd) * 2, 2)], sums_in.at[k], gsems, 5 + k, side)
        for k in range(5)
    ]
    across_copy = [
        remote(mids.at[k, 1 - half], mids_in.at[k], gsems, 10 + k, across) for k in range(5)
    ]
    home_copy = [
        remote(totals.at[k], home.at[k], gsems, 15 + k, (sect, back16 if k == 0 else back8))
        for k in range(3)
    ]

    def add_core(k):
        core_copy[k].wait_recv()
        mine = parts[k, pl.ds(core * 4, 4)]
        sums[k] = (mine.astype(F32) + part_in[k].astype(F32)).astype(BF)
        side_copy[k].start()

    def add_side(k):
        side_copy[k].wait_recv()
        mine = sums[k, pl.ds(odd * 2, 2)]
        mids[k] = (mine.astype(F32) + sums_in[k].astype(F32)).astype(BF)
        across_copy[k].start()

    def add_across(k):
        across_copy[k].wait_recv()
        totals[k] = (mids[k, half].astype(F32) + mids_in[k].astype(F32)).astype(BF)

    @pl.when(sect >= 2)
    def _():
        turn_left()
        l_near.wait_recv()
        l_far.start()
        turn(near_l, near_t)

    @pl.when(sect > 0)
    def _():
        l_far.wait_recv()
        turn(far_l, far_t)

    write_rows(parts.at[0], mm(far_t[...], mxh[2].reshape(2 * T, N)))
    core_copy[0].start()
    for p in (1, 2):
        write_rows(parts.at[p], mm(near_t[...], mxh[p - 1].reshape(2 * T, N)))
        core_copy[p].start()
        if p == 1:
            add_core(0)
    add_core(1)

    @pl.when(sect == 0)
    def _():
        own_terms()

    write_rows(parts.at[3], mm(left_t[...], mx0[...].reshape(2 * N, N)))
    core_copy[3].start()
    add_side(0)
    add_core(2)
    add_side(1)
    add_across(0)
    home_copy[0].start()
    add_core(3)
    add_side(2)
    add_across(1)
    home_copy[1].start()
    add_across(2)
    home_copy[2].start()

    @pl.when(sect == 0)
    def _():
        last1.wait_recv()
        last3.wait_recv()

    @pl.when(sect > 0)
    def _():
        up1.wait_recv()
        up3.wait_recv()

    mixed = pull_near(coef, pull, 0, at1)
    mixed.append(pull_far(coef, pull, 0, at3))
    narrow = [mm(left_t[...], jnp.concatenate(mixed[p], axis=0)) for p in range(3)]
    write_rows(parts.at[4], jnp.concatenate(narrow, axis=1))
    core_copy[4].start()
    add_side(3)
    for p in range(3):
        for w in range(2):
            mx_pull[w, p] = mixed[p][w]
    add_core(4)
    add_across(3)

    @pl.when(sect == 0)
    def _():
        for w in range(2):
            near = mm_t(mx_pull[w, 0], pull[:, :T]) + mm_t(mx_pull[w, 1], pull[:, T : 2 * T])
            far = mm_t(mx_pull[w, 2], pull[:, 2 * T : 3 * T])
            settle(big, env_out, w, c0, at1, at3, near, far)

    add_side(4)
    add_across(4)
    grads_out[:, :N] = totals[3]
    zero = jnp.zeros((48, N - T), BF)
    for p in range(1, 4):
        k = p % 3
        home_copy[k].wait_recv()
        thin = jnp.concatenate([totals[4, :, T * (p - 1) : T * p], zero], axis=1)
        grads_out[:, N * p : N * p + N] = jnp.where(big, thin, home[k])

    for copy in x_peer + f_peer + h_peer + a_peer + [above, l_near, l_far] + core_copy + home_copy:
        copy.wait_send()
    for copy in side_copy + across_copy:
        copy.wait_send()
    for j in range(3):

        @pl.when(sends_halo[j])
        def _(j=j):
            halo_copy(0, j).wait_send()
            halo_copy(1, j).wait_send()

    @pl.when(sect == 0)
    def _():
        last1.wait_send()
        last3.wait_send()

    @pl.when(sect > 0)
    def _():
        down1.wait_send()
        down3.wait_send()
        down0[0].wait_send()
        down0[1].wait_send()
        back0.wait_recv()

    @pl.when(sect < 3)
    def _():
        back0.wait_send()
        up1.wait_send()
        up3.wait_send()


SMEM = pl.BlockSpec(memory_space=pltpu.SMEM)
VMEM = pl.BlockSpec(memory_space=pltpu.VMEM)
HBM = pl.BlockSpec(memory_space=pltpu.HBM)


def local(site_tensor, left_env, boundary_env, sector_sizes, mpo_ops, mpo_mask):
    def buf(*shape):
        return pltpu.VMEM(shape, BF)

    return pl.pallas_call(
        sweep_kernel,
        out_shape=(
            jax.ShapeDtypeStruct((1, 2, N, N), BF),
            jax.ShapeDtypeStruct((1, 48, 4 * N), BF),
        ),
        in_specs=[SMEM] * 3 + [HBM] * 3,
        out_specs=(VMEM, VMEM),
        scratch_shapes=[
            buf(2, N, N),
            buf(2, N, N),
            pltpu.VMEM((2, N, N), F32),
            buf(2 * N, N),
            buf(N, 2 * N),
            buf(G8, 48, N),
            buf(G8, 16, 2 * N),
            buf(G8, 16, N),
            buf(G8, 48, 2 * N),
            buf(2, N, N),
            buf(2, N, N),
            buf(2, H, T),
            buf(2, H, T),
            buf(2, N, N),
            buf(2, H, T),
            buf(2, H, T),
            buf(2, H, T),
            buf(2, H, T),
            buf(2, H, N),
            buf(2, H, N),
            buf(2, N, N),
            buf(3, 2, T, N),
            buf(2, 3, N, T),
            buf(N, 2 * N),
            buf(N, 2 * T),
            buf(N, 2 * T),
            buf(5, G8, 48, N),
            buf(5, 4, 48, N),
            buf(5, 4, 48, N),
            buf(5, 2, 48, N),
            buf(5, 2, 48, N),
            buf(5, 48, N),
            buf(5, 48, N),
            buf(3, 48, N),
            DMA((35,)),
            DMA((35,)),
            DMA((11,)),
            DMA((11,)),
            DMA((18,)),
            DMA((18,)),
            DMA((6,)),
        ],
        compiler_params=pltpu.CompilerParams(
            collective_id=0, has_side_effects=True, vmem_limit_bytes=50_000_000
        ),
        name="sweep",
    )(
        sector_sizes,
        jnp.transpose(mpo_ops, (1, 2, 3, 0)),
        jnp.transpose(mpo_mask, (1, 0)),
        *[pltpu.with_memory_space_constraint(a, pltpu.HBM) for a in (site_tensor, boundary_env, left_env)],
    )


def solution(mesh):
    return jax.shard_map(
        local,
        mesh=mesh,
        in_specs=(
            P("sect", "blk", None),
            P("sect", "blk", None, None),
            P("blk", None, None),
            P(),
            P(),
            P(),
        ),
        out_specs=(P("sect", "blk", None, None), P("sect", "blk", None)),
        check_vma=False,
    )
```

```python
import jax
import jax.numpy as jnp
from jax import lax
from jax.experimental import pallas as pl
from jax.experimental.pallas import tpu as pltpu
from jax.sharding import PartitionSpec as P

N = 384
T = 128
H = 112
G8 = 8
BF = jnp.bfloat16
F32 = jnp.float32
MESH = pl.DeviceIdType.MESH
DMA = pltpu.SemaphoreType.DMA


def mm(a, b):
    return jnp.dot(a, b, preferred_element_type=F32)


def mm_t(a, b):
    return lax.dot_general(a, b, (((1,), (1,)), ((), ())), preferred_element_type=F32)


def mix(coef, prods, target):
    sources = ((0,), (1, 2), (1, 2), (3,))[target]
    out = []
    for w in range(2):
        total = None
        for p in sources:
            for k in range(2):
                term = coef(w, k, p, target) * prods[w ^ k][p].astype(F32)
                total = term if total is None else total + term
        out.append(total.astype(BF))
    return out


def widen(tile):
    return jnp.concatenate([tile, jnp.zeros((T - H, T), BF)], axis=0)


def widen_wide(tile):
    return jnp.concatenate([tile, jnp.zeros((T - H, N), BF)], axis=0)


def pull_near(coef, pull, base, m1):
    prods = []
    for w in range(2):
        near = widen(m1[w])
        prods.append(
            (
                None,
                mm(pull[:, base : base + T], near).astype(BF),
                mm(pull[:, base + T : base + 2 * T], near).astype(BF),
            )
        )
    return [mix(coef, prods, 1), mix(coef, prods, 2)]


def pull_far(coef, pull, base, m3):
    prods = [
        (None, None, None, mm(pull[:, base + 2 * T : base + 3 * T], widen(m3[w])).astype(BF))
        for w in range(2)
    ]
    return mix(coef, prods, 3)


def near_terms(mixed, pull, base, w):
    return mm_t(mixed[0][w], pull[:, base : base + T]) + mm_t(
        mixed[1][w], pull[:, base + T : base + 2 * T]
    )


def far_term(mixed, pull, base, w):
    return mm_t(mixed[w], pull[:, base + 2 * T : base + 3 * T])


def settle(big, out, w, c0, m1, m3, near, far):
    kept = c0[w].astype(F32)
    total = kept + near + far
    small = kept[:H, :T] + m1[w].astype(F32) + m3[w].astype(F32)
    out[w] = jnp.where(big, total, jnp.zeros_like(total)).astype(BF)
    out[w, :H, :T] = jnp.where(big, total[:H, :T], small).astype(BF)


def remote(src, dst, sems, slot, target):
    return pltpu.make_async_remote_copy(
        src_ref=src,
        dst_ref=dst,
        send_sem=sems[0].at[slot],
        recv_sem=sems[1].at[slot],
        device_id=target,
        device_id_type=MESH,
    )


def greet(targets):
    barrier = pltpu.get_barrier_semaphore()
    for target in targets:
        pl.semaphore_signal(barrier, inc=1, device_id=target, device_id_type=MESH)
    return barrier


def write_rows(out, grads):
    for within in range(G8):
        chip = within // 2
        spot = (within % 2) * 4 + (chip % 2) * 2 + chip // 2
        out[spot] = grads[48 * within : 48 * within + 48].astype(BF)


def sweep_kernel(
    sizes_hbm, ops_hbm, mask_hbm, rows3, bound_hbm, left4, env4, grads3,
    sizes, ops, mask, bound, left, near_acc, acol, pull, xs, hn, hf, ab, right, c0, m1, m3, got0, got1, got3, at1, at3, near_l, far_l,
    mx0, mxh, mx_pull, left_t, near_t, far_t, parts, part_in, sums, sums_in, mids, mids_in, totals, home,
    send, recv, csend, crecv, gsend, grecv, own_sem,
):
    rows, left_hbm, env_out, grads_out = rows3.at[0], left4.at[0], env4.at[0], grads3.at[0]
    sect = lax.axis_index("sect")
    blk = lax.axis_index("blk")
    within = lax.rem(blk, G8)
    base = blk - within
    sector = blk // G8
    core = lax.rem(within, 2)
    chip = within // 2
    upper = lax.rem(sect + 1, 4)
    lower = lax.rem(sect + 3, 4)
    mate = (sect, base + chip * 2 + 1 - core)
    peers = [(sect, base + lax.rem(chip + d, 4) * 2 + core) for d in (1, 2, 3)]
    origin = within // 3
    back8, back16 = lax.rem(blk + 120, 128), lax.rem(blk + 112, 128)
    fore8, fore16 = lax.rem(blk + 8, 128), lax.rem(blk + 16, 128)
    barrier = greet(
        peers
        + [mate, (upper, blk), (lower, blk)]
        + [(sect, lax.rem(base + 128 - 8 * d + origin, 128)) for d in (1, 2)]
        + [(upper, fore8), (upper, fore16), (lower, back8), (lower, back16)]
        + [(sect, back8), (sect, back16), (sect, fore8), (sect, fore16)]
    )
    goals = [[(sect, lax.rem(base + 8 * d, 128) + 3 * within + j) for j in range(3)] for d in (1, 2)]
    sends_halo = [(3 * within + j) < G8 for j in range(3)]
    for j in range(3):

        @pl.when(sends_halo[j])
        def _(j=j):
            for d in range(2):
                pl.semaphore_signal(barrier, inc=1, device_id=goals[d][j], device_id_type=MESH)

    own = [pltpu.make_async_copy(rows.at[:, pl.ds(0, N)], xs.at[within], own_sem.at[0])]
    for p in range(1, 4):
        own.append(
            pltpu.make_async_copy(
                rows.at[:, pl.ds(N * p, T)], ab.at[within, :, pl.ds(T * (p - 1), T)], own_sem.at[p]
            )
        )
    for copy in own:
        copy.start()
    bound_in = pltpu.make_async_copy(bound_hbm, bound, own_sem.at[4])
    left_in = pltpu.make_async_copy(left_hbm, left, own_sem.at[5])
    small_in = [
        pltpu.make_async_copy(src, dst, own_sem.at[6 + i])
        for i, (src, dst) in enumerate(((sizes_hbm, sizes), (ops_hbm, ops), (mask_hbm, mask)))
    ]
    for copy in small_in:
        copy.start()
    bound_in.start()
    left_in.start()

    for copy in small_in:
        copy.wait()
    n_own = sizes[sector]
    n_near = jnp.where(sector >= 1, sizes[jnp.maximum(sector - 1, 0)], 0)
    n_far = jnp.where(sector >= 2, sizes[jnp.maximum(sector - 2, 0)], 0)
    big, near_big, far_big = n_own > H, n_near > H, n_far > H

    def coef(w, k, p, target):
        channel = 2 * within + w
        return ops[k, p, target, channel] * mask[k, channel].astype(F32)

    bound_in.wait()
    row = lax.broadcasted_iota(jnp.int32, (N, N), 0)
    col = lax.broadcasted_iota(jnp.int32, (N, N), 1)
    live = jnp.maximum(row, col) < n_own
    for w in range(2):
        right[w] = jnp.where(live, bound[w], jnp.zeros((N, N), BF))
    for copy in own:
        copy.wait()
    extra = jnp.where(within < 2, 6, jnp.where(within == 2, 4, 0))
    pl.semaphore_wait(barrier, 16 + extra)

    sems = (send, recv)

    def halo_copy(d, j):
        width = 2 * N if d == 0 else N
        at = N if d == 0 else 3 * N
        return pltpu.make_async_remote_copy(
            src_ref=rows.at[pl.ds(16 * j, 16), pl.ds(at, width)],
            dst_ref=(hn if d == 0 else hf).at[3 * within + j],
            send_sem=send.at[3 * d + j],
            recv_sem=recv.at[d],
            device_id=goals[d][j],
            device_id_type=MESH,
        )

    for j in range(3):

        @pl.when(sends_halo[j])
        def _(j=j):
            halo_copy(1, j).start()
            halo_copy(0, j).start()

    x_peer = [remote(xs.at[within], xs.at[within], sems, 7 + d, peers[d]) for d in range(3)]
    for copy in x_peer:
        copy.start()
    x_mate = [remote(xs.at[within], xs.at[within], sems, 10, mate)]
    x_mate[0].start()
    above = remote(
        ab.at[within, :, pl.ds(0, N)], ab.at[within, :, pl.ds(N, N)], sems, 6, (lower, blk)
    )
    above.start()
    csems = (csend, crecv)
    l_near = remote(left_hbm.at[:, pl.ds(0, H), :], near_l, csems, 6, (sect, fore8))
    l_far = remote(near_l, far_l, csems, 7, (sect, fore8))

    def landed(ref, slot):
        pltpu.make_async_remote_copy(
            src_ref=ref,
            dst_ref=ref,
            send_sem=send.at[slot],
            recv_sem=recv.at[slot],
            device_id=mate,
            device_id_type=MESH,
        ).wait_recv()

    landed(hf.at[within], 1)
    f_peer = [remote(hf.at[within], hf.at[within], sems, 28 + d, peers[d]) for d in range(3)]
    f_mate = [remote(hf.at[within], hf.at[within], sems, 31, mate)]
    for copy in f_peer + f_mate:
        copy.start()
    landed(hn.at[within], 0)
    h_peer = [remote(hn.at[within], hn.at[within], sems, 21 + d, peers[d]) for d in range(3)]
    h_mate = [remote(hn.at[within], hn.at[within], sems, 24, mate)]
    for copy in h_peer + h_mate:
        copy.start()
    landed(ab.at[within, :, pl.ds(N, N)], 6)
    a_peer = [remote(ab.at[within], ab.at[within], sems, 14 + d, peers[d]) for d in range(3)]
    a_mate = [remote(ab.at[within], ab.at[within], sems, 17, mate)]
    for copy in a_peer + a_mate:
        copy.start()

    def pass_on(buf, first, mine):
        for d in range(3):
            spot = lax.rem(chip + 3 - d, 4) * 2 + core
            landed(buf.at[spot], first + d)
            forward = remote(buf.at[spot], buf.at[spot], sems, first + 4 + d, mate)
            forward.start()
            mine.append(forward)

    down0 = [remote(c0.at[w], got0.at[w], csems, 2 + w, (lower, blk)) for w in range(2)]
    down1 = remote(m1, got1, csems, 0, (lower, back8))
    down3 = remote(m3, got3, csems, 1, (lower, back16))
    last1 = remote(m1, at1, csems, 4, (sect, back8))
    last3 = remote(m3, at3, csems, 5, (sect, back16))
    back0 = remote(right, env_out, csems, 8, (upper, blk))
    up1 = remote(got1, at1, csems, 9, (upper, blk))
    up3 = remote(got3, at3, csems, 10, (upper, blk))

    def own_terms():
        prods = [(mm(acol[:N, :], right[w]).astype(BF),) for w in range(2)]
        blend = mix(coef, prods, 0)
        for w in range(2):
            mx0[w] = blend[w]
            c0[w] = mm_t(blend[w], acol[:N, :]).astype(BF)

            @pl.when(sect > 0)
            def _(w=w):
                down0[w].start()

    def turn(tile, out):
        for w in range(2):
            out[:, T * w : T * w + T] = jnp.transpose(widen_wide(tile[w]))

    def turn_left():
        left_in.wait()
        for w in range(2):
            left_t[:, N * w : N * w + N] = jnp.transpose(left[w])

    def finish_above():
        pass_on(ab, 14, [])
        for d in range(3):
            remote(ab.at[within], ab.at[within], sems, 18 + d, mate).wait()
        a_mate[0].wait()
        for w in range(G8):
            line = lax.broadcasted_iota(jnp.int32, (48, 2 * N), 0) + 48 * w
            pull[48 * w : 48 * w + 48, :] = jnp.where(
                line < n_own, ab[w], jnp.zeros((48, 2 * N), BF)
            )

    pass_on(xs, 7, x_mate)
    for copy in x_mate:
        copy.wait()
    for w in range(G8):
        line = lax.broadcasted_iota(jnp.int32, (48, N), 0) + 48 * w
        acol[48 * w : 48 * w + 48, :] = jnp.where(line < n_own, xs[w], jnp.zeros((48, N), BF))

    @pl.when(sect == 3)
    def _():
        own_terms()

    pass_on(hf, 28, f_mate)
    for copy in f_mate:
        copy.wait()
    for w in range(G8):
        halo_line = lax.broadcasted_iota(jnp.int32, (16, N), 0) + 16 * w
        at = N + 2 * T + 16 * w
        acol[at : at + 16, :] = jnp.where(halo_line < n_far, hf[w], jnp.zeros((16, N), BF))

    def finish_near():
        pass_on(hn, 21, [])
        for d in range(3):
            remote(hn.at[within], hn.at[within], sems, 25 + d, mate).wait()
        h_mate[0].wait()
        for w in range(G8):
            halo_line = lax.broadcasted_iota(jnp.int32, (16, N), 0) + 16 * w
            for block in range(2):
                at = N + T * block + 16 * w
                acol[at : at + 16, :] = jnp.where(
                    halo_line < n_near, hn[w, :, N * block : N * block + N], jnp.zeros((16, N), BF)
                )

    @pl.when(sect < 2)
    def _():
        l_near.start()
        finish_near()
        finish_above()
        l_near.wait_recv()
        l_far.start()
        turn(near_l, near_t)
        turn_left()

    @pl.when(sect == 0)
    def _():
        l_far.wait_recv()
        turn(far_l, far_t)

    @pl.when(sect == 2)
    def _():
        finish_near()
        finish_above()

    @pl.when(sect < 3)
    def _():
        down1.wait_recv()
        mixed = pull_near(coef, pull, N, got1)
        for w in range(2):
            near_acc[w] = near_terms(mixed, pull, N, w)
        down3.wait_recv()
        mixed = pull_far(coef, pull, N, got3)
        for w in range(2):
            down0[w].wait_recv()
            settle(big, right, w, got0, got1, got3, near_acc[w], far_term(mixed, pull, N, w))

    @pl.when((sect > 0) & (sect < 3))
    def _():
        own_terms()

    far_p = [
        (None, None, None, mm(acol[N + 2 * T : 2 * N, :], right[w]).astype(BF)) for w in range(2)
    ]
    blend = mix(coef, far_p, 3)
    for w in range(2):
        mxh[2, w] = blend[w]
        far = mm_t(blend[w], acol[N + 2 * T : 2 * N, :])
        m3[w] = jnp.where(far_big, right[w, :H, :T], far[:H].astype(BF))

    @pl.when(sect > 0)
    def _():
        down3.start()

    @pl.when(sect == 0)
    def _():
        last3.start()

    @pl.when(sect == 3)
    def _():
        finish_near()

    near_p = []
    for w in range(2):
        both = mm(acol[N : N + 2 * T, :], right[w]).astype(BF)
        near_p.append((None, both[:T], both[T:]))
    blend = [mix(coef, near_p, p) for p in (1, 2)]
    for w in range(2):
        mxh[0, w] = blend[0][w]
        mxh[1, w] = blend[1][w]
        near = mm_t(blend[0][w], acol[N : N + T, :]) + mm_t(blend[1][w], acol[N + T : N + 2 * T, :])
        m1[w] = jnp.where(near_big, right[w, :H, :T], near[:H].astype(BF))

    @pl.when(sect > 0)
    def _():
        down1.start()

    @pl.when(sect == 0)
    def _():
        last1.start()

    @pl.when(sect < 3)
    def _():
        up1.start()
        up3.start()
        back0.start()

    @pl.when(sect >= 2)
    def _():
        l_near.start()

    @pl.when(sect == 3)
    def _():
        finish_above()


    gsems = (gsend, grecv)
    core_copy = [
        remote(parts.at[k, pl.ds((1 - core) * 4, 4)], part_in.at[k], gsems, k, mate) for k in range(5)
    ]
    odd, half = lax.rem(chip, 2), chip // 2
    side = (sect, base + (chip + 1 - 2 * odd) * 2 + core)
    across = (sect, base + lax.rem(chip + 2, 4) * 2 + core)
    side_copy = [
        remote(sums.at[k, pl.ds((1 - odd) * 2, 2)], sums_in.at[k], gsems, 5 + k, side)
        for k in range(5)
    ]
    across_copy = [
        remote(mids.at[k, 1 - half], mids_in.at[k], gsems, 10 + k, across) for k in range(5)
    ]
    home_copy = [
        remote(totals.at[k], home.at[k], gsems, 15 + k, (sect, back16 if k == 0 else back8))
        for k in range(3)
    ]

    def add_core(k):
        core_copy[k].wait_recv()
        mine = parts[k, pl.ds(core * 4, 4)]
        sums[k] = (mine.astype(F32) + part_in[k].astype(F32)).astype(BF)
        side_copy[k].start()

    def add_side(k):
        side_copy[k].wait_recv()
        mine = sums[k, pl.ds(odd * 2, 2)]
        mids[k] = (mine.astype(F32) + sums_in[k].astype(F32)).astype(BF)
        across_copy[k].start()

    def add_across(k):
        across_copy[k].wait_recv()
        totals[k] = (mids[k, half].astype(F32) + mids_in[k].astype(F32)).astype(BF)

    @pl.when(sect >= 2)
    def _():
        turn_left()
        l_near.wait_recv()
        l_far.start()
        turn(near_l, near_t)

    @pl.when(sect > 0)
    def _():
        l_far.wait_recv()
        turn(far_l, far_t)

    write_rows(parts.at[0], mm(far_t[...], mxh[2].reshape(2 * T, N)))
    core_copy[0].start()
    for p in (1, 2):
        write_rows(parts.at[p], mm(near_t[...], mxh[p - 1].reshape(2 * T, N)))
        core_copy[p].start()
        if p == 1:
            add_core(0)
    add_core(1)

    @pl.when(sect == 0)
    def _():
        own_terms()

    write_rows(parts.at[3], mm(left_t[...], mx0[...].reshape(2 * N, N)))
    core_copy[3].start()
    add_side(0)
    add_core(2)
    add_side(1)
    add_across(0)
    home_copy[0].start()
    add_core(3)
    add_side(2)
    add_across(1)
    home_copy[1].start()
    add_across(2)
    home_copy[2].start()

    @pl.when(sect == 0)
    def _():
        last1.wait_recv()
        last3.wait_recv()

    @pl.when(sect > 0)
    def _():
        up1.wait_recv()
        up3.wait_recv()

    mixed = pull_near(coef, pull, 0, at1)
    mixed.append(pull_far(coef, pull, 0, at3))
    narrow = [mm(left_t[...], jnp.concatenate(mixed[p], axis=0)) for p in range(3)]
    write_rows(parts.at[4], jnp.concatenate(narrow, axis=1))
    core_copy[4].start()
    add_side(3)
    for p in range(3):
        for w in range(2):
            mx_pull[w, p] = mixed[p][w]
    add_core(4)
    add_across(3)

    @pl.when(sect == 0)
    def _():
        for w in range(2):
            near = mm_t(mx_pull[w, 0], pull[:, :T]) + mm_t(mx_pull[w, 1], pull[:, T : 2 * T])
            far = mm_t(mx_pull[w, 2], pull[:, 2 * T : 3 * T])
            settle(big, env_out, w, c0, at1, at3, near, far)

    add_side(4)
    add_across(4)
    grads_out[:, :N] = totals[3]
    zero = jnp.zeros((48, N - T), BF)
    for p in range(1, 4):
        k = p % 3
        home_copy[k].wait_recv()
        thin = jnp.concatenate([totals[4, :, T * (p - 1) : T * p], zero], axis=1)
        grads_out[:, N * p : N * p + N] = jnp.where(big, thin, home[k])

    for copy in x_peer + f_peer + h_peer + a_peer + [above, l_near, l_far] + core_copy + home_copy:
        copy.wait_send()
    for copy in side_copy + across_copy:
        copy.wait_send()
    for j in range(3):

        @pl.when(sends_halo[j])
        def _(j=j):
            halo_copy(0, j).wait_send()
            halo_copy(1, j).wait_send()

    @pl.when(sect == 0)
    def _():
        last1.wait_send()
        last3.wait_send()

    @pl.when(sect > 0)
    def _():
        down1.wait_send()
        down3.wait_send()
        down0[0].wait_send()
        down0[1].wait_send()
        back0.wait_recv()

    @pl.when(sect < 3)
    def _():
        back0.wait_send()
        up1.wait_send()
        up3.wait_send()


VMEM = pl.BlockSpec(memory_space=pltpu.VMEM)
HBM = pl.BlockSpec(memory_space=pltpu.HBM)


def local(site_tensor, left_env, boundary_env, sector_sizes, mpo_ops, mpo_mask):
    def buf(*shape):
        return pltpu.VMEM(shape, BF)

    return pl.pallas_call(
        sweep_kernel,
        out_shape=(
            jax.ShapeDtypeStruct((1, 2, N, N), BF),
            jax.ShapeDtypeStruct((1, 48, 4 * N), BF),
        ),
        in_specs=[HBM] * 6,
        out_specs=(VMEM, VMEM),
        scratch_shapes=[
            pltpu.SMEM((16,), jnp.int32),
            pltpu.SMEM((2, 4, 4, 16), F32),
            pltpu.SMEM((2, 16), jnp.int32),
            buf(2, N, N),
            buf(2, N, N),
            pltpu.VMEM((2, N, N), F32),
            buf(2 * N, N),
            buf(N, 2 * N),
            buf(G8, 48, N),
            buf(G8, 16, 2 * N),
            buf(G8, 16, N),
            buf(G8, 48, 2 * N),
            buf(2, N, N),
            buf(2, N, N),
            buf(2, H, T),
            buf(2, H, T),
            buf(2, N, N),
            buf(2, H, T),
            buf(2, H, T),
            buf(2, H, T),
            buf(2, H, T),
            buf(2, H, N),
            buf(2, H, N),
            buf(2, N, N),
            buf(3, 2, T, N),
            buf(2, 3, N, T),
            buf(N, 2 * N),
            buf(N, 2 * T),
            buf(N, 2 * T),
            buf(5, G8, 48, N),
            buf(5, 4, 48, N),
            buf(5, 4, 48, N),
            buf(5, 2, 48, N),
            buf(5, 2, 48, N),
            buf(5, 48, N),
            buf(5, 48, N),
            buf(3, 48, N),
            DMA((35,)),
            DMA((35,)),
            DMA((11,)),
            DMA((11,)),
            DMA((18,)),
            DMA((18,)),
            DMA((9,)),
        ],
        compiler_params=pltpu.CompilerParams(
            collective_id=0, has_side_effects=True, vmem_limit_bytes=50_000_000
        ),
        name="sweep",
    )(
        *[
            pltpu.with_memory_space_constraint(a, pltpu.HBM)
            for a in (
                sector_sizes,
                jnp.transpose(mpo_ops, (1, 2, 3, 0)),
                jnp.transpose(mpo_mask, (1, 0)),
                site_tensor,
                boundary_env,
                left_env,
            )
        ]
    )


def solution(mesh):
    return jax.shard_map(
        local,
        mesh=mesh,
        in_specs=(
            P("sect", "blk", None),
            P("sect", "blk", None, None),
            P("blk", None, None),
            P(),
            P(),
            P(),
        ),
        out_specs=(P("sect", "blk", None, None), P("sect", "blk", None)),
        check_vma=False,
    )
```

```python
import jax
import jax.numpy as jnp
from jax import lax
from jax.experimental import pallas as pl
from jax.experimental.pallas import tpu as pltpu
from jax.sharding import PartitionSpec as P

N = 384
T = 128
H = 112
G8 = 8
BF = jnp.bfloat16
F32 = jnp.float32
MESH = pl.DeviceIdType.MESH
DMA = pltpu.SemaphoreType.DMA


def mm(a, b):
    return jnp.dot(a, b, preferred_element_type=F32)


def mm_t(a, b):
    return lax.dot_general(a, b, (((1,), (1,)), ((), ())), preferred_element_type=F32)


def mix(coef, prods, target):
    sources = ((0,), (1, 2), (1, 2), (3,))[target]
    out = []
    for w in range(2):
        total = None
        for p in sources:
            for k in range(2):
                term = coef(w, k, p, target) * prods[w ^ k][p].astype(F32)
                total = term if total is None else total + term
        out.append(total.astype(BF))
    return out


def widen(tile):
    return jnp.concatenate([tile, jnp.zeros((T - H, T), BF)], axis=0)


def widen_wide(tile):
    return jnp.concatenate([tile, jnp.zeros((T - H, N), BF)], axis=0)


def pull_near(coef, pull, base, m1):
    prods = []
    for w in range(2):
        near = widen(m1[w])
        prods.append(
            (
                None,
                mm(pull[:, base : base + T], near).astype(BF),
                mm(pull[:, base + T : base + 2 * T], near).astype(BF),
            )
        )
    return [mix(coef, prods, 1), mix(coef, prods, 2)]


def pull_far(coef, pull, base, m3):
    prods = [
        (None, None, None, mm(pull[:, base + 2 * T : base + 3 * T], widen(m3[w])).astype(BF))
        for w in range(2)
    ]
    return mix(coef, prods, 3)


def near_terms(mixed, pull, base, w):
    return mm_t(mixed[0][w], pull[:, base : base + T]) + mm_t(
        mixed[1][w], pull[:, base + T : base + 2 * T]
    )


def far_term(mixed, pull, base, w):
    return mm_t(mixed[w], pull[:, base + 2 * T : base + 3 * T])


def settle(big, out, w, c0, m1, m3, near, far):
    kept = c0[w].astype(F32)
    total = kept + near + far
    small = kept[:H, :T] + m1[w].astype(F32) + m3[w].astype(F32)
    out[w] = jnp.where(big, total, jnp.zeros_like(total)).astype(BF)
    out[w, :H, :T] = jnp.where(big, total[:H, :T], small).astype(BF)


def remote(src, dst, sems, slot, target):
    return pltpu.make_async_remote_copy(
        src_ref=src,
        dst_ref=dst,
        send_sem=sems[0].at[slot],
        recv_sem=sems[1].at[slot],
        device_id=target,
        device_id_type=MESH,
    )


def greet(targets):
    barrier = pltpu.get_barrier_semaphore()
    for target in targets:
        pl.semaphore_signal(barrier, inc=1, device_id=target, device_id_type=MESH)
    return barrier


def write_rows(out, grads):
    for within in range(G8):
        chip = within // 2
        spot = (within % 2) * 4 + (chip % 2) * 2 + chip // 2
        out[spot] = grads[48 * within : 48 * within + 48].astype(BF)


def sweep_kernel(
    sizes_hbm, ops_hbm, mask_hbm, rows3, bound_hbm, left4, env4, grads3,
    sizes, ops, mask, bound, left, near_acc, acol, pull, xs, hn, hf, ab, right, c0, m1, m3, got0, got1, got3, at1, at3, near_l, far_l,
    mx0, mxh, mx_pull, left_t, near_t, far_t, parts, part_in, sums, sums_in, mids, mids_in, totals, home,
    send, recv, csend, crecv, gsend, grecv, own_sem,
):
    rows, left_hbm, env_out, grads_out = rows3.at[0], left4.at[0], env4.at[0], grads3.at[0]
    sect = lax.axis_index("sect")
    blk = lax.axis_index("blk")
    within = lax.rem(blk, G8)
    base = blk - within
    sector = blk // G8
    core = lax.rem(within, 2)
    chip = within // 2
    upper = lax.rem(sect + 1, 4)
    lower = lax.rem(sect + 3, 4)
    mate = (sect, base + chip * 2 + 1 - core)
    peers = [(sect, base + lax.rem(chip + d, 4) * 2 + core) for d in (1, 2, 3)]
    origin = within // 3
    back8, back16 = lax.rem(blk + 120, 128), lax.rem(blk + 112, 128)
    fore8, fore16 = lax.rem(blk + 8, 128), lax.rem(blk + 16, 128)
    barrier = greet(
        peers
        + [mate, (upper, blk), (lower, blk)]
        + [(sect, lax.rem(base + 128 - 8 * d + origin, 128)) for d in (1, 2)]
        + [(upper, fore8), (upper, fore16), (lower, back8), (lower, back16)]
        + [(sect, back8), (sect, back16), (sect, fore8), (sect, fore16)]
    )
    goals = [[(sect, lax.rem(base + 8 * d, 128) + 3 * within + j) for j in range(3)] for d in (1, 2)]
    sends_halo = [(3 * within + j) < G8 for j in range(3)]
    for j in range(3):

        @pl.when(sends_halo[j])
        def _(j=j):
            for d in range(2):
                pl.semaphore_signal(barrier, inc=1, device_id=goals[d][j], device_id_type=MESH)

    own = [pltpu.make_async_copy(rows.at[:, pl.ds(0, N)], xs.at[within], own_sem.at[0])]
    for p in range(1, 4):
        own.append(
            pltpu.make_async_copy(
                rows.at[:, pl.ds(N * p, T)], ab.at[within, :, pl.ds(T * (p - 1), T)], own_sem.at[p]
            )
        )
    for copy in own:
        copy.start()
    bound_in = pltpu.make_async_copy(bound_hbm, bound, own_sem.at[4])
    left_in = pltpu.make_async_copy(left_hbm, left, own_sem.at[5])
    small_in = [
        pltpu.make_async_copy(src, dst, own_sem.at[6 + i])
        for i, (src, dst) in enumerate(((sizes_hbm, sizes), (ops_hbm, ops), (mask_hbm, mask)))
    ]
    for copy in small_in:
        copy.start()
    bound_in.start()
    left_in.start()

    for copy in small_in:
        copy.wait()
    n_own = sizes[sector]
    n_near = jnp.where(sector >= 1, sizes[jnp.maximum(sector - 1, 0)], 0)
    n_far = jnp.where(sector >= 2, sizes[jnp.maximum(sector - 2, 0)], 0)
    big, near_big, far_big = n_own > H, n_near > H, n_far > H

    def coef(w, k, p, target):
        channel = 2 * within + w
        return ops[k, p, target, channel] * mask[k, channel].astype(F32)

    bound_in.wait()
    row = lax.broadcasted_iota(jnp.int32, (N, N), 0)
    col = lax.broadcasted_iota(jnp.int32, (N, N), 1)
    live = jnp.maximum(row, col) < n_own
    for w in range(2):
        right[w] = jnp.where(live, bound[w], jnp.zeros((N, N), BF))
    for copy in own:
        copy.wait()
    extra = jnp.where(within < 2, 6, jnp.where(within == 2, 4, 0))
    pl.semaphore_wait(barrier, 16 + extra)

    sems = (send, recv)

    def halo_copy(d, j):
        width = 2 * N if d == 0 else N
        at = N if d == 0 else 3 * N
        return pltpu.make_async_remote_copy(
            src_ref=rows.at[pl.ds(16 * j, 16), pl.ds(at, width)],
            dst_ref=(hn if d == 0 else hf).at[3 * within + j],
            send_sem=send.at[3 * d + j],
            recv_sem=recv.at[d],
            device_id=goals[d][j],
            device_id_type=MESH,
        )

    for j in range(3):

        @pl.when(sends_halo[j])
        def _(j=j):
            halo_copy(1, j).start()
            halo_copy(0, j).start()

    x_peer = [remote(xs.at[within], xs.at[within], sems, 7 + d, peers[d]) for d in range(3)]
    for copy in x_peer:
        copy.start()
    x_mate = [remote(xs.at[within], xs.at[within], sems, 10, mate)]
    x_mate[0].start()
    above = remote(
        ab.at[within, :, pl.ds(0, N)], ab.at[within, :, pl.ds(N, N)], sems, 6, (lower, blk)
    )
    above.start()
    csems = (csend, crecv)
    l_near = remote(left_hbm.at[:, pl.ds(0, H), :], near_l, csems, 6, (sect, fore8))
    l_far = remote(near_l, far_l, csems, 7, (sect, fore8))

    def landed(ref, slot):
        pltpu.make_async_remote_copy(
            src_ref=ref,
            dst_ref=ref,
            send_sem=send.at[slot],
            recv_sem=recv.at[slot],
            device_id=mate,
            device_id_type=MESH,
        ).wait_recv()

    landed(hf.at[within], 1)
    f_peer = [remote(hf.at[within], hf.at[within], sems, 28 + d, peers[d]) for d in range(3)]
    f_mate = [remote(hf.at[within], hf.at[within], sems, 31, mate)]
    for copy in f_peer + f_mate:
        copy.start()
    landed(hn.at[within], 0)
    h_peer = [remote(hn.at[within], hn.at[within], sems, 21 + d, peers[d]) for d in range(3)]
    h_mate = [remote(hn.at[within], hn.at[within], sems, 24, mate)]
    for copy in h_peer + h_mate:
        copy.start()
    landed(ab.at[within, :, pl.ds(N, N)], 6)
    a_peer = [remote(ab.at[within], ab.at[within], sems, 14 + d, peers[d]) for d in range(3)]
    a_mate = [remote(ab.at[within], ab.at[within], sems, 17, mate)]
    for copy in a_peer + a_mate:
        copy.start()

    def pass_on(buf, first, mine):
        for d in range(3):
            spot = lax.rem(chip + 3 - d, 4) * 2 + core
            landed(buf.at[spot], first + d)
            forward = remote(buf.at[spot], buf.at[spot], sems, first + 4 + d, mate)
            forward.start()
            mine.append(forward)

    down0 = [remote(c0.at[w], got0.at[w], csems, 2 + w, (lower, blk)) for w in range(2)]
    down1 = remote(m1, got1, csems, 0, (lower, back8))
    down3 = remote(m3, got3, csems, 1, (lower, back16))
    last1 = remote(m1, at1, csems, 4, (sect, back8))
    last3 = remote(m3, at3, csems, 5, (sect, back16))
    back0 = remote(right, env_out, csems, 8, (upper, blk))
    up1 = remote(got1, at1, csems, 9, (upper, blk))
    up3 = remote(got3, at3, csems, 10, (upper, blk))

    gsems = (gsend, grecv)
    core_copy = [
        remote(parts.at[k, pl.ds((1 - core) * 4, 4)], part_in.at[k], gsems, k, mate) for k in range(5)
    ]

    def own_terms():
        prods = [(mm(acol[:N, :], right[w]).astype(BF),) for w in range(2)]
        blend = mix(coef, prods, 0)
        for w in range(2):
            mx0[w] = blend[w]
            c0[w] = mm_t(blend[w], acol[:N, :]).astype(BF)

            @pl.when(sect > 0)
            def _(w=w):
                down0[w].start()

    def turn(tile, out):
        for w in range(2):
            out[:, T * w : T * w + T] = jnp.transpose(widen_wide(tile[w]))

    def turn_left():
        left_in.wait()
        for w in range(2):
            left_t[:, N * w : N * w + N] = jnp.transpose(left[w])

    def finish_above():
        pass_on(ab, 14, [])
        for d in range(3):
            remote(ab.at[within], ab.at[within], sems, 18 + d, mate).wait()
        a_mate[0].wait()
        for w in range(G8):
            line = lax.broadcasted_iota(jnp.int32, (48, 2 * N), 0) + 48 * w
            pull[48 * w : 48 * w + 48, :] = jnp.where(
                line < n_own, ab[w], jnp.zeros((48, 2 * N), BF)
            )

    pass_on(xs, 7, x_mate)
    for copy in x_mate:
        copy.wait()
    for w in range(G8):
        line = lax.broadcasted_iota(jnp.int32, (48, N), 0) + 48 * w
        acol[48 * w : 48 * w + 48, :] = jnp.where(line < n_own, xs[w], jnp.zeros((48, N), BF))

    @pl.when(sect == 3)
    def _():
        own_terms()

    pass_on(hf, 28, f_mate)
    for copy in f_mate:
        copy.wait()
    for w in range(G8):
        halo_line = lax.broadcasted_iota(jnp.int32, (16, N), 0) + 16 * w
        at = N + 2 * T + 16 * w
        acol[at : at + 16, :] = jnp.where(halo_line < n_far, hf[w], jnp.zeros((16, N), BF))

    def finish_near():
        pass_on(hn, 21, [])
        for d in range(3):
            remote(hn.at[within], hn.at[within], sems, 25 + d, mate).wait()
        h_mate[0].wait()
        for w in range(G8):
            halo_line = lax.broadcasted_iota(jnp.int32, (16, N), 0) + 16 * w
            for block in range(2):
                at = N + T * block + 16 * w
                acol[at : at + 16, :] = jnp.where(
                    halo_line < n_near, hn[w, :, N * block : N * block + N], jnp.zeros((16, N), BF)
                )

    @pl.when(sect < 2)
    def _():
        l_near.start()
        finish_near()
        finish_above()
        l_near.wait_recv()
        l_far.start()
        turn(near_l, near_t)
        turn_left()

    @pl.when(sect == 0)
    def _():
        l_far.wait_recv()
        turn(far_l, far_t)

    @pl.when(sect == 2)
    def _():
        finish_near()
        finish_above()

    @pl.when(sect < 3)
    def _():
        down1.wait_recv()
        mixed = pull_near(coef, pull, N, got1)
        for w in range(2):
            near_acc[w] = near_terms(mixed, pull, N, w)
        down3.wait_recv()
        mixed = pull_far(coef, pull, N, got3)
        for w in range(2):
            down0[w].wait_recv()
            settle(big, right, w, got0, got1, got3, near_acc[w], far_term(mixed, pull, N, w))

    @pl.when((sect > 0) & (sect < 3))
    def _():
        own_terms()

    far_p = [
        (None, None, None, mm(acol[N + 2 * T : 2 * N, :], right[w]).astype(BF)) for w in range(2)
    ]
    blend = mix(coef, far_p, 3)
    for w in range(2):
        mxh[2, w] = blend[w]

    def far_part():
        write_rows(parts.at[0], mm(far_t[...], mxh[2].reshape(2 * T, N)))
        core_copy[0].start()

    def near_part(p):
        write_rows(parts.at[p], mm(near_t[...], mxh[p - 1].reshape(2 * T, N)))
        core_copy[p].start()

    @pl.when(sect == 0)
    def _():
        far_part()

    for w in range(2):
        far = mm_t(mxh[2, w], acol[N + 2 * T : 2 * N, :])
        m3[w] = jnp.where(far_big, right[w, :H, :T], far[:H].astype(BF))

    @pl.when(sect > 0)
    def _():
        down3.start()

    @pl.when(sect == 0)
    def _():
        last3.start()

    @pl.when(sect == 3)
    def _():
        finish_near()

    near_p = []
    for w in range(2):
        both = mm(acol[N : N + 2 * T, :], right[w]).astype(BF)
        near_p.append((None, both[:T], both[T:]))
    blend = [mix(coef, near_p, p) for p in (1, 2)]
    for w in range(2):
        mxh[0, w] = blend[0][w]
        mxh[1, w] = blend[1][w]
        near = mm_t(blend[0][w], acol[N : N + T, :]) + mm_t(blend[1][w], acol[N + T : N + 2 * T, :])
        m1[w] = jnp.where(near_big, right[w, :H, :T], near[:H].astype(BF))

    @pl.when(sect > 0)
    def _():
        down1.start()

    @pl.when(sect == 0)
    def _():
        last1.start()
        near_part(1)
        near_part(2)

    @pl.when(sect < 3)
    def _():
        up1.start()
        up3.start()
        back0.start()

    @pl.when(sect >= 2)
    def _():
        l_near.start()

    @pl.when(sect == 3)
    def _():
        finish_above()


    odd, half = lax.rem(chip, 2), chip // 2
    side = (sect, base + (chip + 1 - 2 * odd) * 2 + core)
    across = (sect, base + lax.rem(chip + 2, 4) * 2 + core)
    side_copy = [
        remote(sums.at[k, pl.ds((1 - odd) * 2, 2)], sums_in.at[k], gsems, 5 + k, side)
        for k in range(5)
    ]
    across_copy = [
        remote(mids.at[k, 1 - half], mids_in.at[k], gsems, 10 + k, across) for k in range(5)
    ]
    home_copy = [
        remote(totals.at[k], home.at[k], gsems, 15 + k, (sect, back16 if k == 0 else back8))
        for k in range(3)
    ]

    def add_core(k):
        core_copy[k].wait_recv()
        mine = parts[k, pl.ds(core * 4, 4)]
        sums[k] = (mine.astype(F32) + part_in[k].astype(F32)).astype(BF)
        side_copy[k].start()

    def add_side(k):
        side_copy[k].wait_recv()
        mine = sums[k, pl.ds(odd * 2, 2)]
        mids[k] = (mine.astype(F32) + sums_in[k].astype(F32)).astype(BF)
        across_copy[k].start()

    def add_across(k):
        across_copy[k].wait_recv()
        totals[k] = (mids[k, half].astype(F32) + mids_in[k].astype(F32)).astype(BF)

    @pl.when(sect >= 2)
    def _():
        turn_left()
        l_near.wait_recv()
        l_far.start()
        turn(near_l, near_t)

    @pl.when(sect > 0)
    def _():
        l_far.wait_recv()
        turn(far_l, far_t)

    @pl.when(sect > 0)
    def _():
        far_part()
        near_part(1)
        near_part(2)

    add_core(0)
    add_core(1)

    @pl.when(sect == 0)
    def _():
        own_terms()

    write_rows(parts.at[3], mm(left_t[...], mx0[...].reshape(2 * N, N)))
    core_copy[3].start()
    add_side(0)
    add_core(2)
    add_side(1)
    add_across(0)
    home_copy[0].start()
    add_core(3)
    add_side(2)
    add_across(1)
    home_copy[1].start()
    add_across(2)
    home_copy[2].start()

    @pl.when(sect == 0)
    def _():
        last1.wait_recv()
        last3.wait_recv()

    @pl.when(sect > 0)
    def _():
        up1.wait_recv()
        up3.wait_recv()

    mixed = pull_near(coef, pull, 0, at1)
    mixed.append(pull_far(coef, pull, 0, at3))
    narrow = [mm(left_t[...], jnp.concatenate(mixed[p], axis=0)) for p in range(3)]
    write_rows(parts.at[4], jnp.concatenate(narrow, axis=1))
    core_copy[4].start()
    add_side(3)
    for p in range(3):
        for w in range(2):
            mx_pull[w, p] = mixed[p][w]
    add_core(4)
    add_across(3)

    @pl.when(sect == 0)
    def _():
        for w in range(2):
            near = mm_t(mx_pull[w, 0], pull[:, :T]) + mm_t(mx_pull[w, 1], pull[:, T : 2 * T])
            far = mm_t(mx_pull[w, 2], pull[:, 2 * T : 3 * T])
            settle(big, env_out, w, c0, at1, at3, near, far)

    add_side(4)
    add_across(4)
    grads_out[:, :N] = totals[3]
    zero = jnp.zeros((48, N - T), BF)
    for p in range(1, 4):
        k = p % 3
        home_copy[k].wait_recv()
        thin = jnp.concatenate([totals[4, :, T * (p - 1) : T * p], zero], axis=1)
        grads_out[:, N * p : N * p + N] = jnp.where(big, thin, home[k])

    for copy in x_peer + f_peer + h_peer + a_peer + [above, l_near, l_far] + core_copy + home_copy:
        copy.wait_send()
    for copy in side_copy + across_copy:
        copy.wait_send()
    for j in range(3):

        @pl.when(sends_halo[j])
        def _(j=j):
            halo_copy(0, j).wait_send()
            halo_copy(1, j).wait_send()

    @pl.when(sect == 0)
    def _():
        last1.wait_send()
        last3.wait_send()

    @pl.when(sect > 0)
    def _():
        down1.wait_send()
        down3.wait_send()
        down0[0].wait_send()
        down0[1].wait_send()
        back0.wait_recv()

    @pl.when(sect < 3)
    def _():
        back0.wait_send()
        up1.wait_send()
        up3.wait_send()


VMEM = pl.BlockSpec(memory_space=pltpu.VMEM)
HBM = pl.BlockSpec(memory_space=pltpu.HBM)


def local(site_tensor, left_env, boundary_env, sector_sizes, mpo_ops, mpo_mask):
    def buf(*shape):
        return pltpu.VMEM(shape, BF)

    return pl.pallas_call(
        sweep_kernel,
        out_shape=(
            jax.ShapeDtypeStruct((1, 2, N, N), BF),
            jax.ShapeDtypeStruct((1, 48, 4 * N), BF),
        ),
        in_specs=[HBM] * 6,
        out_specs=(VMEM, VMEM),
        scratch_shapes=[
            pltpu.SMEM((16,), jnp.int32),
            pltpu.SMEM((2, 4, 4, 16), F32),
            pltpu.SMEM((2, 16), jnp.int32),
            buf(2, N, N),
            buf(2, N, N),
            pltpu.VMEM((2, N, N), F32),
            buf(2 * N, N),
            buf(N, 2 * N),
            buf(G8, 48, N),
            buf(G8, 16, 2 * N),
            buf(G8, 16, N),
            buf(G8, 48, 2 * N),
            buf(2, N, N),
            buf(2, N, N),
            buf(2, H, T),
            buf(2, H, T),
            buf(2, N, N),
            buf(2, H, T),
            buf(2, H, T),
            buf(2, H, T),
            buf(2, H, T),
            buf(2, H, N),
            buf(2, H, N),
            buf(2, N, N),
            buf(3, 2, T, N),
            buf(2, 3, N, T),
            buf(N, 2 * N),
            buf(N, 2 * T),
            buf(N, 2 * T),
            buf(5, G8, 48, N),
            buf(5, 4, 48, N),
            buf(5, 4, 48, N),
            buf(5, 2, 48, N),
            buf(5, 2, 48, N),
            buf(5, 48, N),
            buf(5, 48, N),
            buf(3, 48, N),
            DMA((35,)),
            DMA((35,)),
            DMA((11,)),
            DMA((11,)),
            DMA((18,)),
            DMA((18,)),
            DMA((9,)),
        ],
        compiler_params=pltpu.CompilerParams(
            collective_id=0, has_side_effects=True, vmem_limit_bytes=50_000_000
        ),
        name="sweep",
    )(
        *[
            pltpu.with_memory_space_constraint(a, pltpu.HBM)
            for a in (
                sector_sizes,
                jnp.transpose(mpo_ops, (1, 2, 3, 0)),
                jnp.transpose(mpo_mask, (1, 0)),
                site_tensor,
                boundary_env,
                left_env,
            )
        ]
    )


def solution(mesh):
    return jax.shard_map(
        local,
        mesh=mesh,
        in_specs=(
            P("sect", "blk", None),
            P("sect", "blk", None, None),
            P("blk", None, None),
            P(),
            P(),
            P(),
        ),
        out_specs=(P("sect", "blk", None, None), P("sect", "blk", None)),
        check_vma=False,
    )
```
